32 devices in a mesh: wide: 8 (over z, x), narrow: 4 (over y, core).
Axes of the slice: x: 2, y: 2, z: 4, core: 2. Of those that a mesh axis runs over, the one named last changes fastest.
Arguments:
- tokens: bfloat16 [24, 512, 768], P('wide', 'narrow'), may hold values from -6 to 6
- lengths: int32 [24], P('wide'), may hold values from 1 to 512, as said below
- qkv_weight: bfloat16 [768, 2304], replicated, may hold values from -0.21875 to 0.21875
- qv_bias: float32 [2, 768], replicated, may hold values from -3 to 3
- out_weight: bfloat16 [768, 768], replicated, may hold values from -0.875 to 0.875
- out_bias: float32 [768], replicated, may hold values from -2 to 2
- norm1_gain: float32 [768], replicated, may hold values from 0.25 to 1.75
- norm1_shift: float32 [768], replicated, may hold values from -2 to 2
- up_weight: bfloat16 [768, 3072], replicated, may hold values from -0.21875 to 0.21875
- up_bias: float32 [3072], replicated, may hold values from -3 to 3
- down_weight: bfloat16 [3072, 768], replicated, may hold values from -0.109375 to 0.109375
- down_bias: float32 [768], replicated, may hold values from -2 to 2
- norm2_gain: float32 [768], replicated, may hold values from 0.25 to 1.75
- norm2_shift: float32 [768], replicated, may hold values from -2 to 2
- cotangent: bfloat16 [24, 512, 768], P('wide', 'narrow'), may hold values from -6 to 6
Outputs:
- output: bfloat16 [24, 512, 768], P('wide', 'narrow')
- input_grad: bfloat16 [24, 512, 768], P('wide', 'narrow')
- qkv_weight_grad: float32 [768, 2304], P('narrow')
- qv_bias_grad: float32 [2, 768], P(None, 'narrow')
- out_weight_grad: float32 [768, 768], P('narrow')
- out_bias_grad: float32 [768], P('narrow')
- norm1_gain_grad: float32 [768], P('narrow')
- norm1_shift_grad: float32 [768], P('narrow')
- up_weight_grad: float32 [768, 3072], P('narrow')
- up_bias_grad: float32 [3072], P('narrow')
- down_weight_grad: float32 [3072, 768], P('narrow')
- down_bias_grad: float32 [768], P('narrow')
- norm2_gain_grad: float32 [768], P('narrow')
- norm2_shift_grad: float32 [768], P('narrow')
The draws below stay inside these ranges and needn't reach their ends.
Inputs may be any that keep to these rules, and one draw needn't show every extreme that they name: The slots of one group of 3 (aligned blocks) share a bucket b from 1 to 4, with lengths from (b - 1) * 128 + 1 to b * 128; slot 0 has length 512.
All inputs are finite; a program needn't handle non-finite values.
Results may differ from the reference program's by a relative error of at most 0.014.
Values may be sent and summed in bfloat16 or wider, within the bound.
A program may use at most 192 MiB of HBM per device.

```python
import jax
import jax.numpy as jnp
from jax import lax

D = 768
H = 12
HD = 64
FF = 3072
LMAX = 512
SEQ_GROUP = 3
SEQS = 24


def draw_lengths(key, part):
    bucket_key, offset_key = jax.random.split(key)
    group_total = SEQS // SEQ_GROUP
    buckets = jax.random.randint(bucket_key, (group_total,), 1, 5).astype(jnp.int32)
    buckets = buckets.at[0].set(4)
    per_sequence = jnp.repeat(buckets, SEQ_GROUP)
    bucket_width = LMAX // 4
    offsets = jax.random.randint(offset_key, (SEQS,), 0, bucket_width).astype(jnp.int32)
    seq_lengths = per_sequence * bucket_width - offsets
    return seq_lengths.at[0].set(LMAX).astype(jnp.int32)


def block_scale(rng, extent, shards, smallest, top_value):
    def one(dim, blocks):
        steps = jax.random.uniform(jax.random.fold_in(jax.random.fold_in(rng, 6), dim), (blocks,), jnp.float32, smallest / len(shards), top_value / len(shards))
        return jnp.repeat(jnp.exp(steps), extent[dim] // blocks).reshape((-1,) + (1,) * (len(extent) - dim - 1))

    level = one(*shards[0])
    for cut in shards[1:]:
        level = level * one(*cut)
    return level


def normal_values(stream_key, shape, deviation, most, cuts=(), held_as=jnp.bfloat16):
    factor_of = block_scale(stream_key, shape, cuts, -0.22, 0.18) if cuts else 1.0
    values = jax.random.normal(stream_key, shape, jnp.float32) * deviation * factor_of
    return jnp.minimum(jnp.maximum(values, -most), most).astype(held_as)


def setup_inputs(seed: int = 0) -> dict:
    arg_keys = jax.random.split(jax.random.key(seed), 16)
    return {
        "tokens": normal_values(arg_keys[0], (SEQS, LMAX, D), 1.0, 6.0, ((0, 8), (1, 4))),
        "lengths": draw_lengths(jax.random.fold_in(arg_keys[15], 71), 0),
        "qkv_weight": normal_values(arg_keys[2], (D, 3 * D), D ** -0.5, 0.21875),
        "qv_bias": normal_values(arg_keys[3], (2, D), 0.5, 3.0, (), jnp.float32),
        "out_weight": normal_values(arg_keys[4], (D, D), (D // 16) ** -0.5, 0.875),
        "out_bias": normal_values(arg_keys[5], (D,), 0.3, 2.0, (), jnp.float32),
        "norm1_gain": jnp.clip(1.0 + 0.15 * jax.random.normal(arg_keys[6], (D,), jnp.float32), 0.25, 1.75),
        "norm1_shift": normal_values(arg_keys[7], (D,), 0.3, 2.0, (), jnp.float32),
        "up_weight": normal_values(arg_keys[8], (D, FF), D ** -0.5, 0.21875),
        "up_bias": normal_values(arg_keys[9], (FF,), 0.5, 3.0, (), jnp.float32),
        "down_weight": normal_values(arg_keys[10], (FF, D), FF ** -0.5, 0.109375),
        "down_bias": normal_values(arg_keys[11], (D,), 0.3, 2.0, (), jnp.float32),
        "norm2_gain": jnp.clip(1.0 + 0.15 * jax.random.normal(arg_keys[12], (D,), jnp.float32), 0.25, 1.75),
        "norm2_shift": normal_values(arg_keys[13], (D,), 0.3, 2.0, (), jnp.float32),
        "cotangent": normal_values(arg_keys[14], (SEQS, LMAX, D), 1.0, 6.0, ((0, 8), (1, 4))),
    }


@jax.custom_vjp
def low(v):
    return lax.optimization_barrier(v.astype(jnp.bfloat16)).astype(jnp.float32)

@jax.custom_vjp
def low_back(v):
    return v

def low_keep(v):
    return (low(v), None)

def low_pass(kept, grad):
    return (grad,)

def back_keep(v):
    return (v, None)

def back_low(kept, grad):
    return (low(grad),)
low.defvjp(low_keep, low_pass)
low_back.defvjp(back_keep, back_low)
epsilon = 1e-12
highest = lax.Precision.HIGHEST

def layer_norm(values, norm_gain, norm_shift):
    center = values - lax.optimization_barrier(jnp.mean(values, axis=-1, keepdims=True))
    variance = lax.optimization_barrier(jnp.mean(center * center, axis=-1, keepdims=True))
    return center * lax.rsqrt(variance + epsilon) * norm_gain + norm_shift

def gelu_exact(values):
    return 0.5 * values * (1.0 + lax.erf(values * 0.7071067811865476))

def forward(inputs, seq_lengths, qkv_weight, qv_bias, out_weight, out_bias, norm1_gain, norm1_shift, up_weight, up_bias, down_weight, down_bias, norm2_gain, norm2_shift):
    seq_count, seq_span, model_width = inputs.shape
    token_rows = inputs.reshape(seq_count * seq_span, model_width)
    zero_bias = jnp.zeros((H, HD), jnp.float32)
    bias_cols = jnp.stack([qv_bias[0].reshape(H, HD), zero_bias, qv_bias[1].reshape(H, HD)], axis=1)
    packed = jnp.dot(token_rows, qkv_weight, precision=highest) + bias_cols.reshape(3 * model_width)
    packed = low_back(low(packed)).reshape(seq_count, seq_span, H, 3, HD)
    query_part = packed[:, :, :, 0]
    key_part = packed[:, :, :, 1]
    value_part = packed[:, :, :, 2]
    raw_scores = low_back(jnp.einsum('bqhe,bkhe->bhqk', query_part, key_part, precision=highest))
    live_keys = lax.iota(jnp.int32, seq_span)[None, :] < seq_lengths[:, None]
    scores = jnp.where(live_keys[:, None, None, :], raw_scores * 0.125, -1000000000.0)
    row_max = lax.optimization_barrier(jnp.max(scores, axis=-1, keepdims=True))
    exponent = jnp.exp(scores - row_max)
    attn_probs = exponent / lax.optimization_barrier(jnp.sum(exponent, axis=-1, keepdims=True))
    context = jnp.einsum('bhqk,bkhe->bqhe', low(attn_probs), value_part, precision=highest)
    context = low_back(low(context)).reshape(seq_count * seq_span, model_width)
    attended = low_back(jnp.dot(context, out_weight, precision=highest) + out_bias)
    first_norm = layer_norm(token_rows + attended, norm1_gain, norm1_shift)
    pre_act = low_back(jnp.dot(low(first_norm), up_weight, precision=highest) + up_bias)
    ffn_out = low_back(jnp.dot(low(gelu_exact(pre_act)), down_weight, precision=highest) + down_bias)
    result = layer_norm(first_norm + ffn_out, norm2_gain, norm2_shift)
    return result.reshape(seq_count, seq_span, model_width)

def reference(tokens, lengths, qkv_weight, qv_bias, out_weight, out_bias, norm1_gain, norm1_shift, up_weight, up_bias, down_weight, down_bias, norm2_gain, norm2_shift, cotangent):
    parameters = (qkv_weight.astype(jnp.float32), qv_bias, out_weight.astype(jnp.float32), out_bias, norm1_gain, norm1_shift, up_weight.astype(jnp.float32), up_bias, down_weight.astype(jnp.float32), down_bias, norm2_gain, norm2_shift)
    group_total = SEQS // SEQ_GROUP
    inputs = tokens.astype(jnp.float32).reshape(group_total, SEQ_GROUP, LMAX, D)
    group_lengths = lengths.reshape(group_total, SEQ_GROUP)
    cotangents = cotangent.astype(jnp.float32).reshape(group_total, SEQ_GROUP, LMAX, D)

    def one_group(running, member):
        group_inputs, member_lengths, group_cot = member

        def apply_layer(inputs_f32, *weights_f32):
            return forward(inputs_f32, member_lengths, *weights_f32)
        result, pullback = jax.vjp(apply_layer, group_inputs, *parameters)
        row_live = lax.iota(jnp.int32, LMAX)[None, :] < member_lengths[:, None]
        gradients = pullback(jnp.where(row_live[:, :, None], group_cot, 0.0))
        running = tuple((total + part_grad for total, part_grad in zip(running, gradients[1:])))
        return (running, (result.astype(jnp.bfloat16), gradients[0].astype(jnp.bfloat16)))
    initial = tuple((jnp.zeros(param_one.shape, jnp.float32) for param_one in parameters))
    totals, (outputs, input_grads) = lax.scan(one_group, initial, (inputs, group_lengths, cotangents))
    return (outputs.reshape(SEQS, LMAX, D), input_grads.reshape(SEQS, LMAX, D), totals[0], totals[1], totals[2], totals[3], totals[4], totals[5], totals[6], totals[7], totals[8], totals[9], totals[10], totals[11])
```

```python
import functools

import jax
import jax.numpy as jnp
from jax import lax
from jax.experimental import pallas as pl
from jax.experimental.pallas import tpu as pltpu
from jax.sharding import PartitionSpec as P

H = 12
HD = 64
PAIR = 2 * HD
epsilon = 1e-12
root_half = 0.7071067811865476
inv_root_two_pi = 0.3989422804014327
MESH = pl.DeviceIdType.MESH
F32 = jnp.float32
BF = jnp.bfloat16
V = pltpu.VMEM
DMA = pltpu.SemaphoreType.DMA
ANY = pl.ANY


def dg(a, b, ca, cb):
    return lax.dot_general(a, b, (((ca,), (cb,)), ((), ())), preferred_element_type=F32)


def copy_to(src, dst, ss, rs, dev):
    return pltpu.make_async_remote_copy(
        src_ref=src, dst_ref=dst, send_sem=ss, recv_sem=rs, device_id=dev, device_id_type=MESH)


def left_lanes(rows):
    return lax.broadcasted_iota(jnp.int32, (rows, PAIR), 1) < HD


def stack_heads(x):
    left = left_lanes(x.shape[0])
    zero = jnp.zeros_like(x)
    return jnp.concatenate([jnp.where(left, x, zero), jnp.where(left, zero, x)], axis=0)


def unstack_heads(x_t):
    q = x_t.shape[1] // 2
    top = lax.broadcasted_iota(jnp.int32, (PAIR, q), 0) < HD
    return jnp.where(top, x_t[:, :q], x_t[:, q:]).T


def forward_kernel(len_ref, tok_ref, w_hbm, b_ref,
                   ctx_ref, toks_hbm, q_hbm, k_hbm, v_hbm, p_hbm, wp_hbm,
                   w, wp, toks, q, k, v, pr,
                   w_sem, cs, cr, ys, yr, fs, fr, o_sem):
    seqs, quarter, d = tok_ref.shape
    pairs = d // PAIR
    wide, n = lax.axis_index("wide"), lax.axis_index("narrow")
    c, y = n % 2, n // 2
    core_n, y_n = n + 1 - 2 * c, n + 2 - 4 * y
    core_peer, y_peer = (wide, core_n), (wide, y_n)
    w_copy = pltpu.make_async_copy(w_hbm, w, w_sem)
    w_copy.start()
    bar = pltpu.get_barrier_semaphore()
    for peer in (core_peer, y_peer):
        pl.semaphore_signal(bar, inc=1, device_id=peer, device_id_type=MESH)
    pl.semaphore_wait(bar, 2)

    def send_y(s):
        return copy_to(tok_ref.at[s], toks.at[s, n], ys.at[s], yr.at[s], y_peer)

    def send_core(s):
        return copy_to(tok_ref.at[s], toks.at[s, n], cs.at[s], cr.at[s], core_peer)

    def forward_y(s):
        return copy_to(toks.at[s, y_n], toks.at[s, y_n], fs.at[s], fr.at[s], core_peer)

    for s in range(seqs):
        send_y(s).start()
        send_core(s).start()
    for s in range(seqs):
        toks[s, n] = tok_ref[s]
    w_copy.wait()
    left = left_lanes(d)
    for p in range(pairs):
        t0, t1, t2 = (w[:, pl.ds(p * 3 * PAIR + i * PAIR, PAIR)].astype(F32) for i in range(3))
        cols = pl.ds(p * PAIR, PAIR)
        wp[0, :, cols] = jnp.where(left, t0, t1).astype(BF)
        wp[1, :, cols] = pltpu.roll(jnp.where(left, t2, t0), HD, 1).astype(BF)
        wp[2, :, cols] = jnp.where(left, t1, t2).astype(BF)
    wp_out = pltpu.make_async_copy(wp, wp_hbm, o_sem.at[0])
    wp_out.start()
    own = tok_ref[...].reshape(seqs * quarter, d)
    q[...] = ((dg(own, wp[0], 1, 0) + b_ref[0:1, :]).astype(BF) * 0.125).reshape(seqs, quarter, d)
    q_out = pltpu.make_async_copy(q, q_hbm, o_sem.at[1])
    q_out.start()

    def project(s, half):
        blocks = pl.ds(2 * half, 2)
        rows = toks[s, blocks].reshape(2 * quarter, d)
        k[s, blocks] = dg(rows, wp[1], 1, 0).astype(BF).reshape(2, quarter, d)
        v[s, blocks] = (dg(rows, wp[2], 1, 0) + b_ref[1:2, :]).astype(BF).reshape(2, quarter, d)

    for s in range(seqs):
        send_core(s).wait_recv()
    for s in range(seqs):
        project(s, y)

    def fetch_far(s):
        copy_to(toks.at[s, y_n], toks.at[s, y_n], ys.at[s], yr.at[s], y_peer).wait_recv()
        forward_y(s).start()

    outs = []
    fetch_far(0)
    for s in range(seqs):
        far = core_n + 2 - 4 * y
        copy_to(toks.at[s, far], toks.at[s, far], fs.at[s], fr.at[s], core_peer).wait_recv()
        project(s, 1 - y)
        if s + 1 < seqs:
            fetch_far(s + 1)
        for i, (src, dst) in enumerate(((toks, toks_hbm), (k, k_hbm), (v, v_hbm))):
            cp = pltpu.make_async_copy(src.at[s], dst.at[s], o_sem.at[2 + 4 * s + i])
            cp.start()
            outs.append(cp)
        keys = 4 * quarter
        live = lax.broadcasted_iota(jnp.int32, (keys, 2 * quarter), 0) < len_ref[s]

        def unit(p, carry):
            cols = pl.ds(pl.multiple_of(p * PAIR, PAIR), PAIR)
            qs = stack_heads(q[s, :, cols])
            kp = k[s, :, :, cols].reshape(keys, PAIR)
            vp = v[s, :, :, cols].reshape(keys, PAIR)
            scores = jnp.where(live, dg(kp, qs, 1, 1), -1000000000.0)
            e = jnp.exp(scores - jnp.max(scores, axis=0, keepdims=True))
            probs = (e * (1.0 / jnp.sum(e, axis=0, keepdims=True))).astype(BF)
            pr[s, p] = probs
            ctx_ref[s, :, cols] = unstack_heads(dg(vp, probs, 0, 0)).astype(BF)
            return carry

        lax.fori_loop(0, pairs, unit, 0)
        cp = pltpu.make_async_copy(pr.at[s], p_hbm.at[s], o_sem.at[2 + 4 * s + 3])
        cp.start()
        outs.append(cp)
    for s in range(seqs):
        send_y(s).wait_send()
        send_core(s).wait_send()
        forward_y(s).wait_send()
    for cp in [wp_out, q_out] + outs:
        cp.wait()


def attention_forward(tokens, lengths, qkv_weight, qv_bias):
    seqs, quarter, d = tokens.shape
    S = jax.ShapeDtypeStruct
    keys = (seqs, 4, quarter, d)
    pairs = d // PAIR
    shapes = [S((seqs, quarter, d), BF), S(keys, BF), S((seqs, quarter, d), BF), S(keys, BF), S(keys, BF),
              S((seqs, pairs, 4 * quarter, 2 * quarter), BF), S((3, d, d), BF)]
    return pl.pallas_call(
        forward_kernel,
        out_shape=shapes,
        in_specs=[pl.BlockSpec(memory_space=pltpu.SMEM), pl.BlockSpec(memory_space=V),
                  pl.BlockSpec(memory_space=ANY), pl.BlockSpec(memory_space=V)],
        out_specs=[pl.BlockSpec(memory_space=V)] + [pl.BlockSpec(memory_space=ANY)] * 6,
        scratch_shapes=[V(qkv_weight.shape, BF), V((3, d, d), BF), V(keys, BF), V((seqs, quarter, d), BF),
                        V(keys, BF), V(keys, BF), V(shapes[5].shape, BF), DMA]
        + [DMA((seqs,))] * 6 + [DMA((2 + 4 * seqs,))],
        name="attention_forward",
        compiler_params=pltpu.CompilerParams(collective_id=1, has_side_effects=True, vmem_limit_bytes=40 << 20),
    )(lengths, tokens, qkv_weight, qv_bias)


def fold(x):
    return jnp.sum(x.reshape(x.shape[0] // 8, 8, x.shape[1]), axis=0)


def rows_kernel(len_ref, tok_ref, cot_ref, ctx_ref, wo_hbm, bo_ref, g1_ref, s1_ref, wu_hbm, bu_ref, wd_hbm, bd_ref,
                g2_ref, s2_ref,
                out_ref, dsum_ref, dctx_ref, first_ref, act_ref, dpre_ref, dffn_ref, datt_ref, sums_ref,
                wo, wu, wd, val, first, normed1, scale1, slope, dsec, part, part_up, sem):
    rows, d = tok_ref.shape
    ff = wu.shape[1]
    quarter = rows // len_ref.shape[0]
    base = lax.axis_index("narrow") * quarter
    loads = [pltpu.make_async_copy(s, t, sem.at[i])
             for i, (s, t) in enumerate(((wo_hbm, wo), (wu_hbm, wu), (wd_hbm, wd)))]
    for cp in loads:
        cp.start()
    part[...] = jnp.zeros_like(part)
    chunk = 64
    chunks = rows // chunk
    loads[0].wait()
    for b in range(d // 256):
        cols = pl.ds(b * 256, 256)
        val[:, cols] = dg(ctx_ref[...], wo[:, cols], 1, 0) + bo_ref[:, cols] + tok_ref[:, cols].astype(F32)

    def norm1(i, carry):
        r = pl.ds(pl.multiple_of(i * chunk, chunk), chunk)
        v = val[r]
        center = v - jnp.mean(v, axis=-1, keepdims=True)
        scale = lax.rsqrt(jnp.mean(center * center, axis=-1, keepdims=True) + epsilon)
        normed = center * scale
        x = normed * g1_ref[...] + s1_ref[...]
        normed1[r] = normed
        scale1[r] = jnp.broadcast_to(scale, (chunk, 128))
        first[r] = x
        first_ref[r] = x.astype(BF)
        return carry

    lax.fori_loop(0, chunks, norm1, 0)
    loads[1].wait()

    def up(j, carry):
        cols = pl.ds(pl.multiple_of(j * 256, 256), 256)
        pre = dg(first_ref[...], wu[:, cols], 1, 0) + bu_ref[:, cols]
        half = 0.5 + 0.5 * lax.erf(pre * root_half)
        act_ref[:, cols] = (pre * half).astype(BF)
        slope[:, cols] = half + pre * (jnp.exp(-0.5 * pre * pre) * inv_root_two_pi)
        return carry

    lax.fori_loop(0, ff // 256, up, 0)
    loads[2].wait()
    for b in range(d // 256):
        cols = pl.ds(b * 256, 256)
        val[:, cols] = dg(act_ref[...], wd[:, cols], 1, 0) + bd_ref[:, cols] + first[:, cols]

    def norm2(i, carry):
        r = pl.ds(pl.multiple_of(i * chunk, chunk), chunk)
        v = val[r]
        center = v - jnp.mean(v, axis=-1, keepdims=True)
        scale = lax.rsqrt(jnp.mean(center * center, axis=-1, keepdims=True) + epsilon)
        normed = center * scale
        out_ref[r] = (normed * g2_ref[...] + s2_ref[...]).astype(BF)
        s = i * chunk // quarter
        pos = base + i * chunk - s * quarter + lax.broadcasted_iota(jnp.int32, (chunk, d), 0)
        d_out = jnp.where(pos < len_ref[s], cot_ref[r].astype(F32), 0.0)
        part[1] += fold(d_out * normed)
        part[2] += fold(d_out)
        g = d_out * g2_ref[...]
        inner = g - jnp.mean(g, axis=-1, keepdims=True) - normed * jnp.mean(g * normed, axis=-1, keepdims=True)
        d_second = scale * inner
        dsec[r] = d_second
        low = d_second.astype(BF)
        dffn_ref[r] = low
        part[0] += fold(low.astype(F32))
        return carry

    lax.fori_loop(0, chunks, norm2, 0)

    def up_back(j, carry):
        cols = pl.ds(pl.multiple_of(j * 256, 256), 256)
        low = (dg(dffn_ref[...], wd[cols, :], 1, 1) * slope[:, cols]).astype(BF)
        dpre_ref[:, cols] = low
        part_up[:, cols] = fold(low.astype(F32))
        return carry

    lax.fori_loop(0, ff // 256, up_back, 0)
    for b in range(d // 256):
        cols = pl.ds(b * 256, 256)
        val[:, cols] = dsec[:, cols] + dg(dpre_ref[...], wu[cols, :], 1, 1)

    def norm1_back(i, carry):
        r = pl.ds(pl.multiple_of(i * chunk, chunk), chunk)
        d_first, normed = val[r], normed1[r]
        part[4] += fold(d_first * normed)
        part[5] += fold(d_first)
        g = d_first * g1_ref[...]
        inner = g - jnp.mean(g, axis=-1, keepdims=True) - normed * jnp.mean(g * normed, axis=-1, keepdims=True)
        d_sum = scale1[r, :1] * inner
        dsum_ref[r] = d_sum
        low = d_sum.astype(BF)
        datt_ref[r] = low
        part[3] += fold(low.astype(F32))
        return carry

    lax.fori_loop(0, chunks, norm1_back, 0)
    dctx_ref[...] = dg(datt_ref[...], wo[...], 1, 1).astype(BF)
    total = lambda x: jnp.sum(x, axis=0, keepdims=True)
    ups = ff // d
    sums_ref[0:1] = total(part[3])
    sums_ref[1:2] = total(part[4])
    sums_ref[2:3] = total(part[5])
    for i in range(ups):
        sums_ref[3 + i:4 + i] = total(part_up[:, i * d:(i + 1) * d])
    sums_ref[3 + ups:4 + ups] = total(part[0])
    sums_ref[4 + ups:5 + ups] = total(part[1])
    sums_ref[5 + ups:6 + ups] = total(part[2])


def rows_part(tok, cot, ctx, lengths, wo, bo, g1, s1, wu, bu, wd, bd, g2, s2):
    rows, d = tok.shape
    ff = wu.shape[1]
    S = jax.ShapeDtypeStruct
    row = lambda a: a.reshape(1, -1)
    vm, hbm = pl.BlockSpec(memory_space=V), pl.BlockSpec(memory_space=ANY)
    return pl.pallas_call(
        rows_kernel,
        out_shape=[S((rows, d), BF), S((rows, d), F32), S((rows, d), BF), S((rows, d), BF), S((rows, ff), BF),
                   S((rows, ff), BF), S((rows, d), BF), S((rows, d), BF), S((6 + ff // d, d), F32)],
        in_specs=[pl.BlockSpec(memory_space=pltpu.SMEM), vm, vm, vm, hbm, vm, vm, vm, hbm, vm, hbm, vm, vm, vm],
        out_specs=[vm] * 9,
        scratch_shapes=[V(wo.shape, BF), V(wu.shape, BF), V(wd.shape, BF), V((rows, d), F32), V((rows, d), F32),
                        V((rows, d), F32), V((rows, 128), F32), V((rows, ff), F32), V((rows, d), F32),
                        V((6, 8, d), F32), V((8, ff), F32), DMA((3,))],
        name="rows_part",
        compiler_params=pltpu.CompilerParams(vmem_limit_bytes=48 << 20),
    )(lengths, tok, cot, ctx, wo, row(bo), row(g1), row(s1), wu, row(bu), wd, row(bd), row(g2), row(s2))


def backward_kernel(dctx_ref, dsum_ref, toks_ref, q_ref, k_ref, v_ref, p_ref, wp_ref,
                    dtok_ref, dinp_ref, gq_ref, sums_ref, dq, dk, dv):
    seqs, quarter, d = q_ref.shape
    pairs = d // PAIR
    keys = 4 * quarter
    for s in range(seqs):
        def unit(p, carry):
            cols = pl.ds(pl.multiple_of(p * PAIR, PAIR), PAIR)
            qs = stack_heads(q_ref[s, :, cols])
            ds = stack_heads(dctx_ref[s, :, cols])
            kp = k_ref[s, :, :, cols].reshape(keys, PAIR)
            vp = v_ref[s, :, :, cols].reshape(keys, PAIR)
            low = p_ref[s, p]
            probs = low.astype(F32)
            d_probs = dg(vp, ds, 1, 1)
            t = probs * d_probs
            d_raw = (t - probs * jnp.sum(t, axis=0, keepdims=True)).astype(BF)
            dv[s, :, cols] = dg(low, ds, 1, 0).astype(BF)
            dk[s, :, cols] = dg(d_raw, qs, 1, 0).astype(BF)
            dq[s, :, cols] = (unstack_heads(dg(kp, d_raw, 0, 0)) * 0.125).astype(BF)
            return carry

        lax.fori_loop(0, pairs, unit, 0)
        dtok = dg(dk[s], wp_ref[1], 1, 1) + dg(dv[s], wp_ref[2], 1, 1)
        dtok_ref[:, s] = dtok.astype(BF).reshape(4, quarter, d)
    dq_all = dq[...].reshape(seqs * quarter, d)
    dinp_ref[...] = dsum_ref[...] + dg(dq_all, wp_ref[0], 1, 1)
    sums_ref[0:1] = jnp.sum(fold(dq_all.astype(F32)), axis=0, keepdims=True)
    total = jnp.zeros((8, d), F32)
    for s in range(seqs):
        total = total + fold(dv[s].astype(F32))
    sums_ref[1:2] = jnp.sum(total, axis=0, keepdims=True)


def qkv_grad_piece(i, tok_ref, toks_ref, dq, dk, dv, store):
    seqs, quarter, d = tok_ref.shape
    cols = pl.ds(i * 2 * PAIR, 2 * PAIR)
    rows = 4 * quarter
    a = dg(tok_ref[...].reshape(seqs * quarter, d), dq[:, :, cols].reshape(seqs * quarter, 2 * PAIR), 0, 0)
    allt = toks_ref[...].reshape(seqs * rows, d)
    b = dg(allt, dk[:, :, cols].reshape(seqs * rows, 2 * PAIR), 0, 0)
    cgrad = dg(allt, dv[:, :, cols].reshape(seqs * rows, 2 * PAIR), 0, 0)
    left = left_lanes(d)
    for j in range(2):
        sl = slice(j * PAIR, (j + 1) * PAIR)
        aj, bj, cj = a[:, sl], pltpu.roll(b[:, sl], HD, 1), cgrad[:, sl]
        store(3 * j, jnp.where(left, aj, bj))
        store(3 * j + 1, jnp.where(left, cj, aj))
        store(3 * j + 2, jnp.where(left, bj, cj))


def attention_backward(dctx, dsum, toks, q, k, v, probs, wp, tok):
    seqs, quarter, d = q.shape
    S = jax.ShapeDtypeStruct
    vm = pl.BlockSpec(memory_space=V)

    def kernel(dctx_ref, dsum_ref, toks_ref, q_ref, k_ref, v_ref, p_ref, wp_ref, tok_ref,
               dtok_ref, dinp_ref, gq_ref, sums_ref, dq, dk, dv):
        backward_kernel(dctx_ref, dsum_ref, toks_ref, q_ref, k_ref, v_ref, p_ref, wp_ref,
                        dtok_ref, dinp_ref, gq_ref, sums_ref, dq, dk, dv)
        for i in range(3):
            def store(t, x):
                gq_ref[i, :, t * PAIR:(t + 1) * PAIR] = x.astype(BF)
            qkv_grad_piece(i, tok_ref, toks_ref, dq, dk, dv, store)

    return pl.pallas_call(
        kernel,
        out_shape=[S((4, seqs, quarter, d), BF), S((seqs * quarter, d), F32), S((3, d, d), BF), S((2, d), F32)],
        in_specs=[vm] * 9,
        out_specs=[vm] * 4,
        scratch_shapes=[V((seqs, quarter, d), BF), V((seqs, 4 * quarter, d), BF), V((seqs, 4 * quarter, d), BF)],
        name="attention_backward",
        compiler_params=pltpu.CompilerParams(vmem_limit_bytes=56 << 20),
    )(dctx, dsum, toks, q, k, v, probs, wp, tok)


LAGS = (0, 1, 3, 4, 6, 7, 8)


def reduce_kernel(gd, gu, go, gq, dtok, dinp_ref, s_ref, out_hbm, din_ref, so_ref,
                  own, r1, r2, r3, r4, res, sbuf, srecv, xown, x1, x2,
                  s1, q1, s2, q2, s3, q3, s4, q4, s5, q5, s6, q6, ls, os_, ss, sq, xs):
    pieces, _, R, C = own.shape
    nd = gd.shape[2] // R
    nu = gu.shape[3] // C
    h = R // 2
    hr, hc = h // 2, C // 2
    w, n = lax.axis_index("wide"), lax.axis_index("narrow")
    c, y, x, z = n % 2, n // 2, w % 2, (w // 2) % 4
    core_peer, y_peer, x_peer = (w, n + 1 - 2 * c), (w, n + 2 - 4 * y), (w + 1 - 2 * x, n)
    zs = [z + 1 - 2 * (z % 2), z + 2 - 4 * (z // 2), 3 - z]
    z_peers = [(w + 2 * (q - z), n) for q in zs]
    bar = pltpu.get_barrier_semaphore()
    for dev in [core_peer, y_peer, x_peer] + z_peers:
        pl.semaphore_signal(bar, inc=1, device_id=dev, device_id_type=MESH)
    pl.semaphore_wait(bar, 6)

    def cut(j):
        return (pl.ds(pl.multiple_of(x * h + (j // 2) * hr, 16), hr), pl.ds(pl.multiple_of((j % 2) * hc, 128), hc))

    near = pl.ds(pl.multiple_of(x * h, 16), h)
    away = pl.ds(pl.multiple_of((1 - x) * h, 16), h)

    def c1(p, src):
        return copy_to(src, r1.at[p], s1.at[p], q1.at[p], core_peer)

    def c1_any(p):
        return c1(p, own.at[p])

    def load(p, src):
        return pltpu.make_async_copy(src, own.at[p], ls.at[p])

    def c2(p):
        return copy_to(own.at[p, 1 - y], r2.at[p], s2.at[p], q2.at[p], y_peer)

    def c3(p):
        return copy_to(own.at[p, y, away], r3.at[p], s3.at[p], q3.at[p], x_peer)

    def c4(p, d):
        rr, cc = cut(zs[d])
        return copy_to(own.at[p, y, rr, cc], r4.at[p, d], s4.at[p, d], q4.at[p, d], z_peers[d])

    def c5(p, d, j):
        rr, cc = cut(j)
        return copy_to(res.at[p, rr, cc], res.at[p, rr, cc], s5.at[p, d], q5.at[p, d], z_peers[d])

    def c6(p, rr):
        return copy_to(res.at[p, rr], res.at[p, rr], s6.at[p], q6.at[p], x_peer)

    def store(p):
        return pltpu.make_async_copy(res.at[p], out_hbm.at[p], os_.at[p])

    def st0(p):
        def go_from(view):
            c1(p, view(1 - c)).start()
            load(p, view(c)).start()

        @pl.when(p < nd)
        def down():
            go_from(lambda e: gd.at[:, e, pl.ds(p * R, R)])

        @pl.when(jnp.logical_and(p >= nd, p < nd + nu))
        def up():
            go_from(lambda e: gu.at[:, e, :, pl.ds(pl.multiple_of((p - nd) * C, C), C)])

        @pl.when(p == nd + nu)
        def out():
            go_from(lambda e: go.at[:, e])

        @pl.when(p > nd + nu)
        def qkv():
            go_from(lambda e: gq.at[p - (nd + nu + 1), :, e])

    def st1(p):
        load(p, own.at[p]).wait()
        c1_any(p).wait_recv()
        own[p] = (own[p].astype(F32) + r1[p].astype(F32)).astype(BF)
        c2(p).start()

    def st2(p):
        c2(p).wait_recv()
        own[p, y] = (own[p, y].astype(F32) + r2[p].astype(F32)).astype(BF)
        c3(p).start()

    def st3(p):
        c3(p).wait_recv()
        own[p, y, near] = (own[p, y, near].astype(F32) + r3[p].astype(F32)).astype(BF)
        for d in (1, 2, 0):
            c4(p, d).start()

    def st4(p):
        for d in range(3):
            c4(p, d).wait_recv()
        rr, cc = cut(z)
        t = own[p, y, rr, cc].astype(F32) + r4[p, 0].astype(F32) + r4[p, 1].astype(F32) + r4[p, 2].astype(F32)
        res[p, rr, cc] = t.astype(BF)
        for d in (1, 2, 0):
            c5(p, d, z).start()

    def st5(p):
        for d in range(3):
            c5(p, d, zs[d]).wait_recv()
        c6(p, near).start()

    def st6(p):
        c6(p, away).wait_recv()
        store(p).start()

    stages = [st0, st1, st2, st3, st4, st5, st6]

    cx1 = copy_to(dtok.at[:, 1 - c], x1, xs.at[0], xs.at[1], core_peer)
    cx2 = copy_to(xown.at[1 - y], x2, xs.at[2], xs.at[3], y_peer)
    cxl = pltpu.make_async_copy(dtok.at[:, c], xown, xs.at[4])
    cx1.start()
    cxl.start()

    def small(k, slot, dev):
        return copy_to(sbuf.at[k], srecv.at[slot], ss.at[slot], sq.at[slot], dev)

    sbuf[0] = s_ref[...]
    small(0, 0, core_peer).start()
    small(0, 0, core_peer).wait_recv()
    sbuf[1] = sbuf[0] + srecv[0]
    small(1, 1, y_peer).start()
    cxl.wait()
    cx1.wait_recv()

    def addx(i, carry):
        xown[i // 3, i % 3] = (xown[i // 3, i % 3].astype(F32) + x1[i // 3, i % 3].astype(F32)).astype(BF)
        return carry

    lax.fori_loop(0, 2 * xown.shape[1], addx, 0)
    cx2.start()

    def slot(t, carry):
        for k in (6, 5, 4, 3, 2, 1, 0):
            p = t - LAGS[k]

            @pl.when(jnp.logical_and(p >= 0, p < pieces))
            def run():
                stages[k](p)
        return carry

    lax.fori_loop(0, pieces + LAGS[6], slot, 0)
    cx2.wait_recv()

    def outx(i, carry):
        din_ref[i] = (dinp_ref[i] + xown[y, i].astype(F32) + x2[i].astype(F32)).astype(BF)
        return carry

    lax.fori_loop(0, xown.shape[1], outx, 0)
    small(1, 1, y_peer).wait_recv()
    sbuf[2] = sbuf[1] + srecv[1]
    small(2, 2, x_peer).start()
    small(2, 2, x_peer).wait_recv()
    sbuf[3] = sbuf[2] + srecv[2]
    for d in range(3):
        small(3, 3 + d, z_peers[d]).start()
    for d in range(3):
        small(3, 3 + d, z_peers[d]).wait_recv()
    so_ref[...] = sbuf[3] + srecv[3] + srecv[4] + srecv[5]
    small(0, 0, core_peer).wait_send()
    small(1, 1, y_peer).wait_send()
    small(2, 2, x_peer).wait_send()
    for d in range(3):
        small(3, 3 + d, z_peers[d]).wait_send()
    cx1.wait_send()
    cx2.wait_send()

    def drain(p, carry):
        c1_any(p).wait_send()
        c2(p).wait_send()
        c3(p).wait_send()
        c6(p, near).wait_send()
        store(p).wait()
        for d in range(3):
            c4(p, d).wait_send()
            c5(p, d, z).wait_send()
        return carry

    lax.fori_loop(0, pieces, drain, 0)


def reduce_all(gd, gu, go, gq, dtok, dinp, rows):
    d = go.shape[1]
    R = d // 4
    n = gd.shape[0] // d + gu.shape[1] // d + 4
    gd = gd.reshape(2, 2, -1, d)
    gu = gu.reshape(2, 2, R, -1)
    go = go.reshape(2, 2, R, d)
    gq = gq.reshape(3, 2, 2, R, d)
    xshape = (2,) + dtok.shape[1:]
    dtok = dtok.reshape((2,) + xshape)
    h = R // 2
    vm, hbm = pl.BlockSpec(memory_space=V), pl.BlockSpec(memory_space=ANY)
    S = jax.ShapeDtypeStruct
    return pl.pallas_call(
        reduce_kernel,
        out_shape=(S((n, R, d), BF), S(dinp.shape, BF), S(rows.shape, F32)),
        in_specs=[hbm] * 5 + [vm] * 2,
        out_specs=(hbm, vm, vm),
        scratch_shapes=[V((n, 2, R, d), BF), V((n, 2, R, d), BF), V((n, R, d), BF), V((n, h, d), BF),
                        V((n, 3, h // 2, d // 2), BF), V((n, R, d), BF), V((4,) + rows.shape, F32),
                        V((6,) + rows.shape, F32), V(xshape, BF), V(xshape, BF), V(xshape[1:], BF)]
        + [DMA((n,))] * 6 + [DMA((n, 3))] * 4 + [DMA((n,))] * 4 + [DMA((6,))] * 2 + [DMA((5,))],
        name="reduce_all",
        compiler_params=pltpu.CompilerParams(collective_id=2, has_side_effects=True, vmem_limit_bytes=48 << 20),
    )(gd, gu, go, gq, dtok, dinp, rows)


def local(tokens, lengths, qkv_weight, qv_bias, out_weight, out_bias, norm1_gain, norm1_shift, up_weight, up_bias,
          down_weight, down_bias, norm2_gain, norm2_shift, cotangent):
    seqs, quarter, d = tokens.shape
    rows = seqs * quarter
    ctx, toks, q, k, v, probs, wp = attention_forward(tokens, lengths, qkv_weight, qv_bias)
    ctx_rows = ctx.reshape(rows, d)
    output, dsum, dctx, first, act, dpre, dffn, datt, sums = rows_part(
        tokens.reshape(rows, d), cotangent.reshape(rows, d), ctx_rows, lengths, out_weight, out_bias,
        norm1_gain, norm1_shift, up_weight, up_bias, down_weight, down_bias, norm2_gain, norm2_shift)
    gd = dg(act, dffn, 0, 0).astype(BF)
    gu = dg(first, dpre, 0, 0).astype(BF)
    go = dg(ctx_rows, datt, 0, 0).astype(BF)
    dtok, dinp, gq, qv_sums = attention_backward(
        dctx.reshape(seqs, quarter, d), dsum, toks, q, k, v, probs, wp, tokens)
    total, input_grad, sums = reduce_all(
        gd, gu, go, gq, dtok, dinp.reshape(seqs, quarter, d), jnp.concatenate([qv_sums, sums]))
    return finish(output.reshape(seqs, quarter, d), input_grad, total, sums, down_weight.shape[0] // d)


def finish(output, input_grad, total, sums, nd):
    q, d = total.shape[1:]
    nu = nd
    wide = lax.axis_size("wide")
    total = total.astype(F32)
    if wide > 8:
        groups = [[g * 8 + i for g in range(wide // 8)] for i in range(8)]
        total = lax.psum(total, "wide", axis_index_groups=groups)
        sums = lax.psum(sums, "wide", axis_index_groups=groups)
    n = lax.axis_index("narrow")
    wide_cols = lambda a: a.transpose(1, 0, 2).reshape(q, -1)
    part = lambda r: lax.dynamic_slice_in_dim(sums[r], n * q, q, 0)
    k = 5 + nu
    return (
        output, input_grad,
        wide_cols(total[nd + nu + 1:]),
        lax.dynamic_slice_in_dim(sums[:2], n * q, q, 1),
        total[nd + nu],
        part(2), part(3), part(4),
        wide_cols(total[nd:nd + nu]),
        lax.dynamic_slice_in_dim(sums[5:k].reshape(-1), n * (nu * q), nu * q, 0),
        total[:nd].reshape(nd * q, d),
        part(k), part(k + 1), part(k + 2),
    )


def solution(mesh):
    return jax.shard_map(
        local,
        mesh=mesh,
        in_specs=(
            P("wide", "narrow", None),
            P("wide"),
            P(),
            P(),
            P(),
            P(),
            P(),
            P(),
            P(),
            P(),
            P(),
            P(),
            P(),
            P(),
            P("wide", "narrow", None),
        ),
        out_specs=(
            P("wide", "narrow", None),
            P("wide", "narrow", None),
            P("narrow", None),
            P(None, "narrow"),
            P("narrow", None),
            P("narrow"),
            P("narrow"),
            P("narrow"),
            P("narrow", None),
            P("narrow"),
            P("narrow", None),
            P("narrow"),
            P("narrow"),
            P("narrow"),
        ),
        check_vma=False,
    )
```

```python
import functools

import jax
import jax.numpy as jnp
from jax import lax
from jax.experimental import pallas as pl
from jax.experimental.pallas import tpu as pltpu
from jax.sharding import PartitionSpec as P

H = 12
HD = 64
PAIR = 2 * HD
epsilon = 1e-12
root_half = 0.7071067811865476
inv_root_two_pi = 0.3989422804014327
MESH = pl.DeviceIdType.MESH
F32 = jnp.float32
BF = jnp.bfloat16
V = pltpu.VMEM
DMA = pltpu.SemaphoreType.DMA
ANY = pl.ANY


def dg(a, b, ca, cb):
    return lax.dot_general(a, b, (((ca,), (cb,)), ((), ())), preferred_element_type=F32)


def copy_to(src, dst, ss, rs, dev):
    return pltpu.make_async_remote_copy(
        src_ref=src, dst_ref=dst, send_sem=ss, recv_sem=rs, device_id=dev, device_id_type=MESH)


def left_lanes(rows):
    return lax.broadcasted_iota(jnp.int32, (rows, PAIR), 1) < HD


def stack_heads(x):
    left = left_lanes(x.shape[0])
    zero = jnp.zeros_like(x)
    return jnp.concatenate([jnp.where(left, x, zero), jnp.where(left, zero, x)], axis=0)


def unstack_heads(x_t):
    q = x_t.shape[1] // 2
    top = lax.broadcasted_iota(jnp.int32, (PAIR, q), 0) < HD
    return jnp.where(top, x_t[:, :q], x_t[:, q:]).T


def forward_kernel(len_ref, tok_ref, w_hbm, b_ref,
                   ctx_ref, toks_hbm, q_hbm, k_hbm, v_hbm, p_hbm, wp_hbm,
                   w, wp, toks, q, k, v, pr,
                   w_sem, cs, cr, ys, yr, fs, fr, o_sem):
    seqs, quarter, d = tok_ref.shape
    pairs = d // PAIR
    wide, n = lax.axis_index("wide"), lax.axis_index("narrow")
    c, y = n % 2, n // 2
    core_n, y_n = n + 1 - 2 * c, n + 2 - 4 * y
    core_peer, y_peer = (wide, core_n), (wide, y_n)
    w_copy = pltpu.make_async_copy(w_hbm, w, w_sem)
    w_copy.start()
    bar = pltpu.get_barrier_semaphore()
    for peer in (core_peer, y_peer):
        pl.semaphore_signal(bar, inc=1, device_id=peer, device_id_type=MESH)
    pl.semaphore_wait(bar, 2)

    def send_y(s):
        return copy_to(tok_ref.at[s], toks.at[s, n], ys.at[s], yr.at[s], y_peer)

    def send_core(s):
        return copy_to(tok_ref.at[s], toks.at[s, n], cs.at[s], cr.at[s], core_peer)

    def forward_y(s):
        return copy_to(toks.at[s, y_n], toks.at[s, y_n], fs.at[s], fr.at[s], core_peer)

    for s in range(seqs):
        send_y(s).start()
        send_core(s).start()
    for s in range(seqs):
        toks[s, n] = tok_ref[s]
    w_copy.wait()
    left = left_lanes(d)
    for p in range(pairs):
        t0, t1, t2 = (w[:, pl.ds(p * 3 * PAIR + i * PAIR, PAIR)].astype(F32) for i in range(3))
        cols = pl.ds(p * PAIR, PAIR)
        wp[0, :, cols] = jnp.where(left, t0, t1).astype(BF)
        wp[1, :, cols] = pltpu.roll(jnp.where(left, t2, t0), HD, 1).astype(BF)
        wp[2, :, cols] = jnp.where(left, t1, t2).astype(BF)
    wp_out = pltpu.make_async_copy(wp, wp_hbm, o_sem.at[0])
    wp_out.start()
    own = tok_ref[...].reshape(seqs * quarter, d)
    q[...] = ((dg(own, wp[0], 1, 0) + b_ref[0:1, :]).astype(BF) * 0.125).reshape(seqs, quarter, d)
    q_out = pltpu.make_async_copy(q, q_hbm, o_sem.at[1])
    q_out.start()

    def project(s, half):
        blocks = pl.ds(2 * half, 2)
        rows = toks[s, blocks].reshape(2 * quarter, d)
        k[s, blocks] = dg(rows, wp[1], 1, 0).astype(BF).reshape(2, quarter, d)
        v[s, blocks] = (dg(rows, wp[2], 1, 0) + b_ref[1:2, :]).astype(BF).reshape(2, quarter, d)

    for s in range(seqs):
        send_core(s).wait_recv()
    for s in range(seqs):
        project(s, y)

    def fetch_far(s):
        copy_to(toks.at[s, y_n], toks.at[s, y_n], ys.at[s], yr.at[s], y_peer).wait_recv()
        forward_y(s).start()

    outs = []
    fetch_far(0)
    for s in range(seqs):
        far = core_n + 2 - 4 * y
        copy_to(toks.at[s, far], toks.at[s, far], fs.at[s], fr.at[s], core_peer).wait_recv()
        project(s, 1 - y)
        if s + 1 < seqs:
            fetch_far(s + 1)
        for i, (src, dst) in enumerate(((toks, toks_hbm), (k, k_hbm), (v, v_hbm))):
            cp = pltpu.make_async_copy(src.at[s], dst.at[s], o_sem.at[2 + 4 * s + i])
            cp.start()
            outs.append(cp)
        keys = 4 * quarter
        live = lax.broadcasted_iota(jnp.int32, (keys, 2 * quarter), 0) < len_ref[s]

        def unit(p, carry):
            cols = pl.ds(pl.multiple_of(p * PAIR, PAIR), PAIR)
            qs = stack_heads(q[s, :, cols])
            kp = k[s, :, :, cols].reshape(keys, PAIR)
            vp = v[s, :, :, cols].reshape(keys, PAIR)
            scores = jnp.where(live, dg(kp, qs, 1, 1), -1000000000.0)
            e = jnp.exp(scores - jnp.max(scores, axis=0, keepdims=True))
            probs = (e * (1.0 / jnp.sum(e, axis=0, keepdims=True))).astype(BF)
            pr[s, p] = probs
            ctx_ref[s, :, cols] = unstack_heads(dg(vp, probs, 0, 0)).astype(BF)
            return carry

        lax.fori_loop(0, pairs, unit, 0)
        cp = pltpu.make_async_copy(pr.at[s], p_hbm.at[s], o_sem.at[2 + 4 * s + 3])
        cp.start()
        outs.append(cp)
    for s in range(seqs):
        send_y(s).wait_send()
        send_core(s).wait_send()
        forward_y(s).wait_send()
    for cp in [wp_out, q_out] + outs:
        cp.wait()


def attention_forward(tokens, lengths, qkv_weight, qv_bias):
    seqs, quarter, d = tokens.shape
    S = jax.ShapeDtypeStruct
    keys = (seqs, 4, quarter, d)
    pairs = d // PAIR
    shapes = [S((seqs, quarter, d), BF), S(keys, BF), S((seqs, quarter, d), BF), S(keys, BF), S(keys, BF),
              S((seqs, pairs, 4 * quarter, 2 * quarter), BF), S((3, d, d), BF)]
    return pl.pallas_call(
        forward_kernel,
        out_shape=shapes,
        in_specs=[pl.BlockSpec(memory_space=pltpu.SMEM), pl.BlockSpec(memory_space=V),
                  pl.BlockSpec(memory_space=ANY), pl.BlockSpec(memory_space=V)],
        out_specs=[pl.BlockSpec(memory_space=V)] + [pl.BlockSpec(memory_space=ANY)] * 6,
        scratch_shapes=[V(qkv_weight.shape, BF), V((3, d, d), BF), V(keys, BF), V((seqs, quarter, d), BF),
                        V(keys, BF), V(keys, BF), V(shapes[5].shape, BF), DMA]
        + [DMA((seqs,))] * 6 + [DMA((2 + 4 * seqs,))],
        name="attention_forward",
        compiler_params=pltpu.CompilerParams(collective_id=1, has_side_effects=True, vmem_limit_bytes=40 << 20),
    )(lengths, tokens, qkv_weight, qv_bias)


def fold(x):
    return jnp.sum(x.reshape(x.shape[0] // 8, 8, x.shape[1]), axis=0)


def rows_kernel(len_ref, tok_ref, cot_ref, ctx_ref, wo_hbm, bo_ref, g1_ref, s1_ref, wu_hbm, bu_ref, wd_hbm, bd_ref,
                g2_ref, s2_ref,
                out_ref, dsum_ref, dctx_ref, first_ref, act_ref, dpre_ref, dffn_ref, datt_ref, sums_ref,
                wo, wu, wd, val, first, normed1, scale1, slope, dsec, part, part_up, sem):
    rows, d = tok_ref.shape
    ff = wu.shape[1]
    quarter = rows // len_ref.shape[0]
    base = lax.axis_index("narrow") * quarter
    loads = [pltpu.make_async_copy(s, t, sem.at[i])
             for i, (s, t) in enumerate(((wo_hbm, wo), (wu_hbm, wu), (wd_hbm, wd)))]
    for cp in loads:
        cp.start()
    part[...] = jnp.zeros_like(part)
    chunk = 64
    chunks = rows // chunk
    loads[0].wait()
    for b in range(d // 256):
        cols = pl.ds(b * 256, 256)
        val[:, cols] = dg(ctx_ref[...], wo[:, cols], 1, 0) + bo_ref[:, cols] + tok_ref[:, cols].astype(F32)

    def norm1(i, carry):
        r = pl.ds(pl.multiple_of(i * chunk, chunk), chunk)
        v = val[r]
        center = v - jnp.mean(v, axis=-1, keepdims=True)
        scale = lax.rsqrt(jnp.mean(center * center, axis=-1, keepdims=True) + epsilon)
        normed = center * scale
        x = normed * g1_ref[...] + s1_ref[...]
        normed1[r] = normed
        scale1[r] = jnp.broadcast_to(scale, (chunk, 128))
        first[r] = x
        first_ref[r] = x.astype(BF)
        return carry

    lax.fori_loop(0, chunks, norm1, 0)
    loads[1].wait()

    def up(j, carry):
        cols = pl.ds(pl.multiple_of(j * 256, 256), 256)
        pre = dg(first_ref[...], wu[:, cols], 1, 0) + bu_ref[:, cols]
        half = 0.5 + 0.5 * lax.erf(pre * root_half)
        act_ref[j // 3, :, pl.ds(pl.multiple_of(j % 3 * 256, 256), 256)] = (pre * half).astype(BF)
        slope[:, cols] = half + pre * (jnp.exp(-0.5 * pre * pre) * inv_root_two_pi)
        return carry

    lax.fori_loop(0, ff // 256, up, 0)
    loads[2].wait()
    for b in range(d // 256):
        cols = pl.ds(b * 256, 256)
        val[:, cols] = bd_ref[:, cols] + first[:, cols] + sum(
            dg(act_ref[i], wd[i * d:(i + 1) * d, cols], 1, 0) for i in range(ff // d))

    def norm2(i, carry):
        r = pl.ds(pl.multiple_of(i * chunk, chunk), chunk)
        v = val[r]
        center = v - jnp.mean(v, axis=-1, keepdims=True)
        scale = lax.rsqrt(jnp.mean(center * center, axis=-1, keepdims=True) + epsilon)
        normed = center * scale
        out_ref[r] = (normed * g2_ref[...] + s2_ref[...]).astype(BF)
        s = i * chunk // quarter
        pos = base + i * chunk - s * quarter + lax.broadcasted_iota(jnp.int32, (chunk, d), 0)
        d_out = jnp.where(pos < len_ref[s], cot_ref[r].astype(F32), 0.0)
        part[1] += fold(d_out * normed)
        part[2] += fold(d_out)
        g = d_out * g2_ref[...]
        inner = g - jnp.mean(g, axis=-1, keepdims=True) - normed * jnp.mean(g * normed, axis=-1, keepdims=True)
        d_second = scale * inner
        dsec[r] = d_second
        low = d_second.astype(BF)
        dffn_ref[r] = low
        part[0] += fold(low.astype(F32))
        return carry

    lax.fori_loop(0, chunks, norm2, 0)

    def up_back(j, carry):
        cols = pl.ds(pl.multiple_of(j * 256, 256), 256)
        low = (dg(dffn_ref[...], wd[cols, :], 1, 1) * slope[:, cols]).astype(BF)
        dpre_ref[j // 3, :, pl.ds(pl.multiple_of(j % 3 * 256, 256), 256)] = low
        part_up[:, cols] = fold(low.astype(F32))
        return carry

    lax.fori_loop(0, ff // 256, up_back, 0)
    for b in range(d // 256):
        cols = pl.ds(b * 256, 256)
        val[:, cols] = dsec[:, cols] + sum(
            dg(dpre_ref[i], wu[cols, i * d:(i + 1) * d], 1, 1) for i in range(ff // d))

    def norm1_back(i, carry):
        r = pl.ds(pl.multiple_of(i * chunk, chunk), chunk)
        d_first, normed = val[r], normed1[r]
        part[4] += fold(d_first * normed)
        part[5] += fold(d_first)
        g = d_first * g1_ref[...]
        inner = g - jnp.mean(g, axis=-1, keepdims=True) - normed * jnp.mean(g * normed, axis=-1, keepdims=True)
        d_sum = scale1[r, :1] * inner
        dsum_ref[r] = d_sum
        low = d_sum.astype(BF)
        datt_ref[r] = low
        part[3] += fold(low.astype(F32))
        return carry

    lax.fori_loop(0, chunks, norm1_back, 0)
    dctx_ref[...] = dg(datt_ref[...], wo[...], 1, 1).astype(BF)
    total = lambda x: jnp.sum(x, axis=0, keepdims=True)
    ups = ff // d
    sums_ref[0:1] = total(part[3])
    sums_ref[1:2] = total(part[4])
    sums_ref[2:3] = total(part[5])
    for i in range(ups):
        sums_ref[3 + i:4 + i] = total(part_up[:, i * d:(i + 1) * d])
    sums_ref[3 + ups:4 + ups] = total(part[0])
    sums_ref[4 + ups:5 + ups] = total(part[1])
    sums_ref[5 + ups:6 + ups] = total(part[2])


def rows_part(tok, cot, ctx, lengths, wo, bo, g1, s1, wu, bu, wd, bd, g2, s2):
    rows, d = tok.shape
    ff = wu.shape[1]
    S = jax.ShapeDtypeStruct
    row = lambda a: a.reshape(1, -1)
    vm, hbm = pl.BlockSpec(memory_space=V), pl.BlockSpec(memory_space=ANY)
    return pl.pallas_call(
        rows_kernel,
        out_shape=[S((rows, d), BF), S((rows, d), F32), S((rows, d), BF), S((rows, d), BF), S((ff // d, rows, d), BF),
                   S((ff // d, rows, d), BF), S((rows, d), BF), S((rows, d), BF), S((6 + ff // d, d), F32)],
        in_specs=[pl.BlockSpec(memory_space=pltpu.SMEM), vm, vm, vm, hbm, vm, vm, vm, hbm, vm, hbm, vm, vm, vm],
        out_specs=[vm] * 9,
        scratch_shapes=[V(wo.shape, BF), V(wu.shape, BF), V(wd.shape, BF), V((rows, d), F32), V((rows, d), F32),
                        V((rows, d), F32), V((rows, 128), F32), V((rows, ff), F32), V((rows, d), F32),
                        V((6, 8, d), F32), V((8, ff), F32), DMA((3,))],
        name="rows_part",
        compiler_params=pltpu.CompilerParams(vmem_limit_bytes=48 << 20),
    )(lengths, tok, cot, ctx, wo, row(bo), row(g1), row(s1), wu, row(bu), wd, row(bd), row(g2), row(s2))


LAGS = (0, 1, 3, 4, 6, 7, 8)
UNITS = 5


def tail_kernel(act_h, dpre_h, dffn_h, first_h, ctx_h, datt_h, dctx_h, dsum_h, toks_h, tok_h, q_h, k_h, v_h, p_h, wp_h,
                sums_ref,
                od_hbm, ou_hbm, oo_hbm, oq_hbm, din_hbm, so_ref,
                a_buf, b_buf, dffn, first, ctx, datt, dctx, dsum, toks, tok, q, k, v, pr, wp, dq, dtok,
                g, r1, r2, r3, r4, sbuf, srecv, x1, x2, din,
                s1, q1, s2, q2, s3, q3, s4, q4, s5, q5, s6, q6, os_, ss, sq, xs, ls):
    pieces, _, _, R, C = g.shape
    seqs, quarter, d = dctx.shape
    rows, keys, pairs = seqs * quarter, 4 * quarter, d // PAIR
    nd = act_h.shape[0]
    nu = dpre_h.shape[0]
    h = R // 2
    hr, hc = h // 2, C // 2
    w, n = lax.axis_index("wide"), lax.axis_index("narrow")
    c, y, x, z = n % 2, n // 2, w % 2, (w // 2) % 4
    core_peer, y_peer, x_peer = (w, n + 1 - 2 * c), (w, n + 2 - 4 * y), (w + 1 - 2 * x, n)
    zs = [z + 1 - 2 * (z % 2), z + 2 - 4 * (z // 2), 3 - z]
    z_peers = [(w + 2 * (j - z), n) for j in zs]

    a_view, b_view = a_buf.reshape(nd, rows, d), b_buf.reshape(nu, rows, d)
    dk, dv = a_buf.reshape(seqs, keys, d), b_buf.reshape(seqs, keys, d)
    loads = [(act_h, a_view), (dffn_h, dffn), (dpre_h, b_view), (first_h, first), (ctx_h, ctx), (datt_h, datt),
             (v_h, v), (dctx_h, dctx), (p_h, pr), (q_h, q), (k_h, k), (toks_h, toks), (tok_h, tok), (wp_h, wp),
             (dsum_h, dsum)]
    loads = [pltpu.make_async_copy(s, t, ls.at[i]) for i, (s, t) in enumerate(loads)]
    for cp in loads:
        cp.start()
    bar = pltpu.get_barrier_semaphore()
    for dev in [core_peer, y_peer, x_peer] + z_peers:
        pl.semaphore_signal(bar, inc=1, device_id=dev, device_id_type=MESH)

    def cut(j):
        return (pl.ds(pl.multiple_of(x * h + (j // 2) * hr, 16), hr), pl.ds(pl.multiple_of((j % 2) * hc, 128), hc))

    near = pl.ds(pl.multiple_of(x * h, 16), h)
    away = pl.ds(pl.multiple_of((1 - x) * h, 16), h)

    def c1(p):
        return copy_to(g.at[p, 1 - c], r1.at[p], s1.at[p], q1.at[p], core_peer)

    def c2(p):
        return copy_to(g.at[p, c, 1 - y], r2.at[p], s2.at[p], q2.at[p], y_peer)

    def c3(p):
        return copy_to(g.at[p, c, y, away], r3.at[p], s3.at[p], q3.at[p], x_peer)

    def c4(p, e):
        rr, cc = cut(zs[e])
        return copy_to(g.at[p, c, y, rr, cc], r4.at[p, e], s4.at[p, e], q4.at[p, e], z_peers[e])

    def c5(p, e, j):
        rr, cc = cut(j)
        return copy_to(r1.at[p, 0, rr, cc], r1.at[p, 0, rr, cc], s5.at[p, e], q5.at[p, e], z_peers[e])

    def c6(p, rr):
        return copy_to(r1.at[p, 0, rr], r1.at[p, 0, rr], s6.at[p], q6.at[p], x_peer)

    def store(p, dst):
        return pltpu.make_async_copy(r1.at[p, 0], dst, os_.at[p])

    def st1(p):
        c1(p).wait_recv()
        g[p, c] = (g[p, c].astype(F32) + r1[p].astype(F32)).astype(BF)
        c2(p).start()

    def st2(p):
        c2(p).wait_recv()
        g[p, c, y] = (g[p, c, y].astype(F32) + r2[p].astype(F32)).astype(BF)
        c3(p).start()

    def st3(p):
        c3(p).wait_recv()
        g[p, c, y, near] = (g[p, c, y, near].astype(F32) + r3[p].astype(F32)).astype(BF)
        for e in (1, 2, 0):
            c4(p, e).start()

    def st4(p):
        for e in range(3):
            c4(p, e).wait_recv()
        rr, cc = cut(z)
        t = g[p, c, y, rr, cc].astype(F32) + r4[p, 0].astype(F32) + r4[p, 1].astype(F32) + r4[p, 2].astype(F32)
        r1[p, 0, rr, cc] = t.astype(BF)
        for e in (1, 2, 0):
            c5(p, e, z).start()

    def st5(p):
        for e in range(3):
            c5(p, e, zs[e]).wait_recv()
        c6(p, near).start()

    def st6(p):
        c6(p, away).wait_recv()

        @pl.when(p < nd)
        def down():
            store(p, od_hbm.at[pl.ds(p * R, R)]).start()

        @pl.when(jnp.logical_and(p >= nd, p < nd + nu))
        def up():
            store(p, ou_hbm.at[:, pl.ds(pl.multiple_of((p - nd) * C, C), C)]).start()

        @pl.when(p == nd + nu)
        def out():
            store(p, oo_hbm).start()

        @pl.when(p > nd + nu)
        def qkv():
            store(p, oq_hbm.at[:, pl.ds(pl.multiple_of((p - nd - nu - 1) * C, C), C)]).start()

    stages = [None, st1, st2, st3, st4, st5, st6]

    loads[0].wait()
    loads[1].wait()

    def down_block(i, carry):
        t = dg(a_view[i], dffn[...], 0, 0).astype(BF)
        for j in range(nd):
            g[j, i % 2, i // 2] = t[j * R:(j + 1) * R]
        return carry

    lax.fori_loop(0, nd, down_block, 0)
    pl.semaphore_wait(bar, 6)
    for p in range(nd):
        c1(p).start()
    loads[2].wait()
    loads[3].wait()

    def row_block(p, t):
        for j in range(4):
            g[p, j % 2, j // 2] = t[j * R:(j + 1) * R].astype(BF)

    def up_block(i, carry):
        row_block(nd + i, dg(first[...], b_view[i], 0, 0))
        c1(nd + i).start()
        return carry

    lax.fori_loop(0, 2, up_block, 0)
    st1(0)
    st1(1)
    lax.fori_loop(2, nu, up_block, 0)
    loads[4].wait()
    loads[5].wait()
    row_block(nd + nu, dg(ctx[...], datt[...], 0, 0))
    c1(nd + nu).start()
    for cp in loads[6:]:
        cp.wait()

    def unit(u, carry):
        s, p = u // pairs, u % pairs
        cols = pl.ds(pl.multiple_of(p * PAIR, PAIR), PAIR)
        qs = stack_heads(q[s, :, cols])
        ds = stack_heads(dctx[s, :, cols])
        low = pr[s, p]
        probs = low.astype(F32)
        t = probs * dg(v[s, :, cols], ds, 1, 1)
        d_raw = (t - probs * jnp.sum(t, axis=0, keepdims=True)).astype(BF)
        dv[s, :, cols] = dg(low, ds, 1, 0).astype(BF)
        dk[s, :, cols] = dg(d_raw, qs, 1, 0).astype(BF)
        dq[s, :, cols] = (unstack_heads(dg(k[s, :, cols], d_raw, 0, 0)) * 0.125).astype(BF)
        return carry

    def qkv_piece(i):
        cols = pl.ds(i * 2 * PAIR, 2 * PAIR)
        allt = toks[...].reshape(seqs * keys, d)
        ga = dg(tok[...].reshape(rows, d), dq[:, :, cols].reshape(rows, 2 * PAIR), 0, 0)
        gb = dg(allt, a_buf[:, cols], 0, 0)
        gc = dg(allt, b_buf[:, cols], 0, 0)
        left = left_lanes(R)
        p = nd + nu + 1 + i
        for e in range(4):
            rr = slice(e * R, (e + 1) * R)
            for j in range(2):
                sl = slice(j * PAIR, (j + 1) * PAIR)
                aj, bj, cj = ga[rr, sl], pltpu.roll(gb[rr, sl], HD, 1), gc[rr, sl]
                for t, val in enumerate((jnp.where(left, aj, bj), jnp.where(left, cj, aj), jnp.where(left, bj, cj))):
                    g[p, e % 2, e // 2, :, pl.ds((3 * j + t) * PAIR, PAIR)] = val.astype(BF)
        c1(p).start()

    cx1 = copy_to(dtok.at[:, 1 - c], x1, xs.at[0], xs.at[1], core_peer)
    cx2 = copy_to(dtok.at[1 - y, c], x2, xs.at[2], xs.at[3], y_peer)

    def input_part():
        def one(s, carry):
            t = dg(dk[s], wp[1], 1, 1) + dg(dv[s], wp[2], 1, 1)
            for e in range(4):
                dtok[e // 2, e % 2, s] = t[e * quarter:(e + 1) * quarter].astype(BF)
            return carry

        lax.fori_loop(0, seqs, one, 0)
        cx1.start()
        dsum[...] += dg(dq[...].reshape(rows, d), wp[0], 1, 1)

    def small(i, slot, dev):
        return copy_to(sbuf.at[i], srecv.at[slot], ss.at[slot], sq.at[slot], dev)

    def sums0():
        sbuf[0, 0:1] = jnp.sum(fold(dq[...].reshape(rows, d).astype(F32)), axis=0, keepdims=True)

        def add(s, acc):
            return acc + fold(dv[s].astype(F32))

        acc = lax.fori_loop(0, seqs, add, jnp.zeros((8, d), F32))
        sbuf[0, 1:2] = jnp.sum(acc, axis=0, keepdims=True)
        sbuf[0, 2:] = sums_ref[...]
        small(0, 0, core_peer).start()

    def sums1():
        small(0, 0, core_peer).wait_recv()
        sbuf[1] = sbuf[0] + srecv[0]
        small(1, 1, y_peer).start()

    def sums2():
        small(1, 1, y_peer).wait_recv()
        sbuf[2] = sbuf[1] + srecv[1]
        small(2, 2, x_peer).start()

    def sums3():
        small(2, 2, x_peer).wait_recv()
        sbuf[3] = sbuf[2] + srecv[2]
        for e in range(3):
            small(3, 3 + e, z_peers[e]).start()

    def add_x1():
        cx1.wait_recv()

        def add(i, carry):
            a, b = i // seqs, i % seqs
            dtok[a, c, b] = (dtok[a, c, b].astype(F32) + x1[a, b].astype(F32)).astype(BF)
            return carry

        lax.fori_loop(0, 2 * seqs, add, 0)

    units = seqs * pairs
    slots_of_units = -(-units // UNITS)
    extra = {7: [lambda: qkv_piece(0), lambda: qkv_piece(1)], 8: [lambda: qkv_piece(2), sums0, input_part],
             9: [add_x1, sums1], 12: [sums2], 13: [cx2.start, sums3]}

    def slot(t, carry):
        for i in (6, 5, 4, 3, 2, 1):
            p = t - LAGS[i]

            @pl.when(jnp.logical_and(p >= 0, p < pieces))
            def run():
                stages[i](p)

        @pl.when(t < 3 + slots_of_units)
        def attention():
            lo = (t - 3) * UNITS
            lax.fori_loop(lo, jnp.minimum(lo + UNITS, units), unit, 0)

        for at, todo in extra.items():
            @pl.when(t == at)
            def more():
                for f in todo:
                    f()
        return carry

    lax.fori_loop(3, pieces + LAGS[6], slot, 0)
    cx2.wait_recv()

    def out_x(i, carry):
        r = pl.ds(pl.multiple_of(i * quarter, quarter), quarter)
        din[i] = (dsum[r] + dtok[y, c, i].astype(F32) + x2[i].astype(F32)).astype(BF)
        return carry

    lax.fori_loop(0, seqs, out_x, 0)
    din_out = pltpu.make_async_copy(din, din_hbm, xs.at[4])
    din_out.start()
    for e in range(3):
        small(3, 3 + e, z_peers[e]).wait_recv()
    so_ref[...] = sbuf[3] + srecv[3] + srecv[4] + srecv[5]
    small(0, 0, core_peer).wait_send()
    small(1, 1, y_peer).wait_send()
    small(2, 2, x_peer).wait_send()
    for e in range(3):
        small(3, 3 + e, z_peers[e]).wait_send()
    cx1.wait_send()
    cx2.wait_send()

    def drain(p, carry):
        c1(p).wait_send()
        c2(p).wait_send()
        c3(p).wait_send()
        c6(p, near).wait_send()
        store(p, oo_hbm).wait()
        for e in range(3):
            c4(p, e).wait_send()
            c5(p, e, z).wait_send()
        return carry

    lax.fori_loop(0, pieces, drain, 0)
    din_out.wait()


def tail_part(act, dpre, dffn, first, ctx, datt, dctx, dsum, toks, tok, q, k, v, probs, wp, sums):
    seqs, quarter, d = tok.shape
    rows, keys = seqs * quarter, 4 * quarter
    R = d // 4
    nd, nu = act.shape[0], dpre.shape[0]
    n = nd + nu + 4
    h = R // 2
    all_rows = (sums.shape[0] + 2, d)
    vm, hbm = pl.BlockSpec(memory_space=V), pl.BlockSpec(memory_space=ANY)
    S = jax.ShapeDtypeStruct
    own, every = (seqs, quarter, d), (seqs, keys, d)
    return pl.pallas_call(
        tail_kernel,
        out_shape=(S((nd * R, d), BF), S((R, nu * d), BF), S((R, d), BF), S((R, 3 * d), BF), S(own, BF),
                   S(all_rows, F32)),
        in_specs=[hbm] * 15 + [vm],
        out_specs=(hbm, hbm, hbm, hbm, hbm, vm),
        scratch_shapes=[V((seqs * keys, d), BF), V((seqs * keys, d), BF), V((rows, d), BF), V((rows, d), BF),
                        V((rows, d), BF), V((rows, d), BF), V(own, BF), V((rows, d), F32), V(every, BF), V(own, BF),
                        V(own, BF), V(every, BF), V(every, BF), V(probs.shape, BF), V((3, d, d), BF), V(own, BF),
                        V((2, 2) + own, BF),
                        V((n, 2, 2, R, d), BF), V((n, 2, R, d), BF), V((n, R, d), BF), V((n, h, d), BF),
                        V((n, 3, h // 2, d // 2), BF), V((4,) + all_rows, F32), V((6,) + all_rows, F32),
                        V((2,) + own, BF), V(own, BF), V(own, BF)]
        + [DMA((n,))] * 6 + [DMA((n, 3))] * 4 + [DMA((n,))] * 3 + [DMA((6,))] * 2 + [DMA((5,)), DMA((15,))],
        name="tail_part",
        compiler_params=pltpu.CompilerParams(collective_id=2, has_side_effects=True, vmem_limit_bytes=62 << 20),
    )(act, dpre, dffn, first, ctx, datt, dctx, dsum, toks, tok, q, k, v, probs, wp, sums)


def local(tokens, lengths, qkv_weight, qv_bias, out_weight, out_bias, norm1_gain, norm1_shift, up_weight, up_bias,
          down_weight, down_bias, norm2_gain, norm2_shift, cotangent):
    seqs, quarter, d = tokens.shape
    rows = seqs * quarter
    own, every = (seqs, quarter, d), (seqs, 4 * quarter, d)
    ctx, toks, q, k, v, probs, wp = attention_forward(tokens, lengths, qkv_weight, qv_bias)
    ctx_rows = ctx.reshape(rows, d)
    output, dsum, dctx, first, act, dpre, dffn, datt, sums = rows_part(
        tokens.reshape(rows, d), cotangent.reshape(rows, d), ctx_rows, lengths, out_weight, out_bias,
        norm1_gain, norm1_shift, up_weight, up_bias, down_weight, down_bias, norm2_gain, norm2_shift)
    down, up, out, qkv, input_grad, sums = tail_part(
        act, dpre, dffn, first, ctx_rows, datt, dctx.reshape(own), dsum, toks.reshape(every), tokens, q,
        k.reshape(every), v.reshape(every), probs, wp, sums)
    grads = [a.astype(F32) for a in (down, up, out, qkv)]
    wide = lax.axis_size("wide")
    if wide > 8:
        groups = [[j * 8 + i for j in range(wide // 8)] for i in range(8)]
        grads = lax.psum(grads, "wide", axis_index_groups=groups)
        sums = lax.psum(sums, "wide", axis_index_groups=groups)
    down, up, out, qkv = grads
    n = lax.axis_index("narrow")
    R = d // 4
    nu = up.shape[1] // d
    part = lambda r: lax.dynamic_slice_in_dim(sums[r], n * R, R, 0)
    i = 5 + nu
    up_b = lax.dynamic_slice_in_dim(sums[5:i].reshape(-1), n * (nu * R), nu * R, 0)
    return (output.reshape(own), input_grad, qkv, lax.dynamic_slice_in_dim(sums[:2], n * R, R, 1), out,
            part(2), part(3), part(4), up, up_b, down, part(i), part(i + 1), part(i + 2))


def solution(mesh):
    return jax.shard_map(
        local,
        mesh=mesh,
        in_specs=(
            P("wide", "narrow", None),
            P("wide"),
            P(),
            P(),
            P(),
            P(),
            P(),
            P(),
            P(),
            P(),
            P(),
            P(),
            P(),
            P(),
            P("wide", "narrow", None),
        ),
        out_specs=(
            P("wide", "narrow", None),
            P("wide", "narrow", None),
            P("narrow", None),
            P(None, "narrow"),
            P("narrow", None),
            P("narrow"),
            P("narrow"),
            P("narrow"),
            P("narrow", None),
            P("narrow"),
            P("narrow", None),
            P("narrow"),
            P("narrow"),
            P("narrow"),
        ),
        check_vma=False,
    )
```

```python
import functools

import jax
import jax.numpy as jnp
from jax import lax
from jax.experimental import pallas as pl
from jax.experimental.pallas import tpu as pltpu
from jax.sharding import PartitionSpec as P

H = 12
HD = 64
PAIR = 2 * HD
epsilon = 1e-12
root_half = 0.7071067811865476
inv_root_two_pi = 0.3989422804014327
MESH = pl.DeviceIdType.MESH
F32 = jnp.float32
BF = jnp.bfloat16
V = pltpu.VMEM
DMA = pltpu.SemaphoreType.DMA
ANY = pl.ANY
UNROLL_ATT = 1
UNROLL_UP = 1


def dg(a, b, ca, cb):
    return lax.dot_general(a, b, (((ca,), (cb,)), ((), ())), preferred_element_type=F32)


def copy_to(src, dst, ss, rs, dev):
    return pltpu.make_async_remote_copy(
        src_ref=src, dst_ref=dst, send_sem=ss, recv_sem=rs, device_id=dev, device_id_type=MESH)


def left_lanes(rows):
    return lax.broadcasted_iota(jnp.int32, (rows, PAIR), 1) < HD


def stack_heads(x):
    left = left_lanes(x.shape[0])
    zero = jnp.zeros_like(x)
    return jnp.concatenate([jnp.where(left, x, zero), jnp.where(left, zero, x)], axis=0)


def unstack_heads(x_t):
    q = x_t.shape[1] // 2
    top = lax.broadcasted_iota(jnp.int32, (PAIR, q), 0) < HD
    return jnp.where(top, x_t[:, :q], x_t[:, q:]).T


def fold(x):
    return jnp.sum(x.reshape(x.shape[0] // 8, 8, x.shape[1]), axis=0)


def total(x):
    return jnp.sum(x, axis=0, keepdims=True)


def center_scale(v):
    center = v - jnp.mean(v, axis=-1, keepdims=True)
    scale = lax.rsqrt(jnp.mean(center * center, axis=-1, keepdims=True) + epsilon)
    return center * scale, scale


def norm_grad(g, normed):
    return g - jnp.mean(g, axis=-1, keepdims=True) - normed * jnp.mean(g * normed, axis=-1, keepdims=True)


def front_kernel(len_ref, tok_h, cot_h, w_h, wo_h, wu_h, wd_h, qvb_h, bo_h, g1_h, s1_h, bu_h, bd_h, g2_h, s2_h,
                 toks_h, q_h, k_h, v_h, p_h, wp_h, ctx_h, first_h, act_h, slope_h, out_h, dffn_h, dsec_h, normed_h,
                 scale_h, sums_ref,
                 w, wp, toks, q, k, v, pr, tok, cot, wo, wu, wd, ctx, low1, act, slope, out, dffn, dsec, normed1,
                 scale1, val, first, part, qvb_ref, bo_v, g1_v, s1_v, bu_v, bd_v, g2_v, s2_v,
                 ls, cs, cr, ys, yr, fs, fr, os_):
    seqs, quarter, d = tok.shape
    rows, keys, pairs = seqs * quarter, 4 * quarter, d // PAIR
    ff = wu.shape[1]
    wide, n = lax.axis_index("wide"), lax.axis_index("narrow")
    c, y = n % 2, n // 2
    core_n, y_n = n + 1 - 2 * c, n + 2 - 4 * y
    far_n = core_n + 2 - 4 * y
    core_peer, y_peer = (wide, core_n), (wide, y_n)
    loads = [pltpu.make_async_copy(s, t, ls.at[i]) for i, (s, t) in enumerate(
        ((tok_h, tok), (w_h, w), (wo_h, wo), (wu_h, wu), (cot_h, cot), (wd_h, wd), (qvb_h, qvb_ref), (bo_h, bo_v),
         (g1_h, g1_v), (s1_h, s1_v), (bu_h, bu_v), (bd_h, bd_v), (g2_h, g2_v), (s2_h, s2_v)))]
    outs = []

    def emit(src, dst):
        cp = pltpu.make_async_copy(src, dst, os_.at[len(outs)])
        cp.start()
        outs.append(cp)

    for cp in loads[:2]:
        cp.start()
    bar = pltpu.get_barrier_semaphore()
    for peer in (core_peer, y_peer):
        pl.semaphore_signal(bar, inc=1, device_id=peer, device_id_type=MESH)
    pl.semaphore_wait(bar, 2)

    def send_y(s):
        return copy_to(tok_h.at[s], toks.at[s, n], ys.at[s], yr.at[s], y_peer)

    def send_core(s):
        return copy_to(tok_h.at[s], toks.at[s, n], cs.at[s], cr.at[s], core_peer)

    def forward_y(s):
        return copy_to(toks.at[s, y_n], toks.at[s, y_n], fs.at[s], fr.at[s], core_peer)

    for s in range(seqs):
        send_y(s).start()
        send_core(s).start()
    for cp in loads[2:]:
        cp.start()
    loads[0].wait()
    for s in range(seqs):
        toks[s, n] = tok[s]
    loads[1].wait()
    left = left_lanes(d)
    for p in range(pairs):
        t0, t1, t2 = (w[:, pl.ds(p * 3 * PAIR + i * PAIR, PAIR)].astype(F32) for i in range(3))
        cols = pl.ds(p * PAIR, PAIR)
        wp[0, :, cols] = jnp.where(left, t0, t1).astype(BF)
        wp[1, :, cols] = pltpu.roll(jnp.where(left, t2, t0), HD, 1).astype(BF)
        wp[2, :, cols] = jnp.where(left, t1, t2).astype(BF)
    emit(wp, wp_h)
    for cp in loads[6:]:
        cp.wait()
    bo_ref, g1_ref, s1_ref, bd_ref, g2_ref, s2_ref = (
        r[...].reshape(1, d) for r in (bo_v, g1_v, s1_v, bd_v, g2_v, s2_v))
    own = tok[...].reshape(rows, d)
    q[...] = ((dg(own, wp[0], 1, 0) + qvb_ref[0:1, :]).astype(BF) * 0.125).reshape(seqs, quarter, d)
    emit(q, q_h)

    def project(s, half):
        blocks = pl.ds(2 * half, 2)
        x = toks[s, blocks].reshape(2 * quarter, d)
        k[s, blocks] = dg(x, wp[1], 1, 0).astype(BF).reshape(2, quarter, d)
        v[s, blocks] = (dg(x, wp[2], 1, 0) + qvb_ref[1:2, :]).astype(BF).reshape(2, quarter, d)

    for s in range(seqs):
        send_core(s).wait_recv()
    for s in range(seqs):
        project(s, y)

    def fetch_far(s):
        copy_to(toks.at[s, y_n], toks.at[s, y_n], ys.at[s], yr.at[s], y_peer).wait_recv()
        forward_y(s).start()

    fetch_far(0)
    for s in range(seqs):
        copy_to(toks.at[s, far_n], toks.at[s, far_n], fs.at[s], fr.at[s], core_peer).wait_recv()
        project(s, 1 - y)
        if s + 1 < seqs:
            fetch_far(s + 1)
        emit(toks.at[s], toks_h.at[s])
        emit(k.at[s], k_h.at[s])
        emit(v.at[s], v_h.at[s])
        live = lax.broadcasted_iota(jnp.int32, (keys, 2 * quarter), 0) < len_ref[s]

        def unit(p, carry):
            cols = pl.ds(pl.multiple_of(p * PAIR, PAIR), PAIR)
            qs = stack_heads(q[s, :, cols])
            kp = k[s, :, :, cols].reshape(keys, PAIR)
            vp = v[s, :, :, cols].reshape(keys, PAIR)
            scores = jnp.where(live, dg(kp, qs, 1, 1), -1000000000.0)
            e = jnp.exp(scores - jnp.max(scores, axis=0, keepdims=True))
            probs = (e * (1.0 / jnp.sum(e, axis=0, keepdims=True))).astype(BF)
            pr[s, p] = probs
            ctx[s * quarter:(s + 1) * quarter, cols] = unstack_heads(dg(vp, probs, 0, 0)).astype(BF)
            return carry

        lax.fori_loop(0, pairs, unit, 0, unroll=UNROLL_ATT)
        emit(pr.at[s], p_h.at[s])
    emit(ctx, ctx_h)

    part[...] = jnp.zeros_like(part)
    chunk = 64
    chunks = rows // chunk
    loads[2].wait()
    for b in range(d // 256):
        cols = pl.ds(b * 256, 256)
        val[:, cols] = (dg(ctx[...], wo[:, cols], 1, 0) + bo_ref[:, b * 256:(b + 1) * 256]
                        + tok[:, :, cols].reshape(rows, 256).astype(F32))

    def norm1(i, carry):
        r = pl.ds(pl.multiple_of(i * chunk, chunk), chunk)
        normed, scale = center_scale(val[r])
        x = normed * g1_ref + s1_ref
        normed1[r] = normed
        scale1[r] = jnp.broadcast_to(scale, (chunk, 128))
        first[r] = x
        low1[r] = x.astype(BF)
        return carry

    lax.fori_loop(0, chunks, norm1, 0)
    emit(low1, first_h)
    emit(normed1, normed_h)
    emit(scale1, scale_h)
    loads[3].wait()

    def up(j, carry):
        cols = pl.ds(pl.multiple_of(j * 256, 256), 256)
        at = (j // 3, slice(None), pl.ds(pl.multiple_of(j % 3 * 256, 256), 256))
        pre = dg(low1[...], wu[:, cols], 1, 0) + bu_v[cols].reshape(1, 256)
        half = 0.5 + 0.5 * lax.erf(pre * root_half)
        act[at] = (pre * half).astype(BF)
        slope[at] = (half + pre * (jnp.exp(-0.5 * pre * pre) * inv_root_two_pi)).astype(BF)
        return carry

    lax.fori_loop(0, ff // 256, up, 0, unroll=UNROLL_UP)
    emit(act, act_h)
    emit(slope, slope_h)
    loads[4].wait()
    loads[5].wait()
    for b in range(d // 256):
        cols = pl.ds(b * 256, 256)
        val[:, cols] = bd_ref[:, b * 256:(b + 1) * 256] + first[:, cols] + sum(
            dg(act[i], wd[i * d:(i + 1) * d, cols], 1, 0) for i in range(ff // d))

    def norm2(i, carry):
        r = pl.ds(pl.multiple_of(i * chunk, chunk), chunk)
        normed, scale = center_scale(val[r])
        out[r] = (normed * g2_ref + s2_ref).astype(BF)
        s = i * chunk // quarter
        off = pl.multiple_of(i * chunk - s * quarter, chunk)
        pos = n * quarter + off + lax.broadcasted_iota(jnp.int32, (chunk, d), 0)
        d_out = jnp.where(pos < len_ref[s], cot[s, pl.ds(off, chunk)].astype(F32), 0.0)
        part[1] += fold(d_out * normed)
        part[2] += fold(d_out)
        d_second = scale * norm_grad(d_out * g2_ref, normed)
        dsec[r] = d_second
        low = d_second.astype(BF)
        dffn[r] = low
        part[0] += fold(low.astype(F32))
        return carry

    lax.fori_loop(0, chunks, norm2, 0)
    emit(out, out_h)
    emit(dffn, dffn_h)
    emit(dsec, dsec_h)
    for i in range(3):
        sums_ref[i:i + 1] = total(part[i])
    for s in range(seqs):
        send_y(s).wait_send()
        send_core(s).wait_send()
        forward_y(s).wait_send()
    for cp in outs:
        cp.wait()


def front_part(tokens, lengths, w, qvb, wo, bo, g1, s1, wu, bu, wd, bd, g2, s2, cot):
    seqs, quarter, d = tokens.shape
    rows, pairs, ff = seqs * quarter, d // PAIR, wu.shape[1]
    S = jax.ShapeDtypeStruct
    vm, hbm = pl.BlockSpec(memory_space=V), pl.BlockSpec(memory_space=ANY)
    own, keys, flat = (seqs, quarter, d), (seqs, 4, quarter, d), (rows, d)
    probs, hidden = (seqs, pairs, 4 * quarter, 2 * quarter), (ff // d, rows, d)
    return pl.pallas_call(
        front_kernel,
        out_shape=[S(keys, BF), S(own, BF), S(keys, BF), S(keys, BF), S(probs, BF), S((3, d, d), BF), S(flat, BF),
                   S(flat, BF), S(hidden, BF), S(hidden, BF), S(flat, BF), S(flat, BF), S(flat, F32), S(flat, F32),
                   S((rows, 128), F32), S((3, d), F32)],
        in_specs=[pl.BlockSpec(memory_space=pltpu.SMEM)] + [hbm] * 14,
        out_specs=[hbm] * 15 + [vm],
        scratch_shapes=[V(w.shape, BF), V((3, d, d), BF), V(keys, BF), V(own, BF), V(keys, BF), V(keys, BF),
                        V(probs, BF), V(own, BF), V(own, BF), V(wo.shape, BF), V(wu.shape, BF), V(wd.shape, BF),
                        V(flat, BF), V(flat, BF), V(hidden, BF), V(hidden, BF), V(flat, BF), V(flat, BF),
                        V(flat, F32), V(flat, F32), V((rows, 128), F32), V(flat, F32), V(flat, F32),
                        V((3, 8, d), F32), V((2, d), F32), V((d,), F32), V((d,), F32), V((d,), F32), V((ff,), F32),
                        V((d,), F32), V((d,), F32), V((d,), F32), DMA((14,))] + [DMA((seqs,))] * 6 + [DMA((11 + 4 * seqs,))],
        name="front_part",
        compiler_params=pltpu.CompilerParams(collective_id=1, has_side_effects=True, vmem_limit_bytes=56 << 20),
    )(lengths, tokens, cot, w, wo, wu, wd, qvb, bo, g1, s1, bu, bd, g2, s2)


LAGS = (0, 1, 3, 4, 6, 7, 8)
UNITS = 5
UNROLL_BACK = 1


def tail_kernel(act_h, dffn_h, wd_h, slope_h, first_h, wu_h, dsec_h, normed_h, scale_h, wo_h, ctx_h, q_h, toks_h,
                wp_h, k_h, v_h, p_h, g1_h, sums_h,
                od_hbm, ou_hbm, oo_hbm, oq_hbm, din_hbm, so_ref,
                a_buf, b_buf, dffn, first, ctx, datt, dsum, toks, q, kv, pr, wp, dq, dtok, wo, dsec, normed1,
                scale1, part, part_up, g1_v, sums_ref, g, r1, r2, r3, r4, sbuf, srecv, x1, x2,
                s1, q1, s2, q2, s3, q3, s4, q4, s5, q5, s6, q6, os_, ss, sq, xs, ls):
    pieces, _, _, R, C = g.shape
    seqs, quarter, d = q.shape
    rows, keys, pairs = seqs * quarter, 4 * quarter, d // PAIR
    nd = nu = act_h.shape[0]
    ff = nd * d
    h = R // 2
    hr, hc = h // 2, C // 2
    w, n = lax.axis_index("wide"), lax.axis_index("narrow")
    c, y, x, z = n % 2, n // 2, w % 2, (w // 2) % 4
    core_peer, y_peer, x_peer = (w, n + 1 - 2 * c), (w, n + 2 - 4 * y), (w + 1 - 2 * x, n)
    zs = [z + 1 - 2 * (z % 2), z + 2 - 4 * (z // 2), 3 - z]
    z_peers = [(w + 2 * (j - z), n) for j in zs]

    a_view, b_view = a_buf.reshape(nd, rows, d), b_buf.reshape(nu, rows, d)
    dk, dv = a_buf.reshape(seqs, keys, d), b_buf.reshape(seqs, keys, d)
    wd, kvs = kv.reshape(ff, d), kv.reshape(2, seqs, keys, d)
    k, v = kvs.at[0], kvs.at[1]
    wu = pr.reshape(ff // 256, d, 2 * quarter)
    prs = pr.reshape(seqs, pairs, keys, 2 * quarter)
    slope = dtok.reshape(nd, rows, d)
    dctx = first.reshape(seqs, quarter, d)
    early = [(act_h, a_view), (dffn_h, dffn), (wd_h, wd), (slope_h, slope), (first_h, first), (dsec_h, dsec),
             (normed_h, normed1), (scale_h, scale1), (wo_h, wo), (ctx_h, ctx), (q_h, q), (toks_h, toks),
             (wp_h, wp), (g1_h, g1_v), (sums_h, sums_ref)]
    loads = [pltpu.make_async_copy(s, t, ls.at[i]) for i, (s, t) in enumerate(early)]
    wu_loads = [pltpu.make_async_copy(wu_h.at[:, j * 256:(j + 1) * 256], wu.at[j], ls.at[len(early) + j])
                for j in range(ff // 256)]
    after = len(early) + ff // 256
    k_load, v_load, p_load = (pltpu.make_async_copy(s, t, ls.at[after + i]) for i, (s, t) in enumerate(
        ((k_h, k), (v_h, v), (p_h, prs))))
    loads[4:4] = wu_loads
    for cp in loads:
        cp.start()
    bar = pltpu.get_barrier_semaphore()
    for dev in [core_peer, y_peer, x_peer] + z_peers:
        pl.semaphore_signal(bar, inc=1, device_id=dev, device_id_type=MESH)

    def cut(j):
        return (pl.ds(pl.multiple_of(x * h + (j // 2) * hr, 16), hr), pl.ds(pl.multiple_of((j % 2) * hc, 128), hc))

    near = pl.ds(pl.multiple_of(x * h, 16), h)
    away = pl.ds(pl.multiple_of((1 - x) * h, 16), h)

    def c1(p):
        return copy_to(g.at[p, 1 - c], r1.at[p], s1.at[p], q1.at[p], core_peer)

    def c2(p):
        return copy_to(g.at[p, c, 1 - y], r2.at[p], s2.at[p], q2.at[p], y_peer)

    def c3(p):
        return copy_to(g.at[p, c, y, away], r3.at[p], s3.at[p], q3.at[p], x_peer)

    def c4(p, e):
        rr, cc = cut(zs[e])
        return copy_to(g.at[p, c, y, rr, cc], r4.at[p, e], s4.at[p, e], q4.at[p, e], z_peers[e])

    def c5(p, e, j):
        rr, cc = cut(j)
        return copy_to(r1.at[p, 0, rr, cc], r1.at[p, 0, rr, cc], s5.at[p, e], q5.at[p, e], z_peers[e])

    def c6(p, rr):
        return copy_to(r1.at[p, 0, rr], r1.at[p, 0, rr], s6.at[p], q6.at[p], x_peer)

    def store(p, dst):
        return pltpu.make_async_copy(r1.at[p, 0], dst, os_.at[p])

    def st1(p):
        c1(p).wait_recv()
        g[p, c] = (g[p, c].astype(F32) + r1[p].astype(F32)).astype(BF)
        c2(p).start()

    def st2(p):
        c2(p).wait_recv()
        g[p, c, y] = (g[p, c, y].astype(F32) + r2[p].astype(F32)).astype(BF)
        c3(p).start()

    def st3(p):
        c3(p).wait_recv()
        g[p, c, y, near] = (g[p, c, y, near].astype(F32) + r3[p].astype(F32)).astype(BF)
        for e in (1, 2, 0):
            c4(p, e).start()

    def st4(p):
        for e in range(3):
            c4(p, e).wait_recv()
        rr, cc = cut(z)
        t = g[p, c, y, rr, cc].astype(F32) + r4[p, 0].astype(F32) + r4[p, 1].astype(F32) + r4[p, 2].astype(F32)
        r1[p, 0, rr, cc] = t.astype(BF)
        for e in (1, 2, 0):
            c5(p, e, z).start()

    def st5(p):
        for e in range(3):
            c5(p, e, zs[e]).wait_recv()
        c6(p, near).start()

    def st6(p):
        c6(p, away).wait_recv()

        @pl.when(p < nd)
        def down():
            store(p, od_hbm.at[pl.ds(p * R, R)]).start()

        @pl.when(jnp.logical_and(p >= nd, p < nd + nu))
        def up():
            store(p, ou_hbm.at[:, pl.ds(pl.multiple_of((p - nd) * C, C), C)]).start()

        @pl.when(p == nd + nu)
        def out():
            store(p, oo_hbm).start()

        @pl.when(p > nd + nu)
        def qkv():
            store(p, oq_hbm.at[:, pl.ds(pl.multiple_of((p - nd - nu - 1) * C, C), C)]).start()

    stages = [None, st1, st2, st3, st4, st5, st6]

    loads[0].wait()
    loads[1].wait()

    def down_block(i, carry):
        t = dg(a_view[i], dffn[...], 0, 0).astype(BF)
        for j in range(nd):
            g[j, i % 2, i // 2] = t[j * R:(j + 1) * R]
        return carry

    lax.fori_loop(0, nd, down_block, 0)
    pl.semaphore_wait(bar, 6)
    for p in range(nd):
        c1(p).start()
    loads[2].wait()
    loads[3].wait()

    def up_back(j, carry):
        at = (j // 3, slice(None), pl.ds(pl.multiple_of(j % 3 * 256, 256), 256))
        low = (dg(dffn[...], wd[pl.ds(pl.multiple_of(j * 256, 256), 256)], 1, 1) * slope[at].astype(F32)).astype(BF)
        b_view[at] = low
        part_up[:, pl.ds(pl.multiple_of(j * 256, 256), 256)] = fold(low.astype(F32))
        return carry

    lax.fori_loop(0, ff // 512, up_back, 0, unroll=UNROLL_BACK)
    st1(0)
    st1(1)
    lax.fori_loop(ff // 512, ff // 256, up_back, 0, unroll=UNROLL_BACK)
    k_load.start()
    v_load.start()
    for cp in loads[4:]:
        cp.wait()

    def row_block(p, t):
        for j in range(4):
            g[p, j % 2, j // 2] = t[j * R:(j + 1) * R].astype(BF)

    def up_block(i, carry):
        row_block(nd + i, dg(first[...], b_view[i], 0, 0))
        c1(nd + i).start()
        return carry

    lax.fori_loop(0, nu, up_block, 0)

    def rows_back():
        for b in range(d // 256):
            cols = pl.ds(b * 256, 256)
            dsum[:, cols] = dsec[:, cols] + sum(
                dg(b_view[j // 3, :, j % 3 * 256:(j % 3 + 1) * 256], wu[j, cols, :], 1, 1) for j in range(ff // 256))
        p_load.start()
        part[...] = jnp.zeros_like(part)
        chunk = 64
        gain = g1_v[...].reshape(1, d)

        def norm1_back(i, carry):
            r = pl.ds(pl.multiple_of(i * chunk, chunk), chunk)
            d_first, normed = dsum[r], normed1[r]
            part[1] += fold(d_first * normed)
            part[2] += fold(d_first)
            d_sum = scale1[r, :1] * norm_grad(d_first * gain, normed)
            dsum[r] = d_sum
            low = d_sum.astype(BF)
            datt[r] = low
            part[0] += fold(low.astype(F32))
            return carry

        lax.fori_loop(0, rows // chunk, norm1_back, 0)
        row_block(nd + nu, dg(ctx[...], datt[...], 0, 0))
        c1(nd + nu).start()
        dctx[...] = dg(datt[...], wo[...], 1, 1).astype(BF).reshape(seqs, quarter, d)
        k_load.wait()
        v_load.wait()
        p_load.wait()

    def unit(u, carry):
        s, p = u // pairs, u % pairs
        cols = pl.ds(pl.multiple_of(p * PAIR, PAIR), PAIR)
        qs = stack_heads(q[s, :, cols])
        ds = stack_heads(dctx[s, :, cols])
        low = prs[s, p]
        probs = low.astype(F32)
        t = probs * dg(v[s, :, cols], ds, 1, 1)
        d_raw = (t - probs * jnp.sum(t, axis=0, keepdims=True)).astype(BF)
        dv[s, :, cols] = dg(low, ds, 1, 0).astype(BF)
        dk[s, :, cols] = dg(d_raw, qs, 1, 0).astype(BF)
        dq[s, :, cols] = (unstack_heads(dg(k[s, :, cols], d_raw, 0, 0)) * 0.125).astype(BF)
        return carry

    def qkv_piece(i):
        cols = pl.ds(i * 2 * PAIR, 2 * PAIR)
        allt = toks[...].reshape(seqs * keys, d)
        ga = dg(toks[:, pl.ds(pl.multiple_of(n * quarter, quarter), quarter)].reshape(rows, d), dq[:, :, cols].reshape(rows, 2 * PAIR), 0, 0)
        gb = dg(allt, a_buf[:, cols], 0, 0)
        gc = dg(allt, b_buf[:, cols], 0, 0)
        left = left_lanes(R)
        p = nd + nu + 1 + i
        for e in range(4):
            rr = slice(e * R, (e + 1) * R)
            for j in range(2):
                sl = slice(j * PAIR, (j + 1) * PAIR)
                aj, bj, cj = ga[rr, sl], pltpu.roll(gb[rr, sl], HD, 1), gc[rr, sl]
                for t, val in enumerate((jnp.where(left, aj, bj), jnp.where(left, cj, aj), jnp.where(left, bj, cj))):
                    g[p, e % 2, e // 2, :, pl.ds((3 * j + t) * PAIR, PAIR)] = val.astype(BF)
        c1(p).start()

    cx1 = copy_to(dtok.at[:, 1 - c], x1, xs.at[0], xs.at[1], core_peer)
    cx2 = copy_to(dtok.at[1 - y, c], x2, xs.at[2], xs.at[3], y_peer)

    def input_part():
        def one(s, carry):
            t = dg(dk[s], wp[1], 1, 1) + dg(dv[s], wp[2], 1, 1)
            for e in range(4):
                dtok[e // 2, e % 2, s] = t[e * quarter:(e + 1) * quarter].astype(BF)
            return carry

        lax.fori_loop(0, seqs, one, 0)
        cx1.start()
        dsum[...] += dg(dq[...].reshape(rows, d), wp[0], 1, 1)

    def small(i, slot, dev):
        return copy_to(sbuf.at[i], srecv.at[slot], ss.at[slot], sq.at[slot], dev)

    def sums0():
        sbuf[0, 0:1] = jnp.sum(fold(dq[...].reshape(rows, d).astype(F32)), axis=0, keepdims=True)

        def add(s, acc):
            return acc + fold(dv[s].astype(F32))

        acc = lax.fori_loop(0, seqs, add, jnp.zeros((8, d), F32))
        sbuf[0, 1:2] = jnp.sum(acc, axis=0, keepdims=True)
        for i in range(3):
            sbuf[0, 2 + i:3 + i] = total(part[i])
        for i in range(nu):
            sbuf[0, 5 + i:6 + i] = total(part_up[:, i * d:(i + 1) * d])
        sbuf[0, 5 + nu:] = sums_ref[...]
        small(0, 0, core_peer).start()

    def sums1():
        small(0, 0, core_peer).wait_recv()
        sbuf[1] = sbuf[0] + srecv[0]
        small(1, 1, y_peer).start()

    def sums2():
        small(1, 1, y_peer).wait_recv()
        sbuf[2] = sbuf[1] + srecv[1]
        small(2, 2, x_peer).start()

    def sums3():
        small(2, 2, x_peer).wait_recv()
        sbuf[3] = sbuf[2] + srecv[2]
        for e in range(3):
            small(3, 3 + e, z_peers[e]).start()

    def add_x1():
        cx1.wait_recv()

        def add(i, carry):
            a, b = i // seqs, i % seqs
            dtok[a, c, b] = (dtok[a, c, b].astype(F32) + x1[a, b].astype(F32)).astype(BF)
            return carry

        lax.fori_loop(0, 2 * seqs, add, 0)

    units = seqs * pairs
    slots_of_units = -(-units // UNITS)
    extra = {3: [rows_back], 8: [lambda: qkv_piece(0), lambda: qkv_piece(1)],
             9: [lambda: qkv_piece(2), sums0, input_part], 10: [add_x1, sums1], 12: [sums2], 13: [cx2.start, sums3]}

    def slot(t, carry):
        for i in (6, 5, 4, 3, 2, 1):
            p = t - LAGS[i]

            @pl.when(jnp.logical_and(p >= 0, p < pieces))
            def run():
                stages[i](p)

        @pl.when(jnp.logical_and(t > 3, t <= 3 + slots_of_units))
        def attention():
            lo = (t - 4) * UNITS
            lax.fori_loop(lo, jnp.minimum(lo + UNITS, units), unit, 0)

        for at, todo in extra.items():
            @pl.when(t == at)
            def more():
                for f in todo:
                    f()
        return carry

    lax.fori_loop(3, pieces + LAGS[6], slot, 0)
    cx2.wait_recv()

    def out_x(i, carry):
        r = pl.ds(pl.multiple_of(i * quarter, quarter), quarter)
        x1[0, i] = (dsum[r] + dtok[y, c, i].astype(F32) + x2[i].astype(F32)).astype(BF)
        return carry

    lax.fori_loop(0, seqs, out_x, 0)
    din_out = pltpu.make_async_copy(x1.at[0], din_hbm, xs.at[4])
    din_out.start()
    for e in range(3):
        small(3, 3 + e, z_peers[e]).wait_recv()
    so_ref[...] = sbuf[3] + srecv[3] + srecv[4] + srecv[5]
    small(0, 0, core_peer).wait_send()
    small(1, 1, y_peer).wait_send()
    small(2, 2, x_peer).wait_send()
    for e in range(3):
        small(3, 3 + e, z_peers[e]).wait_send()
    cx1.wait_send()
    cx2.wait_send()

    def drain(p, carry):
        c1(p).wait_send()
        c2(p).wait_send()
        c3(p).wait_send()
        c6(p, near).wait_send()
        store(p, oo_hbm).wait()
        for e in range(3):
            c4(p, e).wait_send()
            c5(p, e, z).wait_send()
        return carry

    lax.fori_loop(0, pieces, drain, 0)
    din_out.wait()


def tail_part(act, dffn, wd, slope, first, wu, dsec, normed, scale, wo, ctx, q, toks, wp, k, v, probs, g1, sums):
    seqs, quarter, d = q.shape
    rows, keys = seqs * quarter, 4 * quarter
    R = d // 4
    nd = nu = act.shape[0]
    ff = nd * d
    n = nd + nu + 4
    h = R // 2
    all_rows = (6 + nu + sums.shape[0] - 1, d)
    vm, hbm = pl.BlockSpec(memory_space=V), pl.BlockSpec(memory_space=ANY)
    S = jax.ShapeDtypeStruct
    own, every, flat = (seqs, quarter, d), (seqs, keys, d), (rows, d)
    return pl.pallas_call(
        tail_kernel,
        out_shape=(S((nd * R, d), BF), S((R, nu * d), BF), S((R, d), BF), S((R, 3 * d), BF), S(own, BF),
                   S(all_rows, F32)),
        in_specs=[hbm] * 19,
        out_specs=(hbm, hbm, hbm, hbm, hbm, vm),
        scratch_shapes=[V((seqs * keys, d), BF), V((seqs * keys, d), BF), V(flat, BF), V(flat, BF), V(flat, BF),
                        V(flat, BF), V(flat, F32), V(every, BF), V(own, BF),
                        V((2 * seqs * keys, d), BF), V((seqs * (d // PAIR) * keys, 2 * quarter), BF), V((3, d, d), BF),
                        V(own, BF), V((2, 2) + own, BF), V(wo.shape, BF), V(flat, F32), V(flat, F32),
                        V((rows, 128), F32), V((3, 8, d), F32), V((8, ff), F32), V((d,), F32), V(sums.shape, F32),
                        V((n, 2, 2, R, d), BF), V((n, 2, R, d), BF), V((n, R, d), BF), V((n, h, d), BF),
                        V((n, 3, h // 2, d // 2), BF), V((4,) + all_rows, F32), V((6,) + all_rows, F32),
                        V((2,) + own, BF), V(own, BF)]
        + [DMA((n,))] * 6 + [DMA((n, 3))] * 4 + [DMA((n,))] * 3
        + [DMA((6,))] * 2 + [DMA((5,)), DMA((18 + ff // 256,))],
        name="tail_part",
        compiler_params=pltpu.CompilerParams(collective_id=2, has_side_effects=True, vmem_limit_bytes=63 << 20),
    )(act, dffn, wd, slope, first, wu, dsec, normed, scale, wo, ctx, q, toks, wp, k, v, probs,
      g1, sums)


def finish_kernel(d_h, u_h, o_h, q_h, sums_ref, fd, fu, fo, fq, qvb, outb, n1g, n1s, upb, downb, n2g, n2s,
                  low, full, ls, os_):
    R, C = low.shape[1:]
    nd, nu = d_h.shape[0] // R, u_h.shape[1] // C
    cut = lambda ref, i: ref.at[:, pl.ds(i * C, C)]
    ends = ([(d_h.at[pl.ds(i * R, R)], fd.at[pl.ds(i * R, R)]) for i in range(nd)]
            + [(cut(u_h, i), cut(fu, i)) for i in range(nu)] + [(o_h, fo)]
            + [(cut(q_h, i), cut(fq, i)) for i in range(3)])
    loads = [pltpu.make_async_copy(s, low.at[i], ls.at[i]) for i, (s, _) in enumerate(ends)]
    stores = [pltpu.make_async_copy(full.at[i], t, os_.at[i]) for i, (_, t) in enumerate(ends)]
    for cp in loads:
        cp.start()
    n = lax.axis_index("narrow")
    for i in range(4):
        @pl.when(n == i)
        def pick():
            at = slice(i * R, (i + 1) * R)
            qvb[...] = sums_ref[0:2, at]
            for j, ref in ((2, outb), (3, n1g), (4, n1s), (5 + nu, downb), (6 + nu, n2g), (7 + nu, n2s)):
                ref[...] = sums_ref[j:j + 1, at]
            upb[...] = sums_ref[5 + i:6 + i]
    for i, (a, b) in enumerate(zip(loads, stores)):
        a.wait()
        full[i] = low[i].astype(F32)
        b.start()
    for cp in stores:
        cp.wait()


def finish_part(down, up, out, qkv, sums):
    R, d = out.shape
    n = down.shape[0] // R + up.shape[1] // d + 4
    vm, hbm = pl.BlockSpec(memory_space=V), pl.BlockSpec(memory_space=ANY)
    S = jax.ShapeDtypeStruct
    shapes = [S(a.shape, F32) for a in (down, up, out, qkv)] + [S((2, R), F32)] + [S((1, R), F32)] * 3
    shapes += [S((1, d), F32)] + [S((1, R), F32)] * 3
    return pl.pallas_call(
        finish_kernel,
        out_shape=shapes,
        in_specs=[hbm] * 4 + [vm],
        out_specs=[hbm] * 4 + [vm] * 8,
        scratch_shapes=[V((n, R, d), BF), V((n, R, d), F32), DMA((n,)), DMA((n,))],
        name="finish_part",
        compiler_params=pltpu.CompilerParams(vmem_limit_bytes=60 << 20),
    )(down, up, out, qkv, sums)


def local(tokens, lengths, qkv_weight, qv_bias, out_weight, out_bias, norm1_gain, norm1_shift, up_weight, up_bias,
          down_weight, down_bias, norm2_gain, norm2_shift, cotangent):
    seqs, quarter, d = tokens.shape
    own, every = (seqs, quarter, d), (seqs, 4 * quarter, d)
    (toks, q, k, v, probs, wp, ctx, first, act, slope, output, dffn, dsec, normed, scale, sums) = front_part(
        tokens, lengths, qkv_weight, qv_bias, out_weight, out_bias, norm1_gain, norm1_shift, up_weight, up_bias,
        down_weight, down_bias, norm2_gain, norm2_shift, cotangent)
    down, up, out, qkv, input_grad, sums = tail_part(
        act, dffn, down_weight, slope, first, up_weight, dsec, normed, scale, out_weight, ctx, q, toks.reshape(every),
        wp, k.reshape(every), v.reshape(every), probs, norm1_gain, sums)
    wide = lax.axis_size("wide")
    if wide > 8:
        groups = [[j * 8 + i for j in range(wide // 8)] for i in range(8)]
        down, up, out, qkv = (
            lax.psum(a.astype(F32), "wide", axis_index_groups=groups).astype(BF) for a in (down, up, out, qkv))
        sums = lax.psum(sums, "wide", axis_index_groups=groups)
    down, up, out, qkv, qvb, outb, n1g, n1s, upb, downb, n2g, n2s = finish_part(down, up, out, qkv, sums)
    flat = lambda a: a.reshape(-1)
    return (output.reshape(own), input_grad, qkv, qvb, out, flat(outb), flat(n1g), flat(n1s), up, flat(upb), down,
            flat(downb), flat(n2g), flat(n2s))


def solution(mesh):
    return jax.shard_map(
        local,
        mesh=mesh,
        in_specs=(
            P("wide", "narrow", None),
            P("wide"),
            P(),
            P(),
            P(),
            P(),
            P(),
            P(),
            P(),
            P(),
            P(),
            P(),
            P(),
            P(),
            P("wide", "narrow", None),
        ),
        out_specs=(
            P("wide", "narrow", None),
            P("wide", "narrow", None),
            P("narrow", None),
            P(None, "narrow"),
            P("narrow", None),
            P("narrow"),
            P("narrow"),
            P("narrow"),
            P("narrow", None),
            P("narrow"),
            P("narrow", None),
            P("narrow"),
            P("narrow"),
            P("narrow"),
        ),
        check_vma=False,
    )
```

```python
import functools

import jax
import jax.numpy as jnp
from jax import lax
from jax.experimental import pallas as pl
from jax.experimental.pallas import tpu as pltpu
from jax.sharding import PartitionSpec as P

H = 12
HD = 64
PAIR = 2 * HD
epsilon = 1e-12
root_half = 0.7071067811865476
inv_root_two_pi = 0.3989422804014327
MESH = pl.DeviceIdType.MESH
F32 = jnp.float32
BF = jnp.bfloat16
V = pltpu.VMEM
DMA = pltpu.SemaphoreType.DMA
ANY = pl.ANY
UNROLL_ATT = 6
UNROLL_UP = 3


def dg(a, b, ca, cb):
    return lax.dot_general(a, b, (((ca,), (cb,)), ((), ())), preferred_element_type=F32)


def copy_to(src, dst, ss, rs, dev):
    return pltpu.make_async_remote_copy(
        src_ref=src, dst_ref=dst, send_sem=ss, recv_sem=rs, device_id=dev, device_id_type=MESH)


def left_lanes(rows):
    return lax.broadcasted_iota(jnp.int32, (rows, PAIR), 1) < HD


def stack_heads(x):
    left = left_lanes(x.shape[0])
    zero = jnp.zeros_like(x)
    return jnp.concatenate([jnp.where(left, x, zero), jnp.where(left, zero, x)], axis=0)


def unstack_heads(x_t):
    q = x_t.shape[1] // 2
    top = lax.broadcasted_iota(jnp.int32, (PAIR, q), 0) < HD
    return jnp.where(top, x_t[:, :q], x_t[:, q:]).T


def fold(x):
    return jnp.sum(x.reshape(x.shape[0] // 8, 8, x.shape[1]), axis=0)


def total(x):
    return jnp.sum(x, axis=0, keepdims=True)


def center_scale(v):
    center = v - jnp.mean(v, axis=-1, keepdims=True)
    scale = lax.rsqrt(jnp.mean(center * center, axis=-1, keepdims=True) + epsilon)
    return center * scale, scale


def norm_grad(g, normed):
    return g - jnp.mean(g, axis=-1, keepdims=True) - normed * jnp.mean(g * normed, axis=-1, keepdims=True)


def front_kernel(len_ref, tok_h, cot_h, w_h, wo_h, wu_h, wd_h, qvb_h, bo_h, g1_h, s1_h, bu_h, bd_h, g2_h, s2_h,
                 toks_h, q_h, k_h, v_h, p_h, wp_h, ctx_h, first_h, act_h, slope_h, out_h, dffn_h, dsec_h, normed_h,
                 scale_h, sums_ref,
                 w, wp, toks, q, k, v, pr, tok, cot, wo, wu, wd, ctx, low1, act, slope, out, dffn, dsec, normed1,
                 scale1, val, first, part, qvb_ref, bo_v, g1_v, s1_v, bu_v, bd_v, g2_v, s2_v,
                 ls, cs, cr, ys, yr, fs, fr, os_):
    seqs, quarter, d = tok.shape
    rows, keys, pairs = seqs * quarter, 4 * quarter, d // PAIR
    ff = wu.shape[1]
    wide, n = lax.axis_index("wide"), lax.axis_index("narrow")
    c, y = n % 2, n // 2
    core_n, y_n = n + 1 - 2 * c, n + 2 - 4 * y
    far_n = core_n + 2 - 4 * y
    core_peer, y_peer = (wide, core_n), (wide, y_n)
    loads = [pltpu.make_async_copy(s, t, ls.at[i]) for i, (s, t) in enumerate(
        ((tok_h, tok), (w_h, w), (wo_h, wo), (wu_h, wu), (cot_h, cot), (wd_h, wd), (qvb_h, qvb_ref), (bo_h, bo_v),
         (g1_h, g1_v), (s1_h, s1_v), (bu_h, bu_v), (bd_h, bd_v), (g2_h, g2_v), (s2_h, s2_v)))]
    outs = []

    def emit(src, dst):
        cp = pltpu.make_async_copy(src, dst, os_.at[len(outs)])
        cp.start()
        outs.append(cp)

    for cp in loads[:2]:
        cp.start()
    bar = pltpu.get_barrier_semaphore()
    for peer in (core_peer, y_peer):
        pl.semaphore_signal(bar, inc=1, device_id=peer, device_id_type=MESH)
    pl.semaphore_wait(bar, 2)

    def send_y(s):
        return copy_to(tok_h.at[s], toks.at[s, n], ys.at[s], yr.at[s], y_peer)

    def send_core(s):
        return copy_to(tok_h.at[s], toks.at[s, n], cs.at[s], cr.at[s], core_peer)

    def forward_y(s):
        return copy_to(toks.at[s, y_n], toks.at[s, y_n], fs.at[s], fr.at[s], core_peer)

    for s in range(seqs):
        send_y(s).start()
        send_core(s).start()
    for cp in loads[2:]:
        cp.start()
    loads[0].wait()
    for s in range(seqs):
        toks[s, n] = tok[s]
    loads[1].wait()
    left = left_lanes(d)
    for p in range(pairs):
        t0, t1, t2 = (w[:, pl.ds(p * 3 * PAIR + i * PAIR, PAIR)].astype(F32) for i in range(3))
        cols = pl.ds(p * PAIR, PAIR)
        wp[0, :, cols] = jnp.where(left, t0, t1).astype(BF)
        wp[1, :, cols] = pltpu.roll(jnp.where(left, t2, t0), HD, 1).astype(BF)
        wp[2, :, cols] = jnp.where(left, t1, t2).astype(BF)
    emit(wp, wp_h)
    for cp in loads[6:]:
        cp.wait()
    bo_ref, g1_ref, s1_ref, bd_ref, g2_ref, s2_ref = (
        r[...].reshape(1, d) for r in (bo_v, g1_v, s1_v, bd_v, g2_v, s2_v))
    own = tok[...].reshape(rows, d)
    q[...] = ((dg(own, wp[0], 1, 0) + qvb_ref[0:1, :]).astype(BF) * 0.125).reshape(seqs, quarter, d)
    emit(q, q_h)

    def project(s, half):
        blocks = pl.ds(2 * half, 2)
        x = toks[s, blocks].reshape(2 * quarter, d)
        k[s, blocks] = dg(x, wp[1], 1, 0).astype(BF).reshape(2, quarter, d)
        v[s, blocks] = (dg(x, wp[2], 1, 0) + qvb_ref[1:2, :]).astype(BF).reshape(2, quarter, d)

    for s in range(seqs):
        send_core(s).wait_recv()
    for s in range(seqs):
        project(s, y)

    def fetch_far(s):
        copy_to(toks.at[s, y_n], toks.at[s, y_n], ys.at[s], yr.at[s], y_peer).wait_recv()
        forward_y(s).start()

    fetch_far(0)
    for s in range(seqs):
        copy_to(toks.at[s, far_n], toks.at[s, far_n], fs.at[s], fr.at[s], core_peer).wait_recv()
        project(s, 1 - y)
        if s + 1 < seqs:
            fetch_far(s + 1)
        emit(toks.at[s], toks_h.at[s])
        emit(k.at[s], k_h.at[s])
        emit(v.at[s], v_h.at[s])
        live = lax.broadcasted_iota(jnp.int32, (keys, 2 * quarter), 0) < len_ref[s]

        def unit(p, carry):
            cols = pl.ds(pl.multiple_of(p * PAIR, PAIR), PAIR)
            qs = stack_heads(q[s, :, cols])
            kp = k[s, :, :, cols].reshape(keys, PAIR)
            vp = v[s, :, :, cols].reshape(keys, PAIR)
            scores = jnp.where(live, dg(kp, qs, 1, 1), -1000000000.0)
            e = jnp.exp(scores - jnp.max(scores, axis=0, keepdims=True))
            probs = (e * (1.0 / jnp.sum(e, axis=0, keepdims=True))).astype(BF)
            pr[s, p] = probs
            ctx[s * quarter:(s + 1) * quarter, cols] = unstack_heads(dg(vp, probs, 0, 0)).astype(BF)
            return carry

        lax.fori_loop(0, pairs, unit, 0, unroll=UNROLL_ATT)
        emit(pr.at[s], p_h.at[s])
    emit(ctx, ctx_h)

    part[...] = jnp.zeros_like(part)
    chunk = 64
    chunks = rows // chunk
    loads[2].wait()
    for b in range(d // 256):
        cols = pl.ds(b * 256, 256)
        val[:, cols] = (dg(ctx[...], wo[:, cols], 1, 0) + bo_ref[:, b * 256:(b + 1) * 256]
                        + tok[:, :, cols].reshape(rows, 256).astype(F32))

    def norm1(i, carry):
        r = pl.ds(pl.multiple_of(i * chunk, chunk), chunk)
        normed, scale = center_scale(val[r])
        x = normed * g1_ref + s1_ref
        normed1[r] = normed
        scale1[r] = jnp.broadcast_to(scale, (chunk, 128))
        first[r] = x
        low1[r] = x.astype(BF)
        return carry

    lax.fori_loop(0, chunks, norm1, 0)
    emit(low1, first_h)
    emit(normed1, normed_h)
    emit(scale1, scale_h)
    loads[3].wait()

    def up(j, carry):
        cols = pl.ds(pl.multiple_of(j * 256, 256), 256)
        at = (j // 3, slice(None), pl.ds(pl.multiple_of(j % 3 * 256, 256), 256))
        pre = dg(low1[...], wu[:, cols], 1, 0) + bu_v[cols].reshape(1, 256)
        half = 0.5 + 0.5 * lax.erf(pre * root_half)
        act[at] = (pre * half).astype(BF)
        slope[at] = (half + pre * (jnp.exp(-0.5 * pre * pre) * inv_root_two_pi)).astype(BF)
        return carry

    lax.fori_loop(0, ff // 256, up, 0, unroll=UNROLL_UP)
    emit(act, act_h)
    emit(slope, slope_h)
    loads[4].wait()
    loads[5].wait()
    for b in range(d // 256):
        cols = pl.ds(b * 256, 256)
        val[:, cols] = bd_ref[:, b * 256:(b + 1) * 256] + first[:, cols] + sum(
            dg(act[i], wd[i * d:(i + 1) * d, cols], 1, 0) for i in range(ff // d))

    def norm2(i, carry):
        r = pl.ds(pl.multiple_of(i * chunk, chunk), chunk)
        normed, scale = center_scale(val[r])
        out[r] = (normed * g2_ref + s2_ref).astype(BF)
        s = i * chunk // quarter
        off = pl.multiple_of(i * chunk - s * quarter, chunk)
        pos = n * quarter + off + lax.broadcasted_iota(jnp.int32, (chunk, d), 0)
        d_out = jnp.where(pos < len_ref[s], cot[s, pl.ds(off, chunk)].astype(F32), 0.0)
        part[1] += fold(d_out * normed)
        part[2] += fold(d_out)
        d_second = scale * norm_grad(d_out * g2_ref, normed)
        dsec[r] = d_second
        low = d_second.astype(BF)
        dffn[r] = low
        part[0] += fold(low.astype(F32))
        return carry

    lax.fori_loop(0, chunks, norm2, 0)
    emit(out, out_h)
    emit(dffn, dffn_h)
    emit(dsec, dsec_h)
    for i in range(3):
        sums_ref[i:i + 1] = total(part[i])
    for s in range(seqs):
        send_y(s).wait_send()
        send_core(s).wait_send()
        forward_y(s).wait_send()
    for cp in outs:
        cp.wait()


def front_part(tokens, lengths, w, qvb, wo, bo, g1, s1, wu, bu, wd, bd, g2, s2, cot):
    seqs, quarter, d = tokens.shape
    rows, pairs, ff = seqs * quarter, d // PAIR, wu.shape[1]
    S = jax.ShapeDtypeStruct
    vm, hbm = pl.BlockSpec(memory_space=V), pl.BlockSpec(memory_space=ANY)
    own, keys, flat = (seqs, quarter, d), (seqs, 4, quarter, d), (rows, d)
    probs, hidden = (seqs, pairs, 4 * quarter, 2 * quarter), (ff // d, rows, d)
    return pl.pallas_call(
        front_kernel,
        out_shape=[S(keys, BF), S(own, BF), S(keys, BF), S(keys, BF), S(probs, BF), S((3, d, d), BF), S(flat, BF),
                   S(flat, BF), S(hidden, BF), S(hidden, BF), S(flat, BF), S(flat, BF), S(flat, F32), S(flat, F32),
                   S((rows, 128), F32), S((3, d), F32)],
        in_specs=[pl.BlockSpec(memory_space=pltpu.SMEM)] + [hbm] * 14,
        out_specs=[hbm] * 15 + [vm],
        scratch_shapes=[V(w.shape, BF), V((3, d, d), BF), V(keys, BF), V(own, BF), V(keys, BF), V(keys, BF),
                        V(probs, BF), V(own, BF), V(own, BF), V(wo.shape, BF), V(wu.shape, BF), V(wd.shape, BF),
                        V(flat, BF), V(flat, BF), V(hidden, BF), V(hidden, BF), V(flat, BF), V(flat, BF),
                        V(flat, F32), V(flat, F32), V((rows, 128), F32), V(flat, F32), V(flat, F32),
                        V((3, 8, d), F32), V((2, d), F32), V((d,), F32), V((d,), F32), V((d,), F32), V((ff,), F32),
                        V((d,), F32), V((d,), F32), V((d,), F32), DMA((14,))] + [DMA((seqs,))] * 6 + [DMA((11 + 4 * seqs,))],
        name="front_part",
        compiler_params=pltpu.CompilerParams(collective_id=1, has_side_effects=True, vmem_limit_bytes=56 << 20),
    )(lengths, tokens, cot, w, wo, wu, wd, qvb, bo, g1, s1, bu, bd, g2, s2)


LAGS = (0, 1, 3, 4, 5, 7, 11)
UNITS = 4
ORDER = (3, 1, 6, 4, 2, 5)
UNROLL_BACK = 1


def tail_kernel(act_h, dffn_h, wd_h, slope_h, first_h, wu_h, dsec_h, normed_h, scale_h, wo_h, ctx_h, q_h, toks_h,
                wp_h, k_h, v_h, p_h, g1_h, sums_h,
                od_hbm, ou_hbm, oo_hbm, oq_hbm, din_hbm, so_ref,
                a_buf, b_buf, dffn, first, ctx, datt, dsum, toks, q, kv, pr, wp, dq, dtok, wo, dsec, normed1,
                scale1, part, part_up, g1_v, sums_ref, g, r1, r2, r3, r4, sbuf, srecv, x1, x2,
                s1, q1, s2, q2, s3, q3, s4, q4, s5, q5, s6, q6, os_, ss, sq, xs, ls):
    pieces, _, _, R, C = g.shape
    seqs, quarter, d = q.shape
    rows, keys, pairs = seqs * quarter, 4 * quarter, d // PAIR
    nd = nu = act_h.shape[0]
    ff = nd * d
    h = R // 2
    hr, hc = h // 2, C // 2
    w, n = lax.axis_index("wide"), lax.axis_index("narrow")
    c, y, x, z = n % 2, n // 2, w % 2, (w // 2) % 4
    core_peer, y_peer, x_peer = (w, n + 1 - 2 * c), (w, n + 2 - 4 * y), (w + 1 - 2 * x, n)
    zs = [z + 1 - 2 * (z % 2), z + 2 - 4 * (z // 2), 3 - z]
    z_peers = [(w + 2 * (j - z), n) for j in zs]

    a_view, b_view = a_buf.reshape(nd, rows, d), b_buf.reshape(nu, rows, d)
    dk, dv = a_buf.reshape(seqs, keys, d), b_buf.reshape(seqs, keys, d)
    wd, kvs = kv.reshape(ff, d), kv.reshape(2, seqs, keys, d)
    k, v = kvs.at[0], kvs.at[1]
    wu = pr.reshape(ff // 256, d, 2 * quarter)
    prs = pr.reshape(seqs, pairs, keys, 2 * quarter)
    slope = dtok.reshape(nd, rows, d)
    dctx = first.reshape(seqs, quarter, d)
    early = [(act_h, a_view), (dffn_h, dffn), (wd_h, wd), (slope_h, slope), (first_h, first), (dsec_h, dsec),
             (normed_h, normed1), (scale_h, scale1), (wo_h, wo), (ctx_h, ctx), (q_h, q), (toks_h, toks),
             (wp_h, wp), (g1_h, g1_v), (sums_h, sums_ref)]
    loads = [pltpu.make_async_copy(s, t, ls.at[i]) for i, (s, t) in enumerate(early)]
    wu_loads = [pltpu.make_async_copy(wu_h.at[:, j * 256:(j + 1) * 256], wu.at[j], ls.at[len(early) + j])
                for j in range(ff // 256)]
    after = len(early) + ff // 256
    k_load, v_load, p_load = (pltpu.make_async_copy(s, t, ls.at[after + i]) for i, (s, t) in enumerate(
        ((k_h, k), (v_h, v), (p_h, prs))))
    loads[4:4] = wu_loads
    for cp in loads:
        cp.start()
    bar = pltpu.get_barrier_semaphore()
    for dev in [core_peer, y_peer, x_peer] + z_peers:
        pl.semaphore_signal(bar, inc=1, device_id=dev, device_id_type=MESH)

    def cut(j):
        return (pl.ds(pl.multiple_of(x * h + (j // 2) * hr, 16), hr), pl.ds(pl.multiple_of((j % 2) * hc, 128), hc))

    near = pl.ds(pl.multiple_of(x * h, 16), h)
    away = pl.ds(pl.multiple_of((1 - x) * h, 16), h)

    def c1(p):
        return copy_to(g.at[p, 1 - c], r1.at[p], s1.at[p], q1.at[p], core_peer)

    def c2(p):
        return copy_to(g.at[p, c, 1 - y], r2.at[p], s2.at[p], q2.at[p], y_peer)

    def c3(p):
        return copy_to(g.at[p, c, y, away], r3.at[p], s3.at[p], q3.at[p], x_peer)

    def c4(p, e):
        rr, cc = cut(zs[e])
        return copy_to(g.at[p, c, y, rr, cc], r4.at[p, e], s4.at[p, e], q4.at[p, e], z_peers[e])

    def c5(p, e, j):
        rr, cc = cut(j)
        return copy_to(r1.at[p, 0, rr, cc], r1.at[p, 0, rr, cc], s5.at[p, e], q5.at[p, e], z_peers[e])

    def c6(p, rr):
        return copy_to(r1.at[p, 0, rr], r1.at[p, 0, rr], s6.at[p], q6.at[p], x_peer)

    def store(p, dst):
        return pltpu.make_async_copy(r1.at[p, 0], dst, os_.at[p])

    def st1(p):
        c1(p).wait_recv()
        g[p, c] = (g[p, c].astype(F32) + r1[p].astype(F32)).astype(BF)
        c2(p).start()

    def st2(p):
        c2(p).wait_recv()
        g[p, c, y] = (g[p, c, y].astype(F32) + r2[p].astype(F32)).astype(BF)
        c3(p).start()

    def st3(p):
        c3(p).wait_recv()
        g[p, c, y, near] = (g[p, c, y, near].astype(F32) + r3[p].astype(F32)).astype(BF)
        for e in (1, 2, 0):
            c4(p, e).start()

    def st4(p):
        for e in range(3):
            c4(p, e).wait_recv()
        rr, cc = cut(z)
        t = g[p, c, y, rr, cc].astype(F32) + r4[p, 0].astype(F32) + r4[p, 1].astype(F32) + r4[p, 2].astype(F32)
        r1[p, 0, rr, cc] = t.astype(BF)
        for e in (1, 2, 0):
            c5(p, e, z).start()

    def st5(p):
        for e in range(3):
            c5(p, e, zs[e]).wait_recv()
        c6(p, near).start()

    def st6(p):
        c6(p, away).wait_recv()

        @pl.when(p < nd)
        def down():
            store(p, od_hbm.at[pl.ds(p * R, R)]).start()

        @pl.when(jnp.logical_and(p >= nd, p < nd + nu))
        def up():
            store(p, ou_hbm.at[:, pl.ds(pl.multiple_of((p - nd) * C, C), C)]).start()

        @pl.when(p == nd + nu)
        def out():
            store(p, oo_hbm).start()

        @pl.when(p > nd + nu)
        def qkv():
            store(p, oq_hbm.at[:, pl.ds(pl.multiple_of((p - nd - nu - 1) * C, C), C)]).start()

    stages = [None, st1, st2, st3, st4, st5, st6]

    loads[0].wait()
    loads[1].wait()

    block = 256
    for a in range(d // block):
        def down_block(i, carry):
            t = dg(a_view[i, :, a * block:(a + 1) * block], dffn[...], 0, 0).astype(BF)
            for j in range(nd):
                lo, hi = max(j * R, a * block), min((j + 1) * R, (a + 1) * block)
                if lo < hi:
                    g[j, i % 2, i // 2, lo - j * R:hi - j * R] = t[lo - a * block:hi - a * block]
            return carry

        lax.fori_loop(0, nd, down_block, 0)
        if a == 0:
            pl.semaphore_wait(bar, 6)
        for p in range(a * block // R, nd if a == d // block - 1 else (a + 1) * block // R):
            c1(p).start()
    st1(0)
    st1(1)
    loads[2].wait()
    loads[3].wait()

    def up_back(j, carry):
        at = (j // 3, slice(None), pl.ds(pl.multiple_of(j % 3 * 256, 256), 256))
        low = (dg(dffn[...], wd[pl.ds(pl.multiple_of(j * 256, 256), 256)], 1, 1) * slope[at].astype(F32)).astype(BF)
        b_view[at] = low
        part_up[:, pl.ds(pl.multiple_of(j * 256, 256), 256)] = fold(low.astype(F32))
        return carry

    lax.fori_loop(0, ff // 256, up_back, 0, unroll=UNROLL_BACK)
    k_load.start()
    v_load.start()
    for cp in loads[4:]:
        cp.wait()

    def row_block(p, t):
        for j in range(4):
            g[p, j % 2, j // 2] = t[j * R:(j + 1) * R].astype(BF)

    def up_block(i, carry):
        row_block(nd + i, dg(first[...], b_view[i], 0, 0))
        c1(nd + i).start()
        return carry

    lax.fori_loop(0, nu, up_block, 0)

    def rows_back():
        for b in range(d // 256):
            cols = pl.ds(b * 256, 256)
            dsum[:, cols] = dsec[:, cols] + sum(
                dg(b_view[j // 3, :, j % 3 * 256:(j % 3 + 1) * 256], wu[j, cols, :], 1, 1) for j in range(ff // 256))
        p_load.start()
        part[...] = jnp.zeros_like(part)
        chunk = 64
        gain = g1_v[...].reshape(1, d)

        def norm1_back(i, carry):
            r = pl.ds(pl.multiple_of(i * chunk, chunk), chunk)
            d_first, normed = dsum[r], normed1[r]
            part[1] += fold(d_first * normed)
            part[2] += fold(d_first)
            d_sum = scale1[r, :1] * norm_grad(d_first * gain, normed)
            dsum[r] = d_sum
            low = d_sum.astype(BF)
            datt[r] = low
            part[0] += fold(low.astype(F32))
            return carry

        lax.fori_loop(0, rows // chunk, norm1_back, 0)
        row_block(nd + nu, dg(ctx[...], datt[...], 0, 0))
        c1(nd + nu).start()
        dctx[...] = dg(datt[...], wo[...], 1, 1).astype(BF).reshape(seqs, quarter, d)
        k_load.wait()
        v_load.wait()
        p_load.wait()

    def unit(u, carry):
        s, p = u // pairs, u % pairs
        cols = pl.ds(pl.multiple_of(p * PAIR, PAIR), PAIR)
        qs = stack_heads(q[s, :, cols])
        ds = stack_heads(dctx[s, :, cols])
        low = prs[s, p]
        probs = low.astype(F32)
        t = probs * dg(v[s, :, cols], ds, 1, 1)
        d_raw = (t - probs * jnp.sum(t, axis=0, keepdims=True)).astype(BF)
        dv[s, :, cols] = dg(low, ds, 1, 0).astype(BF)
        dk[s, :, cols] = dg(d_raw, qs, 1, 0).astype(BF)
        dq[s, :, cols] = (unstack_heads(dg(k[s, :, cols], d_raw, 0, 0)) * 0.125).astype(BF)
        return carry

    def qkv_piece(i):
        cols = pl.ds(i * 2 * PAIR, 2 * PAIR)
        allt = toks[...].reshape(seqs * keys, d)
        ga = dg(toks[:, pl.ds(pl.multiple_of(n * quarter, quarter), quarter)].reshape(rows, d), dq[:, :, cols].reshape(rows, 2 * PAIR), 0, 0)
        gb = dg(allt, a_buf[:, cols], 0, 0)
        gc = dg(allt, b_buf[:, cols], 0, 0)
        left = left_lanes(R)
        p = nd + nu + 1 + i
        for e in range(4):
            rr = slice(e * R, (e + 1) * R)
            for j in range(2):
                sl = slice(j * PAIR, (j + 1) * PAIR)
                aj, bj, cj = ga[rr, sl], pltpu.roll(gb[rr, sl], HD, 1), gc[rr, sl]
                for t, val in enumerate((jnp.where(left, aj, bj), jnp.where(left, cj, aj), jnp.where(left, bj, cj))):
                    g[p, e % 2, e // 2, :, pl.ds((3 * j + t) * PAIR, PAIR)] = val.astype(BF)
        c1(p).start()

    cx1 = copy_to(dtok.at[:, 1 - c], x1, xs.at[0], xs.at[1], core_peer)
    cx2 = copy_to(dtok.at[1 - y, c], x2, xs.at[2], xs.at[3], y_peer)

    def input_part():
        def one(s, carry):
            t = dg(dk[s], wp[1], 1, 1) + dg(dv[s], wp[2], 1, 1)
            for e in range(4):
                dtok[e // 2, e % 2, s] = t[e * quarter:(e + 1) * quarter].astype(BF)
            return carry

        lax.fori_loop(0, seqs, one, 0)
        cx1.start()
        dsum[...] += dg(dq[...].reshape(rows, d), wp[0], 1, 1)

    def small(i, slot, dev):
        return copy_to(sbuf.at[i], srecv.at[slot], ss.at[slot], sq.at[slot], dev)

    def sums0():
        sbuf[0, 0:1] = jnp.sum(fold(dq[...].reshape(rows, d).astype(F32)), axis=0, keepdims=True)

        def add(s, acc):
            return acc + fold(dv[s].astype(F32))

        acc = lax.fori_loop(0, seqs, add, jnp.zeros((8, d), F32))
        sbuf[0, 1:2] = jnp.sum(acc, axis=0, keepdims=True)
        for i in range(3):
            sbuf[0, 2 + i:3 + i] = total(part[i])
        for i in range(nu):
            sbuf[0, 5 + i:6 + i] = total(part_up[:, i * d:(i + 1) * d])
        sbuf[0, 5 + nu:] = sums_ref[...]
        small(0, 0, core_peer).start()

    def sums1():
        small(0, 0, core_peer).wait_recv()
        sbuf[1] = sbuf[0] + srecv[0]
        small(1, 1, y_peer).start()

    def sums2():
        small(1, 1, y_peer).wait_recv()
        sbuf[2] = sbuf[1] + srecv[1]
        small(2, 2, x_peer).start()

    def sums3():
        small(2, 2, x_peer).wait_recv()
        sbuf[3] = sbuf[2] + srecv[2]
        for e in range(3):
            small(3, 3 + e, z_peers[e]).start()

    def add_x1():
        cx1.wait_recv()

        def add(i, carry):
            a, b = i // seqs, i % seqs
            dtok[a, c, b] = (dtok[a, c, b].astype(F32) + x1[a, b].astype(F32)).astype(BF)
            return carry

        lax.fori_loop(0, 2 * seqs, add, 0)

    units = seqs * pairs
    slots_of_units = -(-units // UNITS)
    extra = {3: [rows_back], 9: [lambda: qkv_piece(0), sums0], 10: [lambda: qkv_piece(1), sums1],
             11: [lambda: qkv_piece(2), sums2], 12: [sums3], 13: [input_part], 14: [add_x1, cx2.start]}

    def slot(t, carry):
        for i in ORDER:
            p = t - LAGS[i]

            @pl.when(jnp.logical_and(p >= 0, p < pieces))
            def run():
                stages[i](p)

        @pl.when(jnp.logical_and(t > 3, t <= 3 + slots_of_units))
        def attention():
            lo = (t - 4) * UNITS
            lax.fori_loop(lo, jnp.minimum(lo + UNITS, units), unit, 0)

        for at, todo in extra.items():
            @pl.when(t == at)
            def more():
                for f in todo:
                    f()
        return carry

    lax.fori_loop(3, pieces + LAGS[6], slot, 0)
    cx2.wait_recv()

    def out_x(i, carry):
        r = pl.ds(pl.multiple_of(i * quarter, quarter), quarter)
        x1[0, i] = (dsum[r] + dtok[y, c, i].astype(F32) + x2[i].astype(F32)).astype(BF)
        return carry

    lax.fori_loop(0, seqs, out_x, 0)
    din_out = pltpu.make_async_copy(x1.at[0], din_hbm, xs.at[4])
    din_out.start()
    for e in range(3):
        small(3, 3 + e, z_peers[e]).wait_recv()
    so_ref[...] = sbuf[3] + srecv[3] + srecv[4] + srecv[5]
    small(0, 0, core_peer).wait_send()
    small(1, 1, y_peer).wait_send()
    small(2, 2, x_peer).wait_send()
    for e in range(3):
        small(3, 3 + e, z_peers[e]).wait_send()
    cx1.wait_send()
    cx2.wait_send()

    def drain(p, carry):
        c1(p).wait_send()
        c2(p).wait_send()
        c3(p).wait_send()
        c6(p, near).wait_send()
        store(p, oo_hbm).wait()
        for e in range(3):
            c4(p, e).wait_send()
            c5(p, e, z).wait_send()
        return carry

    lax.fori_loop(0, pieces, drain, 0)
    din_out.wait()


def tail_part(act, dffn, wd, slope, first, wu, dsec, normed, scale, wo, ctx, q, toks, wp, k, v, probs, g1, sums):
    seqs, quarter, d = q.shape
    rows, keys = seqs * quarter, 4 * quarter
    R = d // 4
    nd = nu = act.shape[0]
    ff = nd * d
    n = nd + nu + 4
    h = R // 2
    all_rows = (6 + nu + sums.shape[0] - 1, d)
    vm, hbm = pl.BlockSpec(memory_space=V), pl.BlockSpec(memory_space=ANY)
    S = jax.ShapeDtypeStruct
    own, every, flat = (seqs, quarter, d), (seqs, keys, d), (rows, d)
    return pl.pallas_call(
        tail_kernel,
        out_shape=(S((nd * R, d), BF), S((R, nu * d), BF), S((R, d), BF), S((R, 3 * d), BF), S(own, BF),
                   S(all_rows, F32)),
        in_specs=[hbm] * 19,
        out_specs=(hbm, hbm, hbm, hbm, hbm, vm),
        scratch_shapes=[V((seqs * keys, d), BF), V((seqs * keys, d), BF), V(flat, BF), V(flat, BF), V(flat, BF),
                        V(flat, BF), V(flat, F32), V(every, BF), V(own, BF),
                        V((2 * seqs * keys, d), BF), V((seqs * (d // PAIR) * keys, 2 * quarter), BF), V((3, d, d), BF),
                        V(own, BF), V((2, 2) + own, BF), V(wo.shape, BF), V(flat, F32), V(flat, F32),
                        V((rows, 128), F32), V((3, 8, d), F32), V((8, ff), F32), V((d,), F32), V(sums.shape, F32),
                        V((n, 2, 2, R, d), BF), V((n, 2, R, d), BF), V((n, R, d), BF), V((n, h, d), BF),
                        V((n, 3, h // 2, d // 2), BF), V((4,) + all_rows, F32), V((6,) + all_rows, F32),
                        V((2,) + own, BF), V(own, BF)]
        + [DMA((n,))] * 6 + [DMA((n, 3))] * 4 + [DMA((n,))] * 3
        + [DMA((6,))] * 2 + [DMA((5,)), DMA((18 + ff // 256,))],
        name="tail_part",
        compiler_params=pltpu.CompilerParams(collective_id=2, has_side_effects=True, vmem_limit_bytes=63 << 20),
    )(act, dffn, wd, slope, first, wu, dsec, normed, scale, wo, ctx, q, toks, wp, k, v, probs,
      g1, sums)


def finish_kernel(d_h, u_h, o_h, q_h, sums_ref, fd, fu, fo, fq, qvb, outb, n1g, n1s, upb, downb, n2g, n2s,
                  low, full, ls, os_):
    R, C = low.shape[1:]
    nd, nu = d_h.shape[0] // R, u_h.shape[1] // C
    cut = lambda ref, i: ref.at[:, pl.ds(i * C, C)]
    ends = ([(d_h.at[pl.ds(i * R, R)], fd.at[pl.ds(i * R, R)]) for i in range(nd)]
            + [(cut(u_h, i), cut(fu, i)) for i in range(nu)] + [(o_h, fo)]
            + [(cut(q_h, i), cut(fq, i)) for i in range(3)])
    loads = [pltpu.make_async_copy(s, low.at[i], ls.at[i]) for i, (s, _) in enumerate(ends)]
    stores = [pltpu.make_async_copy(full.at[i], t, os_.at[i]) for i, (_, t) in enumerate(ends)]
    for cp in loads:
        cp.start()
    n = lax.axis_index("narrow")
    for i in range(4):
        @pl.when(n == i)
        def pick():
            at = slice(i * R, (i + 1) * R)
            qvb[...] = sums_ref[0:2, at]
            for j, ref in ((2, outb), (3, n1g), (4, n1s), (5 + nu, downb), (6 + nu, n2g), (7 + nu, n2s)):
                ref[...] = sums_ref[j, at]
            upb[...] = sums_ref[5 + i]
    for i, (a, b) in enumerate(zip(loads, stores)):
        a.wait()
        full[i] = low[i].astype(F32)
        b.start()
    for cp in stores:
        cp.wait()


def finish_part(down, up, out, qkv, sums):
    R, d = out.shape
    n = down.shape[0] // R + up.shape[1] // d + 4
    vm, hbm = pl.BlockSpec(memory_space=V), pl.BlockSpec(memory_space=ANY)
    S = jax.ShapeDtypeStruct
    shapes = [S(a.shape, F32) for a in (down, up, out, qkv)] + [S((2, R), F32)] + [S((R,), F32)] * 3
    shapes += [S((d,), F32)] + [S((R,), F32)] * 3
    return pl.pallas_call(
        finish_kernel,
        out_shape=shapes,
        in_specs=[hbm] * 4 + [vm],
        out_specs=[hbm] * 4 + [vm] * 8,
        scratch_shapes=[V((n, R, d), BF), V((n, R, d), F32), DMA((n,)), DMA((n,))],
        name="finish_part",
        compiler_params=pltpu.CompilerParams(vmem_limit_bytes=60 << 20),
    )(down, up, out, qkv, sums)


def local(tokens, lengths, qkv_weight, qv_bias, out_weight, out_bias, norm1_gain, norm1_shift, up_weight, up_bias,
          down_weight, down_bias, norm2_gain, norm2_shift, cotangent):
    seqs, quarter, d = tokens.shape
    own, every = (seqs, quarter, d), (seqs, 4 * quarter, d)
    (toks, q, k, v, probs, wp, ctx, first, act, slope, output, dffn, dsec, normed, scale, sums) = front_part(
        tokens, lengths, qkv_weight, qv_bias, out_weight, out_bias, norm1_gain, norm1_shift, up_weight, up_bias,
        down_weight, down_bias, norm2_gain, norm2_shift, cotangent)
    down, up, out, qkv, input_grad, sums = tail_part(
        act, dffn, down_weight, slope, first, up_weight, dsec, normed, scale, out_weight, ctx, q, toks.reshape(every),
        wp, k.reshape(every), v.reshape(every), probs, norm1_gain, sums)
    wide = lax.axis_size("wide")
    if wide > 8:
        groups = [[j * 8 + i for j in range(wide // 8)] for i in range(8)]
        down, up, out, qkv = (
            lax.psum(a.astype(F32), "wide", axis_index_groups=groups).astype(BF) for a in (down, up, out, qkv))
        sums = lax.psum(sums, "wide", axis_index_groups=groups)
    down, up, out, qkv, qvb, outb, n1g, n1s, upb, downb, n2g, n2s = finish_part(down, up, out, qkv, sums)
    return (output.reshape(own), input_grad, qkv, qvb, out, outb, n1g, n1s, up, upb, down,
            downb, n2g, n2s)


def solution(mesh):
    return jax.shard_map(
        local,
        mesh=mesh,
        in_specs=(
            P("wide", "narrow", None),
            P("wide"),
            P(),
            P(),
            P(),
            P(),
            P(),
            P(),
            P(),
            P(),
            P(),
            P(),
            P(),
            P(),
            P("wide", "narrow", None),
        ),
        out_specs=(
            P("wide", "narrow", None),
            P("wide", "narrow", None),
            P("narrow", None),
            P(None, "narrow"),
            P("narrow", None),
            P("narrow"),
            P("narrow"),
            P("narrow"),
            P("narrow", None),
            P("narrow"),
            P("narrow", None),
            P("narrow"),
            P("narrow"),
            P("narrow"),
        ),
        check_vma=False,
    )
```

```python
import functools

import jax
import jax.numpy as jnp
from jax import lax
from jax.experimental import pallas as pl
from jax.experimental.pallas import tpu as pltpu
from jax.sharding import PartitionSpec as P

H = 12
HD = 64
PAIR = 2 * HD
epsilon = 1e-12
root_half = 0.7071067811865476
inv_root_two_pi = 0.3989422804014327
MESH = pl.DeviceIdType.MESH
F32 = jnp.float32
BF = jnp.bfloat16
V = pltpu.VMEM
DMA = pltpu.SemaphoreType.DMA
ANY = pl.ANY
UNROLL_ATT = 6
UNROLL_UP = 3


def dg(a, b, ca, cb):
    return lax.dot_general(a, b, (((ca,), (cb,)), ((), ())), preferred_element_type=F32)


def copy_to(src, dst, ss, rs, dev):
    return pltpu.make_async_remote_copy(
        src_ref=src, dst_ref=dst, send_sem=ss, recv_sem=rs, device_id=dev, device_id_type=MESH)


def left_lanes(rows):
    return lax.broadcasted_iota(jnp.int32, (rows, PAIR), 1) < HD


def stack_heads(x):
    left = left_lanes(x.shape[0])
    zero = jnp.zeros_like(x)
    return jnp.concatenate([jnp.where(left, x, zero), jnp.where(left, zero, x)], axis=0)


def unstack_heads(x_t):
    q = x_t.shape[1] // 2
    top = lax.broadcasted_iota(jnp.int32, (PAIR, q), 0) < HD
    return jnp.where(top, x_t[:, :q], x_t[:, q:]).T


def fold(x):
    return jnp.sum(x.reshape(x.shape[0] // 8, 8, x.shape[1]), axis=0)


def total(x):
    return jnp.sum(x, axis=0, keepdims=True)


def center_scale(v):
    center = v - jnp.mean(v, axis=-1, keepdims=True)
    scale = lax.rsqrt(jnp.mean(center * center, axis=-1, keepdims=True) + epsilon)
    return center * scale, scale


def norm_grad(g, normed):
    return g - jnp.mean(g, axis=-1, keepdims=True) - normed * jnp.mean(g * normed, axis=-1, keepdims=True)


LAGS = (0, 1, 3, 4, 5, 7, 11)
UNITS = 4
ORDER = (3, 1, 6, 4, 2, 5)
UNROLL_BACK = 1


def layer_kernel(len_ref, tok_h, cot_h, w_h, wo_h, wu_h, wd_h, qvb_h, bo_h, g1_h, s1_h, bu_h, bd_h, g2_h, s2_h,
                 out_h, od_hbm, ou_hbm, oo_hbm, oq_hbm, din_hbm, so_ref,
                 a_buf, b_buf, dtok, toks, k, v, q, pr, wp, ctx, low1, dffn, datt, dq, wo, dsum, first, normed1,
                 scale1, part, part2, part_up, qvb_ref, bo_v, g1_v, s1_v, bu_v, bd_v, g2_v, s2_v,
                 g, r1, r2, r3, r4, sbuf, srecv, x1, x2,
                 ls, cs, cr, ys, yr, fs, fr,
                 s1, q1, s2, q2, s3, q3, s4, q4, s5, q5, s6, q6, os_, ss, sq, xs):
    pieces, _, _, R, C = g.shape
    seqs, quarter, d = q.shape
    rows, keys, pairs = seqs * quarter, 4 * quarter, d // PAIR
    ff = wu_h.shape[1]
    nd = nu = ff // d
    h = R // 2
    hr, hc = h // 2, C // 2
    w, n = lax.axis_index("wide"), lax.axis_index("narrow")
    c, y, x, z = n % 2, n // 2, w % 2, (w // 2) % 4
    core_n, y_n = n + 1 - 2 * c, n + 2 - 4 * y
    far_n = core_n + 2 - 4 * y
    core_peer, y_peer, x_peer = (w, core_n), (w, y_n), (w + 1 - 2 * x, n)
    zs = [z + 1 - 2 * (z % 2), z + 2 - 4 * (z // 2), 3 - z]
    z_peers = [(w + 2 * (j - z), n) for j in zs]
    gp = g.reshape(pieces, d, d)
    a_view, b_view = a_buf.reshape(nd, rows, d), b_buf.reshape(nu, rows, d)
    dk, dv = a_buf.reshape(seqs, keys, d), b_buf.reshape(seqs, keys, d)
    slope = dtok.reshape(nd, rows, d)
    tok = datt.reshape(seqs, quarter, d)
    dctx = low1.reshape(seqs, quarter, d)
    out = dq.reshape(rows, d)
    cot = dffn.reshape(seqs, quarter, d)
    toks3, k3, v3 = (r.reshape(seqs, keys, d) for r in (toks, k, v))
    blocks = lambda ref, i: ref.at[:, i * d:(i + 1) * d]
    moves = [(tok_h, tok)] + [(blocks(w_h, i), gp.at[i]) for i in range(3)] + [
        (qvb_h, qvb_ref), (bo_h, bo_v), (g1_h, g1_v), (s1_h, s1_v), (bu_h, bu_v), (bd_h, bd_v), (g2_h, g2_v),
        (s2_h, s2_v), (wo_h, wo)] + [(blocks(wu_h, i), gp.at[nd + i]) for i in range(nu)] + [(cot_h, cot)] + [
        (wd_h.at[pl.ds(i * d, d)], gp.at[nd + nu + i]) for i in range(nd)]
    loads = [pltpu.make_async_copy(s, t, ls.at[i]) for i, (s, t) in enumerate(moves)]
    for cp in loads[:4]:
        cp.start()
    bar = pltpu.get_barrier_semaphore()
    for dev in [core_peer, y_peer, x_peer] + z_peers:
        pl.semaphore_signal(bar, inc=1, device_id=dev, device_id_type=MESH)
    pl.semaphore_wait(bar, 6)

    def send_y(s):
        return copy_to(tok_h.at[s], toks.at[s, n], ys.at[s], yr.at[s], y_peer)

    def send_core(s):
        return copy_to(tok_h.at[s], toks.at[s, n], cs.at[s], cr.at[s], core_peer)

    def forward_y(s):
        return copy_to(toks.at[s, y_n], toks.at[s, y_n], fs.at[s], fr.at[s], core_peer)

    for s in range(seqs):
        send_y(s).start()
        send_core(s).start()
    for cp in loads[4:]:
        cp.start()
    loads[0].wait()
    for s in range(seqs):
        toks[s, n] = tok[s]
    for cp in loads[1:4]:
        cp.wait()
    left = left_lanes(d)
    for p in range(pairs):
        t0, t1, t2 = (gp[p // 2, :, pl.ds((p % 2 * 3 + i) * PAIR, PAIR)].astype(F32) for i in range(3))
        cols = pl.ds(p * PAIR, PAIR)
        wp[0, :, cols] = jnp.where(left, t0, t1).astype(BF)
        wp[1, :, cols] = pltpu.roll(jnp.where(left, t2, t0), HD, 1).astype(BF)
        wp[2, :, cols] = jnp.where(left, t1, t2).astype(BF)
    for cp in loads[4:12]:
        cp.wait()
    bo_ref, g1_ref, s1_ref, bd_ref, g2_ref, s2_ref = (
        r[...].reshape(1, d) for r in (bo_v, g1_v, s1_v, bd_v, g2_v, s2_v))
    own = tok[...].reshape(rows, d)
    q[...] = ((dg(own, wp[0], 1, 0) + qvb_ref[0:1, :]).astype(BF) * 0.125).reshape(seqs, quarter, d)

    def project(s, half):
        blocks = pl.ds(2 * half, 2)
        x = toks[s, blocks].reshape(2 * quarter, d)
        k[s, blocks] = dg(x, wp[1], 1, 0).astype(BF).reshape(2, quarter, d)
        v[s, blocks] = (dg(x, wp[2], 1, 0) + qvb_ref[1:2, :]).astype(BF).reshape(2, quarter, d)

    for s in range(seqs):
        send_core(s).wait_recv()
    for s in range(seqs):
        project(s, y)

    def fetch_far(s):
        copy_to(toks.at[s, y_n], toks.at[s, y_n], ys.at[s], yr.at[s], y_peer).wait_recv()
        forward_y(s).start()

    fetch_far(0)
    for s in range(seqs):
        copy_to(toks.at[s, far_n], toks.at[s, far_n], fs.at[s], fr.at[s], core_peer).wait_recv()
        project(s, 1 - y)
        if s + 1 < seqs:
            fetch_far(s + 1)
        live = lax.broadcasted_iota(jnp.int32, (keys, 2 * quarter), 0) < len_ref[s]

        def unit(p, carry):
            cols = pl.ds(pl.multiple_of(p * PAIR, PAIR), PAIR)
            qs = stack_heads(q[s, :, cols])
            kp = k[s, :, :, cols].reshape(keys, PAIR)
            vp = v[s, :, :, cols].reshape(keys, PAIR)
            scores = jnp.where(live, dg(kp, qs, 1, 1), -1000000000.0)
            e = jnp.exp(scores - jnp.max(scores, axis=0, keepdims=True))
            probs = (e * (1.0 / jnp.sum(e, axis=0, keepdims=True))).astype(BF)
            pr[s, p] = probs
            ctx[s * quarter:(s + 1) * quarter, cols] = unstack_heads(dg(vp, probs, 0, 0)).astype(BF)
            return carry

        lax.fori_loop(0, pairs, unit, 0, unroll=UNROLL_ATT)

    part2[...] = jnp.zeros_like(part2)
    chunk = 64
    chunks = rows // chunk
    loads[12].wait()
    for b in range(d // 256):
        cols = pl.ds(b * 256, 256)
        dsum[:, cols] = (dg(ctx[...], wo[:, cols], 1, 0) + bo_ref[:, b * 256:(b + 1) * 256]
                        + tok[:, :, cols].reshape(rows, 256).astype(F32))

    def norm1(i, carry):
        r = pl.ds(pl.multiple_of(i * chunk, chunk), chunk)
        normed, scale = center_scale(dsum[r])
        x = normed * g1_ref + s1_ref
        normed1[r] = normed
        scale1[r] = jnp.broadcast_to(scale, (chunk, 128))
        first[r] = x
        low1[r] = x.astype(BF)
        return carry

    lax.fori_loop(0, chunks, norm1, 0)
    for cp in loads[13:13 + nu]:
        cp.wait()

    def up(j, carry):
        cols = pl.ds(pl.multiple_of(j * 256, 256), 256)
        at = (j // 3, slice(None), pl.ds(pl.multiple_of(j % 3 * 256, 256), 256))
        pre = dg(low1[...], gp[(nd + at[0],) + at[1:]], 1, 0) + bu_v[cols].reshape(1, 256)
        half = 0.5 + 0.5 * lax.erf(pre * root_half)
        a_view[at] = (pre * half).astype(BF)
        slope[at] = (half + pre * (jnp.exp(-0.5 * pre * pre) * inv_root_two_pi)).astype(BF)
        return carry

    lax.fori_loop(0, ff // 256, up, 0, unroll=UNROLL_UP)
    for cp in loads[13 + nu:]:
        cp.wait()
    for b in range(d // 256):
        cols = pl.ds(b * 256, 256)
        dsum[:, cols] = bd_ref[:, b * 256:(b + 1) * 256] + first[:, cols] + sum(
            dg(a_view[i], gp[nd + nu + i, :, cols], 1, 0) for i in range(ff // d))

    def norm2(i, carry):
        r = pl.ds(pl.multiple_of(i * chunk, chunk), chunk)
        normed, scale = center_scale(dsum[r])
        out[r] = (normed * g2_ref + s2_ref).astype(BF)
        s = i * chunk // quarter
        off = pl.multiple_of(i * chunk - s * quarter, chunk)
        pos = n * quarter + off + lax.broadcasted_iota(jnp.int32, (chunk, d), 0)
        d_out = jnp.where(pos < len_ref[s], cot[s, pl.ds(off, chunk)].astype(F32), 0.0)
        part2[1] += fold(d_out * normed)
        part2[2] += fold(d_out)
        d_second = scale * norm_grad(d_out * g2_ref, normed)
        dsum[r] = d_second
        low = d_second.astype(BF)
        dffn[r] = low
        part2[0] += fold(low.astype(F32))
        return carry

    lax.fori_loop(0, chunks, norm2, 0)
    out_store = pltpu.make_async_copy(out, out_h, xs.at[5])
    out_store.start()

    def cut(j):
        return (pl.ds(pl.multiple_of(x * h + (j // 2) * hr, 16), hr), pl.ds(pl.multiple_of((j % 2) * hc, 128), hc))

    near = pl.ds(pl.multiple_of(x * h, 16), h)
    away = pl.ds(pl.multiple_of((1 - x) * h, 16), h)

    def c1(p):
        return copy_to(g.at[p, 1 - c], r1.at[p], s1.at[p], q1.at[p], core_peer)

    def c2(p):
        return copy_to(g.at[p, c, 1 - y], r2.at[p], s2.at[p], q2.at[p], y_peer)

    def c3(p):
        return copy_to(g.at[p, c, y, away], r3.at[p], s3.at[p], q3.at[p], x_peer)

    def c4(p, e):
        rr, cc = cut(zs[e])
        return copy_to(g.at[p, c, y, rr, cc], r4.at[p, e], s4.at[p, e], q4.at[p, e], z_peers[e])

    def c5(p, e, j):
        rr, cc = cut(j)
        return copy_to(r1.at[p, 0, rr, cc], r1.at[p, 0, rr, cc], s5.at[p, e], q5.at[p, e], z_peers[e])

    def c6(p, rr):
        return copy_to(r1.at[p, 0, rr], r1.at[p, 0, rr], s6.at[p], q6.at[p], x_peer)

    def store(p, dst):
        return pltpu.make_async_copy(r1.at[p, 0], dst, os_.at[p])

    def st1(p):
        c1(p).wait_recv()
        g[p, c] = (g[p, c].astype(F32) + r1[p].astype(F32)).astype(BF)
        c2(p).start()

    def st2(p):
        c2(p).wait_recv()
        g[p, c, y] = (g[p, c, y].astype(F32) + r2[p].astype(F32)).astype(BF)
        c3(p).start()

    def st3(p):
        c3(p).wait_recv()
        g[p, c, y, near] = (g[p, c, y, near].astype(F32) + r3[p].astype(F32)).astype(BF)
        for e in (1, 2, 0):
            c4(p, e).start()

    def st4(p):
        for e in range(3):
            c4(p, e).wait_recv()
        rr, cc = cut(z)
        t = g[p, c, y, rr, cc].astype(F32) + r4[p, 0].astype(F32) + r4[p, 1].astype(F32) + r4[p, 2].astype(F32)
        r1[p, 0, rr, cc] = t.astype(BF)
        for e in (1, 2, 0):
            c5(p, e, z).start()

    def st5(p):
        for e in range(3):
            c5(p, e, zs[e]).wait_recv()
        c6(p, near).start()

    def st6(p):
        c6(p, away).wait_recv()

        @pl.when(p < nd)
        def down():
            store(p, od_hbm.at[pl.ds(p * R, R)]).start()

        @pl.when(jnp.logical_and(p >= nd, p < nd + nu))
        def up():
            store(p, ou_hbm.at[:, pl.ds(pl.multiple_of((p - nd) * C, C), C)]).start()

        @pl.when(p == nd + nu)
        def out():
            store(p, oo_hbm).start()

        @pl.when(p > nd + nu)
        def qkv():
            store(p, oq_hbm.at[:, pl.ds(pl.multiple_of((p - nd - nu - 1) * C, C), C)]).start()

    stages = [None, st1, st2, st3, st4, st5, st6]

    block = 256
    for a in range(d // block):
        def down_block(i, carry):
            t = dg(a_view[i, :, a * block:(a + 1) * block], dffn[...], 0, 0).astype(BF)
            for j in range(nd):
                lo, hi = max(j * R, a * block), min((j + 1) * R, (a + 1) * block)
                if lo < hi:
                    g[j, i % 2, i // 2, lo - j * R:hi - j * R] = t[lo - a * block:hi - a * block]
            return carry

        lax.fori_loop(0, nd, down_block, 0)
        for p in range(a * block // R, nd if a == d // block - 1 else (a + 1) * block // R):
            c1(p).start()
    st1(0)
    st1(1)

    def up_back(j, carry):
        at = (j // 3, slice(None), pl.ds(pl.multiple_of(j % 3 * 256, 256), 256))
        low = (dg(dffn[...], gp[nd + nu + j // 3, pl.ds(pl.multiple_of(j % 3 * 256, 256), 256)], 1, 1) * slope[at].astype(F32)).astype(BF)
        b_view[at] = low
        part_up[:, pl.ds(pl.multiple_of(j * 256, 256), 256)] = fold(low.astype(F32))
        return carry

    lax.fori_loop(0, ff // 256, up_back, 0, unroll=UNROLL_BACK)
    for b in range(d // 256):
        cols = pl.ds(b * 256, 256)
        dsum[:, cols] += sum(dg(b_view[i], gp[nd + i, cols, :], 1, 1) for i in range(nu))

    def row_block(p, t):
        for j in range(4):
            g[p, j % 2, j // 2] = t[j * R:(j + 1) * R].astype(BF)

    def up_block(i, carry):
        row_block(nd + i, dg(low1[...], b_view[i], 0, 0))
        c1(nd + i).start()
        return carry

    lax.fori_loop(0, nu, up_block, 0)

    def rows_back():
        part[...] = jnp.zeros_like(part)
        chunk = 64
        gain = g1_v[...].reshape(1, d)

        def norm1_back(i, carry):
            r = pl.ds(pl.multiple_of(i * chunk, chunk), chunk)
            d_first, normed = dsum[r], normed1[r]
            part[1] += fold(d_first * normed)
            part[2] += fold(d_first)
            d_sum = scale1[r, :1] * norm_grad(d_first * gain, normed)
            dsum[r] = d_sum
            low = d_sum.astype(BF)
            datt[r] = low
            part[0] += fold(low.astype(F32))
            return carry

        lax.fori_loop(0, rows // chunk, norm1_back, 0)
        row_block(nd + nu, dg(ctx[...], datt[...], 0, 0))
        c1(nd + nu).start()
        dctx[...] = dg(datt[...], wo[...], 1, 1).astype(BF).reshape(seqs, quarter, d)
        out_store.wait()

    def unit(u, carry):
        s, p = u // pairs, u % pairs
        cols = pl.ds(pl.multiple_of(p * PAIR, PAIR), PAIR)
        qs = stack_heads(q[s, :, cols])
        ds = stack_heads(dctx[s, :, cols])
        low = pr[s, p]
        probs = low.astype(F32)
        t = probs * dg(v3[s, :, cols], ds, 1, 1)
        d_raw = (t - probs * jnp.sum(t, axis=0, keepdims=True)).astype(BF)
        dv[s, :, cols] = dg(low, ds, 1, 0).astype(BF)
        dk[s, :, cols] = dg(d_raw, qs, 1, 0).astype(BF)
        dq[s, :, cols] = (unstack_heads(dg(k3[s, :, cols], d_raw, 0, 0)) * 0.125).astype(BF)
        return carry

    def qkv_piece(i):
        cols = pl.ds(i * 2 * PAIR, 2 * PAIR)
        allt = toks3[...].reshape(seqs * keys, d)
        ga = dg(toks3[:, pl.ds(pl.multiple_of(n * quarter, quarter), quarter)].reshape(rows, d), dq[:, :, cols].reshape(rows, 2 * PAIR), 0, 0)
        gb = dg(allt, a_buf[:, cols], 0, 0)
        gc = dg(allt, b_buf[:, cols], 0, 0)
        left = left_lanes(R)
        p = nd + nu + 1 + i
        for e in range(4):
            rr = slice(e * R, (e + 1) * R)
            for j in range(2):
                sl = slice(j * PAIR, (j + 1) * PAIR)
                aj, bj, cj = ga[rr, sl], pltpu.roll(gb[rr, sl], HD, 1), gc[rr, sl]
                for t, val in enumerate((jnp.where(left, aj, bj), jnp.where(left, cj, aj), jnp.where(left, bj, cj))):
                    g[p, e % 2, e // 2, :, pl.ds((3 * j + t) * PAIR, PAIR)] = val.astype(BF)
        c1(p).start()

    cx1 = copy_to(dtok.at[:, 1 - c], x1, xs.at[0], xs.at[1], core_peer)
    cx2 = copy_to(dtok.at[1 - y, c], x2, xs.at[2], xs.at[3], y_peer)

    def input_part():
        def one(s, carry):
            t = dg(dk[s], wp[1], 1, 1) + dg(dv[s], wp[2], 1, 1)
            for e in range(4):
                dtok[e // 2, e % 2, s] = t[e * quarter:(e + 1) * quarter].astype(BF)
            return carry

        lax.fori_loop(0, seqs, one, 0)
        cx1.start()
        dsum[...] += dg(dq[...].reshape(rows, d), wp[0], 1, 1)

    def small(i, slot, dev):
        return copy_to(sbuf.at[i], srecv.at[slot], ss.at[slot], sq.at[slot], dev)

    def sums0():
        sbuf[0, 0:1] = jnp.sum(fold(dq[...].reshape(rows, d).astype(F32)), axis=0, keepdims=True)

        def add(s, acc):
            return acc + fold(dv[s].astype(F32))

        acc = lax.fori_loop(0, seqs, add, jnp.zeros((8, d), F32))
        sbuf[0, 1:2] = jnp.sum(acc, axis=0, keepdims=True)
        for i in range(3):
            sbuf[0, 2 + i:3 + i] = total(part[i])
        for i in range(nu):
            sbuf[0, 5 + i:6 + i] = total(part_up[:, i * d:(i + 1) * d])
        for i in range(3):
            sbuf[0, 5 + nu + i:6 + nu + i] = total(part2[i])
        small(0, 0, core_peer).start()

    def sums1():
        small(0, 0, core_peer).wait_recv()
        sbuf[1] = sbuf[0] + srecv[0]
        small(1, 1, y_peer).start()

    def sums2():
        small(1, 1, y_peer).wait_recv()
        sbuf[2] = sbuf[1] + srecv[1]
        small(2, 2, x_peer).start()

    def sums3():
        small(2, 2, x_peer).wait_recv()
        sbuf[3] = sbuf[2] + srecv[2]
        for e in range(3):
            small(3, 3 + e, z_peers[e]).start()

    def add_x1():
        cx1.wait_recv()

        def add(i, carry):
            a, b = i // seqs, i % seqs
            dtok[a, c, b] = (dtok[a, c, b].astype(F32) + x1[a, b].astype(F32)).astype(BF)
            return carry

        lax.fori_loop(0, 2 * seqs, add, 0)

    units = seqs * pairs
    slots_of_units = -(-units // UNITS)
    extra = {3: [rows_back], 9: [lambda: qkv_piece(0), sums0], 10: [lambda: qkv_piece(1), sums1],
             11: [lambda: qkv_piece(2), sums2], 12: [sums3], 13: [input_part], 14: [add_x1, cx2.start]}

    def slot(t, carry):
        for i in ORDER:
            p = t - LAGS[i]

            @pl.when(jnp.logical_and(p >= 0, p < pieces))
            def run():
                stages[i](p)

        @pl.when(jnp.logical_and(t > 3, t <= 3 + slots_of_units))
        def attention():
            lo = (t - 4) * UNITS
            lax.fori_loop(lo, jnp.minimum(lo + UNITS, units), unit, 0)

        for at, todo in extra.items():
            @pl.when(t == at)
            def more():
                for f in todo:
                    f()
        return carry

    lax.fori_loop(3, pieces + LAGS[6], slot, 0)
    cx2.wait_recv()

    def out_x(i, carry):
        r = pl.ds(pl.multiple_of(i * quarter, quarter), quarter)
        x1[0, i] = (dsum[r] + dtok[y, c, i].astype(F32) + x2[i].astype(F32)).astype(BF)
        return carry

    lax.fori_loop(0, seqs, out_x, 0)
    din_out = pltpu.make_async_copy(x1.at[0], din_hbm, xs.at[4])
    din_out.start()
    for e in range(3):
        small(3, 3 + e, z_peers[e]).wait_recv()
    so_ref[...] = sbuf[3] + srecv[3] + srecv[4] + srecv[5]
    small(0, 0, core_peer).wait_send()
    small(1, 1, y_peer).wait_send()
    small(2, 2, x_peer).wait_send()
    for e in range(3):
        small(3, 3 + e, z_peers[e]).wait_send()
    cx1.wait_send()
    cx2.wait_send()

    def drain(p, carry):
        c1(p).wait_send()
        c2(p).wait_send()
        c3(p).wait_send()
        c6(p, near).wait_send()
        store(p, oo_hbm).wait()
        for e in range(3):
            c4(p, e).wait_send()
            c5(p, e, z).wait_send()
        return carry

    lax.fori_loop(0, pieces, drain, 0)
    for s in range(seqs):
        send_y(s).wait_send()
        send_core(s).wait_send()
        forward_y(s).wait_send()
    din_out.wait()


def layer_part(tokens, lengths, w, qvb, wo, bo, g1, s1, wu, bu, wd, bd, g2, s2, cot):
    seqs, quarter, d = tokens.shape
    rows, keys, pairs, ff = seqs * quarter, 4 * quarter, d // PAIR, wu.shape[1]
    R = d // 4
    nd = nu = ff // d
    n = nd + nu + 4
    h = R // 2
    all_rows = (8 + nu, d)
    vm, hbm = pl.BlockSpec(memory_space=V), pl.BlockSpec(memory_space=ANY)
    S = jax.ShapeDtypeStruct
    own, every, flat = (seqs, quarter, d), (seqs, 4, quarter, d), (rows, d)
    row = V((d,), F32)
    return pl.pallas_call(
        layer_kernel,
        out_shape=(S(flat, BF), S((nd * R, d), BF), S((R, nu * d), BF), S((R, d), BF), S((R, 3 * d), BF), S(own, BF),
                   S(all_rows, F32)),
        in_specs=[pl.BlockSpec(memory_space=pltpu.SMEM)] + [hbm] * 14,
        out_specs=[hbm] * 6 + [vm],
        scratch_shapes=[V((seqs * keys, d), BF), V((seqs * keys, d), BF), V((2, 2) + own, BF), V(every, BF), V(every, BF),
                        V(every, BF), V(own, BF), V((seqs, pairs, keys, 2 * quarter), BF), V((3, d, d), BF),
                        V(flat, BF), V(flat, BF), V(flat, BF), V(flat, BF), V(own, BF), V(wo.shape, BF),
                        V(flat, F32), V(flat, F32), V(flat, F32), V((rows, 128), F32), V((3, 8, d), F32),
                        V((3, 8, d), F32), V((8, ff), F32), V((2, d), F32), row, row, row, V((ff,), F32), row, row, row,
                        V((n, 2, 2, R, d), BF), V((n, 2, R, d), BF), V((n, R, d), BF), V((n, h, d), BF),
                        V((n, 3, h // 2, d // 2), BF), V((4,) + all_rows, F32), V((6,) + all_rows, F32),
                        V((2,) + own, BF), V(own, BF), DMA((14 + nd + nu,))]
        + [DMA((seqs,))] * 6 + [DMA((n,))] * 6 + [DMA((n, 3))] * 4 + [DMA((n,))] * 3
        + [DMA((6,))] * 2 + [DMA((6,))],
        name="layer_part",
        compiler_params=pltpu.CompilerParams(collective_id=1, has_side_effects=True, vmem_limit_bytes=63 << 20),
    )(lengths, tokens, cot, w, wo, wu, wd, qvb, bo, g1, s1, bu, bd, g2, s2)


def finish_kernel(d_h, u_h, o_h, q_h, out_h, din_h, sums_ref, fd, fu, fo, fq, fout, fdin, qvb, outb, n1g, n1s, upb, downb, n2g, n2s,
                  low, full, rows, ls, os_):
    R, C = low.shape[1:]
    nd, nu = d_h.shape[0] // R, u_h.shape[1] // C
    cut = lambda ref, i: ref.at[:, pl.ds(i * C, C)]
    ends = ([(d_h.at[pl.ds(i * R, R)], fd.at[pl.ds(i * R, R)]) for i in range(nd)]
            + [(cut(u_h, i), cut(fu, i)) for i in range(nu)] + [(o_h, fo)]
            + [(cut(q_h, i), cut(fq, i)) for i in range(3)])
    loads = [pltpu.make_async_copy(s, low.at[i], ls.at[i]) for i, (s, _) in enumerate(ends)]
    stores = [pltpu.make_async_copy(full.at[i], t, os_.at[i]) for i, (_, t) in enumerate(ends)]
    pieces = len(ends)
    loads += [pltpu.make_async_copy(s, rows.at[i], ls.at[pieces + i]) for i, s in enumerate((out_h, din_h))]
    stores += [pltpu.make_async_copy(rows.at[i], t, os_.at[pieces + i]) for i, t in enumerate((fout, fdin))]
    for cp in loads:
        cp.start()
    n = lax.axis_index("narrow")
    for i in range(4):
        @pl.when(n == i)
        def pick():
            at = slice(i * R, (i + 1) * R)
            qvb[...] = sums_ref[0:2, at]
            for j, ref in ((2, outb), (3, n1g), (4, n1s), (5 + nu, downb), (6 + nu, n2g), (7 + nu, n2s)):
                ref[...] = sums_ref[j, at]
            upb[...] = sums_ref[5 + i]
    for i, (a, b) in enumerate(zip(loads, stores)):
        a.wait()
        if i < pieces:
            full[i] = low[i].astype(F32)
        b.start()
    for cp in stores:
        cp.wait()


def finish_part(down, up, out, qkv, output, input_grad, sums):
    R, d = out.shape
    n = down.shape[0] // R + up.shape[1] // d + 4
    vm, hbm = pl.BlockSpec(memory_space=V), pl.BlockSpec(memory_space=ANY)
    S = jax.ShapeDtypeStruct
    shapes = [S(a.shape, F32) for a in (down, up, out, qkv)] + [S(output.shape, BF)] * 2 + [S((2, R), F32)] + [S((R,), F32)] * 3
    shapes += [S((d,), F32)] + [S((R,), F32)] * 3
    return pl.pallas_call(
        finish_kernel,
        out_shape=shapes,
        in_specs=[hbm] * 6 + [vm],
        out_specs=[hbm] * 6 + [vm] * 8,
        scratch_shapes=[V((n, R, d), BF), V((n, R, d), F32), V((2,) + output.shape, BF), DMA((n + 2,)), DMA((n + 2,))],
        name="finish_part",
        compiler_params=pltpu.CompilerParams(vmem_limit_bytes=60 << 20),
    )(down, up, out, qkv, output, input_grad, sums)


def local(tokens, lengths, qkv_weight, qv_bias, out_weight, out_bias, norm1_gain, norm1_shift, up_weight, up_bias,
          down_weight, down_bias, norm2_gain, norm2_shift, cotangent):
    own = tokens.shape
    output, down, up, out, qkv, input_grad, sums = layer_part(
        tokens, lengths, qkv_weight, qv_bias, out_weight, out_bias, norm1_gain, norm1_shift, up_weight, up_bias,
        down_weight, down_bias, norm2_gain, norm2_shift, cotangent)
    wide = lax.axis_size("wide")
    if wide > 8:
        groups = [[j * 8 + i for j in range(wide // 8)] for i in range(8)]
        down, up, out, qkv = (
            lax.psum(a.astype(F32), "wide", axis_index_groups=groups).astype(BF) for a in (down, up, out, qkv))
        sums = lax.psum(sums, "wide", axis_index_groups=groups)
    down, up, out, qkv, output, input_grad, qvb, outb, n1g, n1s, upb, downb, n2g, n2s = finish_part(
        down, up, out, qkv, output, input_grad.reshape(output.shape), sums)
    return (output.reshape(own), input_grad.reshape(own), qkv, qvb, out, outb, n1g, n1s, up, upb, down, downb, n2g, n2s)


def solution(mesh):
    return jax.shard_map(
        local,
        mesh=mesh,
        in_specs=(
            P("wide", "narrow", None),
            P("wide"),
            P(),
            P(),
            P(),
            P(),
            P(),
            P(),
            P(),
            P(),
            P(),
            P(),
            P(),
            P(),
            P("wide", "narrow", None),
        ),
        out_specs=(
            P("wide", "narrow", None),
            P("wide", "narrow", None),
            P("narrow", None),
            P(None, "narrow"),
            P("narrow", None),
            P("narrow"),
            P("narrow"),
            P("narrow"),
            P("narrow", None),
            P("narrow"),
            P("narrow", None),
            P("narrow"),
            P("narrow"),
            P("narrow"),
        ),
        check_vma=False,
    )
```

```python
import functools

import jax
import jax.numpy as jnp
from jax import lax
from jax.experimental import pallas as pl
from jax.experimental.pallas import tpu as pltpu
from jax.sharding import PartitionSpec as P

H = 12
HD = 64
PAIR = 2 * HD
epsilon = 1e-12
root_half = 0.7071067811865476
inv_root_two_pi = 0.3989422804014327
MESH = pl.DeviceIdType.MESH
F32 = jnp.float32
BF = jnp.bfloat16
V = pltpu.VMEM
DMA = pltpu.SemaphoreType.DMA
ANY = pl.ANY
UNROLL_ATT = 6
UNROLL_UP = 3


def dg(a, b, ca, cb):
    return lax.dot_general(a, b, (((ca,), (cb,)), ((), ())), preferred_element_type=F32)


def copy_to(src, dst, ss, rs, dev):
    return pltpu.make_async_remote_copy(
        src_ref=src, dst_ref=dst, send_sem=ss, recv_sem=rs, device_id=dev, device_id_type=MESH)


def left_lanes(rows):
    return lax.broadcasted_iota(jnp.int32, (rows, PAIR), 1) < HD


def stack_heads(x):
    left = left_lanes(x.shape[0])
    zero = jnp.zeros_like(x)
    return jnp.concatenate([jnp.where(left, x, zero), jnp.where(left, zero, x)], axis=0)


def unstack_heads(x_t):
    q = x_t.shape[1] // 2
    top = lax.broadcasted_iota(jnp.int32, (PAIR, q), 0) < HD
    return jnp.where(top, x_t[:, :q], x_t[:, q:]).T


def fold(x):
    return jnp.sum(x.reshape(x.shape[0] // 8, 8, x.shape[1]), axis=0)


def total(x):
    return jnp.sum(x, axis=0, keepdims=True)


def center_scale(v):
    center = v - jnp.mean(v, axis=-1, keepdims=True)
    scale = lax.rsqrt(jnp.mean(center * center, axis=-1, keepdims=True) + epsilon)
    return center * scale, scale


def norm_grad(g, normed):
    return g - jnp.mean(g, axis=-1, keepdims=True) - normed * jnp.mean(g * normed, axis=-1, keepdims=True)


LAGS = (0, 1, 3, 4, 5, 7, 11)
UNITS = 4
ORDER = (3, 2, 5, 4, 6, 1)
UNROLL_BACK = 1


def layer_kernel(len_ref, tok_h, cot_h, w_h, wo_h, wu_h, wd_h, qvb_h, bo_h, g1_h, s1_h, bu_h, bd_h, g2_h, s2_h,
                 out_h, od_hbm, ou_hbm, oo_hbm, oq_hbm, din_hbm, so_hbm,
                 a_buf, b_buf, dtok, toks, k, v, q, pr, wp, ctx, low1, dffn, datt, dq, wo, dsum, first, normed1,
                 scale1, part, part2, part_up, qvb_ref, bo_v, g1_v, s1_v, bu_v, bd_v, g2_v, s2_v,
                 g, r1, r2, r3, r4, sbuf, srecv, so_v, x1, x2,
                 ls, cs, cr, ys, yr, fs, fr,
                 s1, q1, s2, q2, s3, q3, s4, q4, s5, q5, s6, q6, os_, ss, sq, xs):
    pieces, _, _, R, C = g.shape
    seqs, quarter, d = q.shape
    rows, keys, pairs = seqs * quarter, 4 * quarter, d // PAIR
    ff = wu_h.shape[1]
    nd = nu = ff // d
    h = R // 2
    hr, hc = h // 2, C // 2
    w, n = lax.axis_index("wide"), lax.axis_index("narrow")
    c, y, x, z = n % 2, n // 2, w % 2, (w // 2) % 4
    core_n, y_n = n + 1 - 2 * c, n + 2 - 4 * y
    far_n = core_n + 2 - 4 * y
    core_peer, y_peer, x_peer = (w, core_n), (w, y_n), (w + 1 - 2 * x, n)
    zs = [z + 1 - 2 * (z % 2), z + 2 - 4 * (z // 2), 3 - z]
    z_peers = [(w + 2 * (j - z), n) for j in zs]
    gp = g.reshape(pieces, d, d)
    a_view, b_view = a_buf.reshape(nd, rows, d), b_buf.reshape(nu, rows, d)
    dk, dv = a_buf.reshape(seqs, keys, d), b_buf.reshape(seqs, keys, d)
    slope = dtok.reshape(nd, rows, d)
    tok = datt.reshape(seqs, quarter, d)
    dctx = low1.reshape(seqs, quarter, d)
    out = dq.reshape(rows, d)
    cot = dffn.reshape(seqs, quarter, d)
    toks3, k3, v3 = (r.reshape(seqs, keys, d) for r in (toks, k, v))
    blocks = lambda ref, i: ref.at[:, i * d:(i + 1) * d]
    moves = [(tok_h, tok)] + [(blocks(w_h, i), gp.at[i]) for i in range(3)] + [
        (qvb_h, qvb_ref), (bo_h, bo_v), (g1_h, g1_v), (s1_h, s1_v), (bu_h, bu_v), (bd_h, bd_v), (g2_h, g2_v),
        (s2_h, s2_v), (wo_h, wo)] + [(blocks(wu_h, i), gp.at[nd + i]) for i in range(nu)] + [(cot_h, cot)] + [
        (wd_h.at[pl.ds(i * d, d)], gp.at[nd + nu + i]) for i in range(nd)]
    loads = [pltpu.make_async_copy(s, t, ls.at[i]) for i, (s, t) in enumerate(moves)]
    for cp in loads[:4]:
        cp.start()
    bar = pltpu.get_barrier_semaphore()
    for dev in [core_peer, y_peer, x_peer] + z_peers:
        pl.semaphore_signal(bar, inc=1, device_id=dev, device_id_type=MESH)
    pl.semaphore_wait(bar, 6)

    def send_y(s):
        return copy_to(tok_h.at[s], toks.at[s, n], ys.at[s], yr.at[s], y_peer)

    def send_core(s):
        return copy_to(tok_h.at[s], toks.at[s, n], cs.at[s], cr.at[s], core_peer)

    def forward_y(s):
        return copy_to(toks.at[s, y_n], toks.at[s, y_n], fs.at[s], fr.at[s], core_peer)

    for s in range(seqs):
        send_y(s).start()
        send_core(s).start()
    for cp in loads[4:]:
        cp.start()
    loads[0].wait()
    for s in range(seqs):
        toks[s, n] = tok[s]
    for cp in loads[1:4]:
        cp.wait()
    left = left_lanes(d)
    for p in range(pairs):
        t0, t1, t2 = (gp[p // 2, :, pl.ds((p % 2 * 3 + i) * PAIR, PAIR)].astype(F32) for i in range(3))
        cols = pl.ds(p * PAIR, PAIR)
        wp[0, :, cols] = jnp.where(left, t0, t1).astype(BF)
        wp[1, :, cols] = pltpu.roll(jnp.where(left, t2, t0), HD, 1).astype(BF)
        wp[2, :, cols] = jnp.where(left, t1, t2).astype(BF)
    for cp in loads[4:12]:
        cp.wait()
    bo_ref, g1_ref, s1_ref, bd_ref, g2_ref, s2_ref = (
        r[...].reshape(1, d) for r in (bo_v, g1_v, s1_v, bd_v, g2_v, s2_v))
    own = tok[...].reshape(rows, d)
    q[...] = ((dg(own, wp[0], 1, 0) + qvb_ref[0:1, :]).astype(BF) * 0.125).reshape(seqs, quarter, d)

    def project(s, half):
        blocks = pl.ds(2 * half, 2)
        x = toks[s, blocks].reshape(2 * quarter, d)
        k[s, blocks] = dg(x, wp[1], 1, 0).astype(BF).reshape(2, quarter, d)
        v[s, blocks] = (dg(x, wp[2], 1, 0) + qvb_ref[1:2, :]).astype(BF).reshape(2, quarter, d)

    for s in range(seqs):
        send_core(s).wait_recv()
    for s in range(seqs):
        project(s, y)

    def fetch_far(s):
        copy_to(toks.at[s, y_n], toks.at[s, y_n], ys.at[s], yr.at[s], y_peer).wait_recv()
        forward_y(s).start()

    fetch_far(0)
    for s in range(seqs):
        copy_to(toks.at[s, far_n], toks.at[s, far_n], fs.at[s], fr.at[s], core_peer).wait_recv()
        project(s, 1 - y)
        if s + 1 < seqs:
            fetch_far(s + 1)
        live = lax.broadcasted_iota(jnp.int32, (keys, 2 * quarter), 0) < len_ref[s]

        def unit(p, carry):
            cols = pl.ds(pl.multiple_of(p * PAIR, PAIR), PAIR)
            qs = stack_heads(q[s, :, cols])
            kp = k[s, :, :, cols].reshape(keys, PAIR)
            vp = v[s, :, :, cols].reshape(keys, PAIR)
            scores = jnp.where(live, dg(kp, qs, 1, 1), -1000000000.0)
            e = jnp.exp(scores - jnp.max(scores, axis=0, keepdims=True))
            probs = (e * (1.0 / jnp.sum(e, axis=0, keepdims=True))).astype(BF)
            pr[s, p] = probs
            ctx[s * quarter:(s + 1) * quarter, cols] = unstack_heads(dg(vp, probs, 0, 0)).astype(BF)
            return carry

        lax.fori_loop(0, pairs, unit, 0, unroll=UNROLL_ATT)

    part2[...] = jnp.zeros_like(part2)
    chunk = 64
    chunks = rows // chunk
    loads[12].wait()
    for b in range(d // 256):
        cols = pl.ds(b * 256, 256)
        dsum[:, cols] = (dg(ctx[...], wo[:, cols], 1, 0) + bo_ref[:, b * 256:(b + 1) * 256]
                        + tok[:, :, cols].reshape(rows, 256).astype(F32))

    def norm1(i, carry):
        r = pl.ds(pl.multiple_of(i * chunk, chunk), chunk)
        normed, scale = center_scale(dsum[r])
        x = normed * g1_ref + s1_ref
        normed1[r] = normed
        scale1[r] = jnp.broadcast_to(scale, (chunk, 128))
        first[r] = x
        low1[r] = x.astype(BF)
        return carry

    lax.fori_loop(0, chunks, norm1, 0)
    for cp in loads[13:13 + nu]:
        cp.wait()

    def up(j, carry):
        cols = pl.ds(pl.multiple_of(j * 256, 256), 256)
        at = (j // 3, slice(None), pl.ds(pl.multiple_of(j % 3 * 256, 256), 256))
        pre = dg(low1[...], gp[(nd + at[0],) + at[1:]], 1, 0) + bu_v[cols].reshape(1, 256)
        half = 0.5 + 0.5 * lax.erf(pre * root_half)
        a_view[at] = (pre * half).astype(BF)
        slope[at] = (half + pre * (jnp.exp(-0.5 * pre * pre) * inv_root_two_pi)).astype(BF)
        return carry

    lax.fori_loop(0, ff // 256, up, 0, unroll=UNROLL_UP)
    for cp in loads[13 + nu:]:
        cp.wait()
    for b in range(d // 256):
        cols = pl.ds(b * 256, 256)
        dsum[:, cols] = bd_ref[:, b * 256:(b + 1) * 256] + first[:, cols] + sum(
            dg(a_view[i], gp[nd + nu + i, :, cols], 1, 0) for i in range(ff // d))

    def norm2(i, carry):
        r = pl.ds(pl.multiple_of(i * chunk, chunk), chunk)
        normed, scale = center_scale(dsum[r])
        out[r] = (normed * g2_ref + s2_ref).astype(BF)
        s = i * chunk // quarter
        off = pl.multiple_of(i * chunk - s * quarter, chunk)
        pos = n * quarter + off + lax.broadcasted_iota(jnp.int32, (chunk, d), 0)
        d_out = jnp.where(pos < len_ref[s], cot[s, pl.ds(off, chunk)].astype(F32), 0.0)
        part2[1] += fold(d_out * normed)
        part2[2] += fold(d_out)
        d_second = scale * norm_grad(d_out * g2_ref, normed)
        dsum[r] = d_second
        low = d_second.astype(BF)
        dffn[r] = low
        part2[0] += fold(low.astype(F32))
        return carry

    lax.fori_loop(0, chunks, norm2, 0)
    out_store = pltpu.make_async_copy(out, out_h, xs.at[5])
    out_store.start()

    def cut(j):
        return (pl.ds(pl.multiple_of(x * h + (j // 2) * hr, 16), hr), pl.ds(pl.multiple_of((j % 2) * hc, 128), hc))

    near = pl.ds(pl.multiple_of(x * h, 16), h)
    away = pl.ds(pl.multiple_of((1 - x) * h, 16), h)

    def c1(p):
        return copy_to(g.at[p, 1 - c], r1.at[p], s1.at[p], q1.at[p], core_peer)

    def c2(p):
        return copy_to(g.at[p, c, 1 - y], r2.at[p], s2.at[p], q2.at[p], y_peer)

    def c3(p):
        return copy_to(g.at[p, c, y, away], r3.at[p], s3.at[p], q3.at[p], x_peer)

    def c4(p, e):
        rr, cc = cut(zs[e])
        return copy_to(g.at[p, c, y, rr, cc], r4.at[p, e], s4.at[p, e], q4.at[p, e], z_peers[e])

    def c5(p, e, j):
        rr, cc = cut(j)
        return copy_to(r1.at[p, 0, rr, cc], r1.at[p, 0, rr, cc], s5.at[p, e], q5.at[p, e], z_peers[e])

    def c6(p, rr):
        return copy_to(r1.at[p, 0, rr], r1.at[p, 0, rr], s6.at[p], q6.at[p], x_peer)

    def store(p, dst):
        return pltpu.make_async_copy(r1.at[p, 0], dst, os_.at[p])

    def st1(p):
        c1(p).wait_recv()
        g[p, c] = (g[p, c].astype(F32) + r1[p].astype(F32)).astype(BF)
        c2(p).start()

    def st2(p):
        c2(p).wait_recv()
        g[p, c, y] = (g[p, c, y].astype(F32) + r2[p].astype(F32)).astype(BF)
        c3(p).start()

    def st3(p):
        c3(p).wait_recv()
        g[p, c, y, near] = (g[p, c, y, near].astype(F32) + r3[p].astype(F32)).astype(BF)
        for e in (1, 2, 0):
            c4(p, e).start()

    def st4(p):
        for e in range(3):
            c4(p, e).wait_recv()
        rr, cc = cut(z)
        t = g[p, c, y, rr, cc].astype(F32) + r4[p, 0].astype(F32) + r4[p, 1].astype(F32) + r4[p, 2].astype(F32)
        r1[p, 0, rr, cc] = t.astype(BF)
        for e in (1, 2, 0):
            c5(p, e, z).start()

    def st5(p):
        for e in range(3):
            c5(p, e, zs[e]).wait_recv()
        c6(p, near).start()

    def st6(p):
        c6(p, away).wait_recv()

        @pl.when(p < nd)
        def down():
            store(p, od_hbm.at[pl.ds(p * R, R)]).start()

        @pl.when(jnp.logical_and(p >= nd, p < nd + nu))
        def up():
            store(p, ou_hbm.at[:, pl.ds(pl.multiple_of((p - nd) * C, C), C)]).start()

        @pl.when(p == nd + nu)
        def out():
            store(p, oo_hbm).start()

        @pl.when(p > nd + nu)
        def qkv():
            store(p, oq_hbm.at[:, pl.ds(pl.multiple_of((p - nd - nu - 1) * C, C), C)]).start()

    stages = [None, st1, st2, st3, st4, st5, st6]

    block = 256
    for a in range(d // block):
        def down_block(i, carry):
            t = dg(a_view[i, :, a * block:(a + 1) * block], dffn[...], 0, 0).astype(BF)
            for j in range(nd):
                lo, hi = max(j * R, a * block), min((j + 1) * R, (a + 1) * block)
                if lo < hi:
                    g[j, i % 2, i // 2, lo - j * R:hi - j * R] = t[lo - a * block:hi - a * block]
            return carry

        lax.fori_loop(0, nd, down_block, 0)
        for p in range(a * block // R, nd if a == d // block - 1 else (a + 1) * block // R):
            c1(p).start()
        if a == 1:
            st1(0)
    st1(1)

    def up_back(j, carry):
        at = (j // 3, slice(None), pl.ds(pl.multiple_of(j % 3 * 256, 256), 256))
        low = (dg(dffn[...], gp[nd + nu + j // 3, pl.ds(pl.multiple_of(j % 3 * 256, 256), 256)], 1, 1) * slope[at].astype(F32)).astype(BF)
        b_view[at] = low
        part_up[:, pl.ds(pl.multiple_of(j * 256, 256), 256)] = fold(low.astype(F32))
        return carry

    lax.fori_loop(0, ff // 256, up_back, 0, unroll=UNROLL_BACK)
    for b in range(d // 256):
        cols = pl.ds(b * 256, 256)
        dsum[:, cols] += sum(dg(b_view[i], gp[nd + i, cols, :], 1, 1) for i in range(nu))

    def row_block(p, t):
        for j in range(4):
            g[p, j % 2, j // 2] = t[j * R:(j + 1) * R].astype(BF)

    def up_block(i, carry):
        row_block(nd + i, dg(low1[...], b_view[i], 0, 0))
        c1(nd + i).start()
        return carry

    lax.fori_loop(0, nu, up_block, 0)

    def rows_back():
        part[...] = jnp.zeros_like(part)
        chunk = 64
        gain = g1_v[...].reshape(1, d)

        def norm1_back(i, carry):
            r = pl.ds(pl.multiple_of(i * chunk, chunk), chunk)
            d_first, normed = dsum[r], normed1[r]
            part[1] += fold(d_first * normed)
            part[2] += fold(d_first)
            d_sum = scale1[r, :1] * norm_grad(d_first * gain, normed)
            dsum[r] = d_sum
            low = d_sum.astype(BF)
            datt[r] = low
            part[0] += fold(low.astype(F32))
            return carry

        lax.fori_loop(0, rows // chunk, norm1_back, 0)
        row_block(nd + nu, dg(ctx[...], datt[...], 0, 0))
        c1(nd + nu).start()
        dctx[...] = dg(datt[...], wo[...], 1, 1).astype(BF).reshape(seqs, quarter, d)
        out_store.wait()

    def unit(u, carry):
        s, p = u // pairs, u % pairs
        cols = pl.ds(pl.multiple_of(p * PAIR, PAIR), PAIR)
        qs = stack_heads(q[s, :, cols])
        ds = stack_heads(dctx[s, :, cols])
        low = pr[s, p]
        probs = low.astype(F32)
        t = probs * dg(v3[s, :, cols], ds, 1, 1)
        d_raw = (t - probs * jnp.sum(t, axis=0, keepdims=True)).astype(BF)
        dv[s, :, cols] = dg(low, ds, 1, 0).astype(BF)
        dk[s, :, cols] = dg(d_raw, qs, 1, 0).astype(BF)
        dq[s, :, cols] = (unstack_heads(dg(k3[s, :, cols], d_raw, 0, 0)) * 0.125).astype(BF)
        return carry

    def qkv_piece(i):
        cols = pl.ds(i * 2 * PAIR, 2 * PAIR)
        allt = toks3[...].reshape(seqs * keys, d)
        ga = dg(toks3[:, pl.ds(pl.multiple_of(n * quarter, quarter), quarter)].reshape(rows, d), dq[:, :, cols].reshape(rows, 2 * PAIR), 0, 0)
        gb = dg(allt, a_buf[:, cols], 0, 0)
        gc = dg(allt, b_buf[:, cols], 0, 0)
        left = left_lanes(R)
        p = nd + nu + 1 + i
        for e in range(4):
            rr = slice(e * R, (e + 1) * R)
            for j in range(2):
                sl = slice(j * PAIR, (j + 1) * PAIR)
                aj, bj, cj = ga[rr, sl], pltpu.roll(gb[rr, sl], HD, 1), gc[rr, sl]
                for t, val in enumerate((jnp.where(left, aj, bj), jnp.where(left, cj, aj), jnp.where(left, bj, cj))):
                    g[p, e % 2, e // 2, :, pl.ds((3 * j + t) * PAIR, PAIR)] = val.astype(BF)
        c1(p).start()

    cx1 = copy_to(dtok.at[:, 1 - c], x1, xs.at[0], xs.at[1], core_peer)
    cx2 = copy_to(dtok.at[1 - y, c], x2, xs.at[2], xs.at[3], y_peer)

    def input_part():
        def one(s, carry):
            t = dg(dk[s], wp[1], 1, 1) + dg(dv[s], wp[2], 1, 1)
            for e in range(4):
                dtok[e // 2, e % 2, s] = t[e * quarter:(e + 1) * quarter].astype(BF)
            return carry

        lax.fori_loop(0, seqs, one, 0)
        cx1.start()
        dsum[...] += dg(dq[...].reshape(rows, d), wp[0], 1, 1)

    def small(i, slot, dev):
        return copy_to(sbuf.at[i], srecv.at[slot], ss.at[slot], sq.at[slot], dev)

    def sums0():
        sbuf[0, 0:1] = jnp.sum(fold(dq[...].reshape(rows, d).astype(F32)), axis=0, keepdims=True)

        def add(s, acc):
            return acc + fold(dv[s].astype(F32))

        acc = lax.fori_loop(0, seqs, add, jnp.zeros((8, d), F32))
        sbuf[0, 1:2] = jnp.sum(acc, axis=0, keepdims=True)
        for i in range(3):
            sbuf[0, 2 + i:3 + i] = total(part[i])
        for i in range(nu):
            sbuf[0, 5 + i:6 + i] = total(part_up[:, i * d:(i + 1) * d])
        for i in range(3):
            sbuf[0, 5 + nu + i:6 + nu + i] = total(part2[i])
        small(0, 0, core_peer).start()

    def sums1():
        small(0, 0, core_peer).wait_recv()
        sbuf[1] = sbuf[0] + srecv[0]
        small(1, 1, y_peer).start()

    def sums2():
        small(1, 1, y_peer).wait_recv()
        sbuf[2] = sbuf[1] + srecv[1]
        small(2, 2, x_peer).start()

    def sums3():
        small(2, 2, x_peer).wait_recv()
        sbuf[3] = sbuf[2] + srecv[2]
        for e in range(3):
            small(3, 3 + e, z_peers[e]).start()

    so_store = pltpu.make_async_copy(so_v, so_hbm, xs.at[6])

    def sums4():
        for e in range(3):
            small(3, 3 + e, z_peers[e]).wait_recv()
        so_v[...] = sbuf[3] + srecv[3] + srecv[4] + srecv[5]
        so_store.start()

    def add_x1():
        cx1.wait_recv()

        def add(i, carry):
            a, b = i // seqs, i % seqs
            dtok[a, c, b] = (dtok[a, c, b].astype(F32) + x1[a, b].astype(F32)).astype(BF)
            return carry

        lax.fori_loop(0, 2 * seqs, add, 0)

    units = seqs * pairs
    slots_of_units = -(-units // UNITS)
    extra = {3: [rows_back], 9: [lambda: qkv_piece(0)], 10: [lambda: qkv_piece(1), lambda: qkv_piece(2), sums0],
             11: [input_part, sums1], 12: [add_x1, sums2], 13: [cx2.start, sums3], 16: [sums4]}

    def drain(p):
        c1(p).wait_send()
        c2(p).wait_send()
        c3(p).wait_send()
        c6(p, near).wait_send()
        for e in range(3):
            c4(p, e).wait_send()
            c5(p, e, z).wait_send()

    def slot(t, carry):
        for i in ORDER:
            p = t - LAGS[i]

            @pl.when(jnp.logical_and(p >= 0, p < pieces))
            def run():
                stages[i](p)

        @pl.when(jnp.logical_and(t > 3, t <= 3 + slots_of_units))
        def attention():
            lo = (t - 4) * UNITS
            lax.fori_loop(lo, jnp.minimum(lo + UNITS, units), unit, 0)

        for at, todo in extra.items():
            @pl.when(t == at)
            def more():
                for f in todo:
                    f()

        old = t - LAGS[5] - 3

        @pl.when(jnp.logical_and(old >= 0, old < pieces))
        def finished():
            drain(old)
        return carry

    lax.fori_loop(3, pieces + LAGS[6], slot, 0)
    cx2.wait_recv()

    def out_x(i, carry):
        r = pl.ds(pl.multiple_of(i * quarter, quarter), quarter)
        x1[0, i] = (dsum[r] + dtok[y, c, i].astype(F32) + x2[i].astype(F32)).astype(BF)
        return carry

    lax.fori_loop(0, seqs, out_x, 0)
    din_out = pltpu.make_async_copy(x1.at[0], din_hbm, xs.at[4])
    din_out.start()
    small(0, 0, core_peer).wait_send()
    small(1, 1, y_peer).wait_send()
    small(2, 2, x_peer).wait_send()
    for e in range(3):
        small(3, 3 + e, z_peers[e]).wait_send()
    cx1.wait_send()
    cx2.wait_send()

    def stored(p, carry):
        store(p, oo_hbm).wait()
        return carry

    lax.fori_loop(0, pieces, stored, 0)
    for s in range(seqs):
        send_y(s).wait_send()
        send_core(s).wait_send()
        forward_y(s).wait_send()
    din_out.wait()
    so_store.wait()


def layer_part(tokens, lengths, w, qvb, wo, bo, g1, s1, wu, bu, wd, bd, g2, s2, cot):
    seqs, quarter, d = tokens.shape
    rows, keys, pairs, ff = seqs * quarter, 4 * quarter, d // PAIR, wu.shape[1]
    R = d // 4
    nd = nu = ff // d
    n = nd + nu + 4
    h = R // 2
    all_rows = (8 + nu, d)
    vm, hbm = pl.BlockSpec(memory_space=V), pl.BlockSpec(memory_space=ANY)
    S = jax.ShapeDtypeStruct
    own, every, flat = (seqs, quarter, d), (seqs, 4, quarter, d), (rows, d)
    row = V((d,), F32)
    return pl.pallas_call(
        layer_kernel,
        out_shape=(S(flat, BF), S((nd * R, d), BF), S((R, nu * d), BF), S((R, d), BF), S((R, 3 * d), BF), S(own, BF),
                   S(all_rows, F32)),
        in_specs=[pl.BlockSpec(memory_space=pltpu.SMEM)] + [hbm] * 14,
        out_specs=[hbm] * 7,
        scratch_shapes=[V((seqs * keys, d), BF), V((seqs * keys, d), BF), V((2, 2) + own, BF), V(every, BF), V(every, BF),
                        V(every, BF), V(own, BF), V((seqs, pairs, keys, 2 * quarter), BF), V((3, d, d), BF),
                        V(flat, BF), V(flat, BF), V(flat, BF), V(flat, BF), V(own, BF), V(wo.shape, BF),
                        V(flat, F32), V(flat, F32), V(flat, F32), V((rows, 128), F32), V((3, 8, d), F32),
                        V((3, 8, d), F32), V((8, ff), F32), V((2, d), F32), row, row, row, V((ff,), F32), row, row, row,
                        V((n, 2, 2, R, d), BF), V((n, 2, R, d), BF), V((n, R, d), BF), V((n, h, d), BF),
                        V((n, 3, h // 2, d // 2), BF), V((4,) + all_rows, F32), V((6,) + all_rows, F32),
                        V(all_rows, F32), V((2,) + own, BF), V(own, BF), DMA((14 + nd + nu,))]
        + [DMA((seqs,))] * 6 + [DMA((n,))] * 6 + [DMA((n, 3))] * 4 + [DMA((n,))] * 3
        + [DMA((6,))] * 2 + [DMA((7,))],
        name="layer_part",
        compiler_params=pltpu.CompilerParams(collective_id=1, has_side_effects=True, vmem_limit_bytes=63 << 20),
    )(lengths, tokens, cot, w, wo, wu, wd, qvb, bo, g1, s1, bu, bd, g2, s2)


def finish_kernel(d_h, u_h, o_h, q_h, out_h, din_h, sums_h, fd, fu, fo, fq, fout, fdin,
                  qvb_h, outb_h, n1g_h, n1s_h, upb_h, downb_h, n2g_h, n2s_h,
                  low, full, rows, sums_ref, qvb, outb, n1g, n1s, upb, downb, n2g, n2s, ls, os_, ms):
    R, C = low.shape[1:]
    nd, nu = d_h.shape[0] // R, u_h.shape[1] // C
    cut = lambda ref, i: ref.at[:, pl.ds(i * C, C)]
    ends = ([(d_h.at[pl.ds(i * R, R)], fd.at[pl.ds(i * R, R)]) for i in range(nd)]
            + [(cut(u_h, i), cut(fu, i)) for i in range(nu)] + [(o_h, fo)]
            + [(cut(q_h, i), cut(fq, i)) for i in range(3)])
    loads = [pltpu.make_async_copy(s, low.at[i], ls.at[i]) for i, (s, _) in enumerate(ends)]
    stores = [pltpu.make_async_copy(full.at[i], t, os_.at[i]) for i, (_, t) in enumerate(ends)]
    pieces = len(ends)
    loads += [pltpu.make_async_copy(s, rows.at[i], ls.at[pieces + i]) for i, s in enumerate((out_h, din_h))]
    stores += [pltpu.make_async_copy(rows.at[i], t, os_.at[pieces + i]) for i, t in enumerate((fout, fdin))]
    sums_load = pltpu.make_async_copy(sums_h, sums_ref, ms.at[8])
    sums_load.start()
    for cp in loads:
        cp.start()
    small = [pltpu.make_async_copy(s, t, ms.at[i]) for i, (s, t) in enumerate(
        ((qvb, qvb_h), (outb, outb_h), (n1g, n1g_h), (n1s, n1s_h), (upb, upb_h), (downb, downb_h), (n2g, n2g_h),
         (n2s, n2s_h)))]
    sums_load.wait()
    n = lax.axis_index("narrow")
    for i in range(4):
        @pl.when(n == i)
        def pick():
            at = slice(i * R, (i + 1) * R)
            qvb[...] = sums_ref[0:2, at]
            for j, ref in ((2, outb), (3, n1g), (4, n1s), (5 + nu, downb), (6 + nu, n2g), (7 + nu, n2s)):
                ref[...] = sums_ref[j, at]
            upb[...] = sums_ref[5 + i]
    for cp in small:
        cp.start()
    for i, (a, b) in enumerate(zip(loads, stores)):
        a.wait()
        if i < pieces:
            full[i] = low[i].astype(F32)
        b.start()
    for cp in stores + small:
        cp.wait()


def finish_part(down, up, out, qkv, output, input_grad, sums):
    R, d = out.shape
    n = down.shape[0] // R + up.shape[1] // d + 4
    vm, hbm = pl.BlockSpec(memory_space=V), pl.BlockSpec(memory_space=ANY)
    S = jax.ShapeDtypeStruct
    shapes = [S(a.shape, F32) for a in (down, up, out, qkv)] + [S(output.shape, BF)] * 2 + [S((2, R), F32)] + [S((R,), F32)] * 3
    shapes += [S((d,), F32)] + [S((R,), F32)] * 3
    return pl.pallas_call(
        finish_kernel,
        out_shape=shapes,
        in_specs=[hbm] * 7,
        out_specs=[hbm] * 14,
        scratch_shapes=[V((n, R, d), BF), V((n, R, d), F32), V((2,) + output.shape, BF), V(sums.shape, F32)]
        + [V(a.shape, F32) for a in shapes[6:]] + [DMA((n + 2,)), DMA((n + 2,)), DMA((9,))],
        name="finish_part",
        compiler_params=pltpu.CompilerParams(vmem_limit_bytes=60 << 20),
    )(down, up, out, qkv, output, input_grad, sums)


def local(tokens, lengths, qkv_weight, qv_bias, out_weight, out_bias, norm1_gain, norm1_shift, up_weight, up_bias,
          down_weight, down_bias, norm2_gain, norm2_shift, cotangent):
    own = tokens.shape
    output, down, up, out, qkv, input_grad, sums = layer_part(
        tokens, lengths, qkv_weight, qv_bias, out_weight, out_bias, norm1_gain, norm1_shift, up_weight, up_bias,
        down_weight, down_bias, norm2_gain, norm2_shift, cotangent)
    wide = lax.axis_size("wide")
    if wide > 8:
        groups = [[j * 8 + i for j in range(wide // 8)] for i in range(8)]
        down, up, out, qkv = (
            lax.psum(a.astype(F32), "wide", axis_index_groups=groups).astype(BF) for a in (down, up, out, qkv))
        sums = lax.psum(sums, "wide", axis_index_groups=groups)
    down, up, out, qkv, output, input_grad, qvb, outb, n1g, n1s, upb, downb, n2g, n2s = finish_part(
        down, up, out, qkv, output, input_grad.reshape(output.shape), sums)
    return (output.reshape(own), input_grad.reshape(own), qkv, qvb, out, outb, n1g, n1s, up, upb, down, downb, n2g, n2s)


def solution(mesh):
    return jax.shard_map(
        local,
        mesh=mesh,
        in_specs=(
            P("wide", "narrow", None),
            P("wide"),
            P(),
            P(),
            P(),
            P(),
            P(),
            P(),
            P(),
            P(),
            P(),
            P(),
            P(),
            P(),
            P("wide", "narrow", None),
        ),
        out_specs=(
            P("wide", "narrow", None),
            P("wide", "narrow", None),
            P("narrow", None),
            P(None, "narrow"),
            P("narrow", None),
            P("narrow"),
            P("narrow"),
            P("narrow"),
            P("narrow", None),
            P("narrow"),
            P("narrow", None),
            P("narrow"),
            P("narrow"),
            P("narrow"),
        ),
        check_vma=False,
    )
```

```python
import functools

import jax
import jax.numpy as jnp
from jax import lax
from jax.experimental import pallas as pl
from jax.experimental.pallas import tpu as pltpu
from jax.sharding import PartitionSpec as P

H = 12
HD = 64
PAIR = 2 * HD
epsilon = 1e-12
root_half = 0.7071067811865476
inv_root_two_pi = 0.3989422804014327
MESH = pl.DeviceIdType.MESH
F32 = jnp.float32
BF = jnp.bfloat16
V = pltpu.VMEM
DMA = pltpu.SemaphoreType.DMA
ANY = pl.ANY
UNROLL_ATT = 6
UNROLL_UP = 6


def dg(a, b, ca, cb):
    return lax.dot_general(a, b, (((ca,), (cb,)), ((), ())), preferred_element_type=F32)


def copy_to(src, dst, ss, rs, dev):
    return pltpu.make_async_remote_copy(
        src_ref=src, dst_ref=dst, send_sem=ss, recv_sem=rs, device_id=dev, device_id_type=MESH)


def left_lanes(rows):
    return lax.broadcasted_iota(jnp.int32, (rows, PAIR), 1) < HD


def stack_heads(x):
    left = left_lanes(x.shape[0])
    zero = jnp.zeros_like(x)
    return jnp.concatenate([jnp.where(left, x, zero), jnp.where(left, zero, x)], axis=0)


def unstack_heads(x_t):
    q = x_t.shape[1] // 2
    top = lax.broadcasted_iota(jnp.int32, (PAIR, q), 0) < HD
    return jnp.where(top, x_t[:, :q], x_t[:, q:]).T


def fold(x):
    return jnp.sum(x.reshape(x.shape[0] // 8, 8, x.shape[1]), axis=0)


def total(x):
    return jnp.sum(x, axis=0, keepdims=True)


def center_scale(v):
    center = v - jnp.mean(v, axis=-1, keepdims=True)
    scale = lax.rsqrt(jnp.mean(center * center, axis=-1, keepdims=True) + epsilon)
    return center * scale, scale


def norm_grad(g, normed):
    return g - jnp.mean(g, axis=-1, keepdims=True) - normed * jnp.mean(g * normed, axis=-1, keepdims=True)


LAGS = (0, 1, 3, 4, 5, 7, 11)
UNITS = 4
ORDER = (3, 2, 5, 4, 6, 1)
UNROLL_BACK = 3


def layer_kernel(len_ref, tok_h, cot_h, w_h, wo_h, wu_h, wd_h, qvb_h, bo_h, g1_h, s1_h, bu_h, bd_h, g2_h, s2_h,
                 out_h, od_hbm, ou_hbm, oo_hbm, oq_hbm, din_hbm, so_hbm,
                 a_buf, b_buf, dtok, toks, k, v, q, pr, wp, ctx, low1, dffn, datt, dq, wo, dsum, first, normed1,
                 scale1, part, part2, part_up, qvb_ref, bo_v, g1_v, s1_v, bu_v, bd_v, g2_v, s2_v,
                 g, r1, r2, r3, r4, sbuf, srecv, so_v, x1, x2,
                 ls, cs, cr, ys, yr, fs, fr,
                 s1, q1, s2, q2, s3, q3, s4, q4, s5, q5, s6, q6, os_, ss, sq, xs):
    pieces, _, _, R, C = g.shape
    seqs, quarter, d = q.shape
    rows, keys, pairs = seqs * quarter, 4 * quarter, d // PAIR
    ff = wu_h.shape[1]
    nd = nu = ff // d
    h = R // 2
    hr, hc = h // 2, C // 2
    w, n = lax.axis_index("wide"), lax.axis_index("narrow")
    c, y, x, z = n % 2, n // 2, w % 2, (w // 2) % 4
    core_n, y_n = n + 1 - 2 * c, n + 2 - 4 * y
    far_n = core_n + 2 - 4 * y
    core_peer, y_peer, x_peer = (w, core_n), (w, y_n), (w + 1 - 2 * x, n)
    zs = [z + 1 - 2 * (z % 2), z + 2 - 4 * (z // 2), 3 - z]
    z_peers = [(w + 2 * (j - z), n) for j in zs]
    gp = g.reshape(pieces, d, d)
    a_view, b_view = a_buf.reshape(nd, rows, d), b_buf.reshape(nu, rows, d)
    dk, dv = a_buf.reshape(seqs, keys, d), b_buf.reshape(seqs, keys, d)
    slope = dtok.reshape(nd, rows, d)
    tok = datt.reshape(seqs, quarter, d)
    dctx = low1.reshape(seqs, quarter, d)
    out = dq.reshape(rows, d)
    cot = dffn.reshape(seqs, quarter, d)
    toks3, k3, v3 = (r.reshape(seqs, keys, d) for r in (toks, k, v))
    blocks = lambda ref, i: ref.at[:, i * d:(i + 1) * d]
    moves = [(tok_h, tok)] + [(blocks(w_h, i), gp.at[i]) for i in range(3)] + [
        (qvb_h, qvb_ref), (bo_h, bo_v), (g1_h, g1_v), (s1_h, s1_v), (bu_h, bu_v), (bd_h, bd_v), (g2_h, g2_v),
        (s2_h, s2_v), (wo_h, wo)] + [(blocks(wu_h, i), gp.at[nd + i]) for i in range(nu)] + [(cot_h, cot)] + [
        (wd_h.at[pl.ds(i * d, d)], gp.at[nd + nu + i]) for i in range(nd)]
    loads = [pltpu.make_async_copy(s, t, ls.at[i]) for i, (s, t) in enumerate(moves)]
    for cp in loads[:4]:
        cp.start()
    bar = pltpu.get_barrier_semaphore()
    for dev in [core_peer, y_peer, x_peer] + z_peers:
        pl.semaphore_signal(bar, inc=1, device_id=dev, device_id_type=MESH)
    pl.semaphore_wait(bar, 6)

    def send_y(s):
        return copy_to(tok_h.at[s], toks.at[s, n], ys.at[s], yr.at[s], y_peer)

    def send_core(s):
        return copy_to(tok_h.at[s], toks.at[s, n], cs.at[s], cr.at[s], core_peer)

    def forward_y(s):
        return copy_to(toks.at[s, y_n], toks.at[s, y_n], fs.at[s], fr.at[s], core_peer)

    for s in range(seqs):
        send_y(s).start()
        send_core(s).start()
    for cp in loads[4:]:
        cp.start()
    loads[0].wait()
    for s in range(seqs):
        toks[s, n] = tok[s]
    for cp in loads[1:4]:
        cp.wait()
    left = left_lanes(d)
    for p in range(pairs):
        t0, t1, t2 = (gp[p // 2, :, pl.ds((p % 2 * 3 + i) * PAIR, PAIR)].astype(F32) for i in range(3))
        cols = pl.ds(p * PAIR, PAIR)
        wp[0, :, cols] = jnp.where(left, t0, t1).astype(BF)
        wp[1, :, cols] = pltpu.roll(jnp.where(left, t2, t0), HD, 1).astype(BF)
        wp[2, :, cols] = jnp.where(left, t1, t2).astype(BF)
    for cp in loads[4:12]:
        cp.wait()
    bo_ref, g1_ref, s1_ref, bd_ref, g2_ref, s2_ref = (
        r[...].reshape(1, d) for r in (bo_v, g1_v, s1_v, bd_v, g2_v, s2_v))
    own = tok[...].reshape(rows, d)
    q[...] = ((dg(own, wp[0], 1, 0) + qvb_ref[0:1, :]).astype(BF) * 0.125).reshape(seqs, quarter, d)

    def project(s, half):
        blocks = pl.ds(2 * half, 2)
        x = toks[s, blocks].reshape(2 * quarter, d)
        k[s, blocks] = dg(x, wp[1], 1, 0).astype(BF).reshape(2, quarter, d)
        v[s, blocks] = (dg(x, wp[2], 1, 0) + qvb_ref[1:2, :]).astype(BF).reshape(2, quarter, d)

    for s in range(seqs):
        send_core(s).wait_recv()
    for s in range(seqs):
        project(s, y)

    def fetch_far(s):
        copy_to(toks.at[s, y_n], toks.at[s, y_n], ys.at[s], yr.at[s], y_peer).wait_recv()
        forward_y(s).start()

    fetch_far(0)
    for s in range(seqs):
        copy_to(toks.at[s, far_n], toks.at[s, far_n], fs.at[s], fr.at[s], core_peer).wait_recv()
        project(s, 1 - y)
        if s + 1 < seqs:
            fetch_far(s + 1)
        live = lax.broadcasted_iota(jnp.int32, (keys, 2 * quarter), 0) < len_ref[s]

        def unit(p, carry):
            cols = pl.ds(pl.multiple_of(p * PAIR, PAIR), PAIR)
            qs = stack_heads(q[s, :, cols])
            kp = k[s, :, :, cols].reshape(keys, PAIR)
            vp = v[s, :, :, cols].reshape(keys, PAIR)
            scores = jnp.where(live, dg(kp, qs, 1, 1), -1000000000.0)
            e = jnp.exp(scores - jnp.max(scores, axis=0, keepdims=True))
            probs = (e * (1.0 / jnp.sum(e, axis=0, keepdims=True))).astype(BF)
            pr[s, p] = probs
            ctx[s * quarter:(s + 1) * quarter, cols] = unstack_heads(dg(vp, probs, 0, 0)).astype(BF)
            return carry

        lax.fori_loop(0, pairs, unit, 0, unroll=UNROLL_ATT)

    part2[...] = jnp.zeros_like(part2)
    chunk = 64
    chunks = rows // chunk
    loads[12].wait()
    for b in range(d // 256):
        cols = pl.ds(b * 256, 256)
        dsum[:, cols] = (dg(ctx[...], wo[:, cols], 1, 0) + bo_ref[:, b * 256:(b + 1) * 256]
                        + tok[:, :, cols].reshape(rows, 256).astype(F32))

    def norm1(i, carry):
        r = pl.ds(pl.multiple_of(i * chunk, chunk), chunk)
        normed, scale = center_scale(dsum[r])
        x = normed * g1_ref + s1_ref
        normed1[r] = normed
        scale1[r] = jnp.broadcast_to(scale, (chunk, 128))
        first[r] = x
        low1[r] = x.astype(BF)
        return carry

    lax.fori_loop(0, chunks, norm1, 0)
    for cp in loads[13:13 + nu]:
        cp.wait()

    def up(j, carry):
        cols = pl.ds(pl.multiple_of(j * 256, 256), 256)
        at = (j // 3, slice(None), pl.ds(pl.multiple_of(j % 3 * 256, 256), 256))
        pre = dg(low1[...], gp[(nd + at[0],) + at[1:]], 1, 0) + bu_v[cols].reshape(1, 256)
        half = 0.5 + 0.5 * lax.erf(pre * root_half)
        a_view[at] = (pre * half).astype(BF)
        slope[at] = (half + pre * (jnp.exp(-0.5 * pre * pre) * inv_root_two_pi)).astype(BF)
        return carry

    lax.fori_loop(0, ff // 256, up, 0, unroll=UNROLL_UP)
    for cp in loads[13 + nu:]:
        cp.wait()
    for b in range(d // 256):
        cols = pl.ds(b * 256, 256)
        dsum[:, cols] = bd_ref[:, b * 256:(b + 1) * 256] + first[:, cols] + sum(
            dg(a_view[i], gp[nd + nu + i, :, cols], 1, 0) for i in range(ff // d))

    def norm2(i, carry):
        r = pl.ds(pl.multiple_of(i * chunk, chunk), chunk)
        normed, scale = center_scale(dsum[r])
        out[r] = (normed * g2_ref + s2_ref).astype(BF)
        s = i * chunk // quarter
        off = pl.multiple_of(i * chunk - s * quarter, chunk)
        pos = n * quarter + off + lax.broadcasted_iota(jnp.int32, (chunk, d), 0)
        d_out = jnp.where(pos < len_ref[s], cot[s, pl.ds(off, chunk)].astype(F32), 0.0)
        part2[1] += fold(d_out * normed)
        part2[2] += fold(d_out)
        d_second = scale * norm_grad(d_out * g2_ref, normed)
        dsum[r] = d_second
        low = d_second.astype(BF)
        dffn[r] = low
        part2[0] += fold(low.astype(F32))
        return carry

    lax.fori_loop(0, chunks, norm2, 0)
    out_store = pltpu.make_async_copy(out, out_h, xs.at[5])
    out_store.start()

    def cut(j):
        return (pl.ds(pl.multiple_of(x * h + (j // 2) * hr, 16), hr), pl.ds(pl.multiple_of((j % 2) * hc, 128), hc))

    near = pl.ds(pl.multiple_of(x * h, 16), h)
    away = pl.ds(pl.multiple_of((1 - x) * h, 16), h)

    def c1(p):
        return copy_to(g.at[p, 1 - c], r1.at[p], s1.at[p], q1.at[p], core_peer)

    def c2(p):
        return copy_to(g.at[p, c, 1 - y], r2.at[p], s2.at[p], q2.at[p], y_peer)

    def c3(p):
        return copy_to(g.at[p, c, y, away], r3.at[p], s3.at[p], q3.at[p], x_peer)

    def c4(p, e):
        rr, cc = cut(zs[e])
        return copy_to(g.at[p, c, y, rr, cc], r4.at[p, e], s4.at[p, e], q4.at[p, e], z_peers[e])

    def c5(p, e, j):
        rr, cc = cut(j)
        return copy_to(r1.at[p, 0, rr, cc], r1.at[p, 0, rr, cc], s5.at[p, e], q5.at[p, e], z_peers[e])

    def c6(p, rr):
        return copy_to(r1.at[p, 0, rr], r1.at[p, 0, rr], s6.at[p], q6.at[p], x_peer)

    def store(p, dst):
        return pltpu.make_async_copy(r1.at[p, 0], dst, os_.at[p])

    def st1(p):
        c1(p).wait_recv()
        g[p, c] = (g[p, c].astype(F32) + r1[p].astype(F32)).astype(BF)
        c2(p).start()

    def st2(p):
        c2(p).wait_recv()
        g[p, c, y] = (g[p, c, y].astype(F32) + r2[p].astype(F32)).astype(BF)
        c3(p).start()

    def st3(p):
        c3(p).wait_recv()
        g[p, c, y, near] = (g[p, c, y, near].astype(F32) + r3[p].astype(F32)).astype(BF)
        for e in (1, 2, 0):
            c4(p, e).start()

    def st4(p):
        for e in range(3):
            c4(p, e).wait_recv()
        rr, cc = cut(z)
        t = g[p, c, y, rr, cc].astype(F32) + r4[p, 0].astype(F32) + r4[p, 1].astype(F32) + r4[p, 2].astype(F32)
        r1[p, 0, rr, cc] = t.astype(BF)
        for e in (1, 2, 0):
            c5(p, e, z).start()

    def st5(p):
        for e in range(3):
            c5(p, e, zs[e]).wait_recv()
        c6(p, near).start()

    def st6(p):
        c6(p, away).wait_recv()

        @pl.when(p < nd)
        def down():
            store(p, od_hbm.at[pl.ds(p * R, R)]).start()

        @pl.when(jnp.logical_and(p >= nd, p < nd + nu))
        def up():
            store(p, ou_hbm.at[:, pl.ds(pl.multiple_of((p - nd) * C, C), C)]).start()

        @pl.when(p == nd + nu)
        def out():
            store(p, oo_hbm).start()

        @pl.when(p > nd + nu)
        def qkv():
            store(p, oq_hbm.at[:, pl.ds(pl.multiple_of((p - nd - nu - 1) * C, C), C)]).start()

    stages = [None, st1, st2, st3, st4, st5, st6]

    block = 256
    for a in range(d // block):
        def down_block(i, carry):
            t = dg(a_view[i, :, a * block:(a + 1) * block], dffn[...], 0, 0).astype(BF)
            for j in range(nd):
                lo, hi = max(j * R, a * block), min((j + 1) * R, (a + 1) * block)
                if lo < hi:
                    g[j, i % 2, i // 2, lo - j * R:hi - j * R] = t[lo - a * block:hi - a * block]
            return carry

        lax.fori_loop(0, nd, down_block, 0)
        for p in range(a * block // R, nd if a == d // block - 1 else (a + 1) * block // R):
            c1(p).start()
        if a == 1:
            st1(0)
    st1(1)

    def up_back(j, carry):
        at = (j // 3, slice(None), pl.ds(pl.multiple_of(j % 3 * 256, 256), 256))
        low = (dg(dffn[...], gp[nd + nu + j // 3, pl.ds(pl.multiple_of(j % 3 * 256, 256), 256)], 1, 1) * slope[at].astype(F32)).astype(BF)
        b_view[at] = low
        part_up[:, pl.ds(pl.multiple_of(j * 256, 256), 256)] = fold(low.astype(F32))
        return carry

    lax.fori_loop(0, ff // 256, up_back, 0, unroll=UNROLL_BACK)
    for b in range(d // 256):
        cols = pl.ds(b * 256, 256)
        dsum[:, cols] += sum(dg(b_view[i], gp[nd + i, cols, :], 1, 1) for i in range(nu))

    def row_block(p, t):
        for j in range(4):
            g[p, j % 2, j // 2] = t[j * R:(j + 1) * R].astype(BF)

    def up_block(i, carry):
        row_block(nd + i, dg(low1[...], b_view[i], 0, 0))
        c1(nd + i).start()
        return carry

    lax.fori_loop(0, nu, up_block, 0)

    def rows_back():
        part[...] = jnp.zeros_like(part)
        chunk = 64
        gain = g1_v[...].reshape(1, d)

        def norm1_back(i, carry):
            r = pl.ds(pl.multiple_of(i * chunk, chunk), chunk)
            d_first, normed = dsum[r], normed1[r]
            part[1] += fold(d_first * normed)
            part[2] += fold(d_first)
            d_sum = scale1[r, :1] * norm_grad(d_first * gain, normed)
            dsum[r] = d_sum
            low = d_sum.astype(BF)
            datt[r] = low
            part[0] += fold(low.astype(F32))
            return carry

        lax.fori_loop(0, rows // chunk, norm1_back, 0)
        row_block(nd + nu, dg(ctx[...], datt[...], 0, 0))
        c1(nd + nu).start()
        dctx[...] = dg(datt[...], wo[...], 1, 1).astype(BF).reshape(seqs, quarter, d)
        out_store.wait()

    def unit(u, carry):
        s, p = u // pairs, u % pairs
        cols = pl.ds(pl.multiple_of(p * PAIR, PAIR), PAIR)
        qs = stack_heads(q[s, :, cols])
        ds = stack_heads(dctx[s, :, cols])
        low = pr[s, p]
        probs = low.astype(F32)
        t = probs * dg(v3[s, :, cols], ds, 1, 1)
        d_raw = (t - probs * jnp.sum(t, axis=0, keepdims=True)).astype(BF)
        dv[s, :, cols] = dg(low, ds, 1, 0).astype(BF)
        dk[s, :, cols] = dg(d_raw, qs, 1, 0).astype(BF)
        dq[s, :, cols] = (unstack_heads(dg(k3[s, :, cols], d_raw, 0, 0)) * 0.125).astype(BF)
        return carry

    def qkv_piece(i):
        cols = pl.ds(i * 2 * PAIR, 2 * PAIR)
        allt = toks3[...].reshape(seqs * keys, d)
        ga = dg(toks3[:, pl.ds(pl.multiple_of(n * quarter, quarter), quarter)].reshape(rows, d), dq[:, :, cols].reshape(rows, 2 * PAIR), 0, 0)
        gb = dg(allt, a_buf[:, cols], 0, 0)
        gc = dg(allt, b_buf[:, cols], 0, 0)
        left = left_lanes(R)
        p = nd + nu + 1 + i
        for e in range(4):
            rr = slice(e * R, (e + 1) * R)
            for j in range(2):
                sl = slice(j * PAIR, (j + 1) * PAIR)
                aj, bj, cj = ga[rr, sl], pltpu.roll(gb[rr, sl], HD, 1), gc[rr, sl]
                for t, val in enumerate((jnp.where(left, aj, bj), jnp.where(left, cj, aj), jnp.where(left, bj, cj))):
                    g[p, e % 2, e // 2, :, pl.ds((3 * j + t) * PAIR, PAIR)] = val.astype(BF)
        c1(p).start()

    cx1 = copy_to(dtok.at[:, 1 - c], x1, xs.at[0], xs.at[1], core_peer)
    cx2 = copy_to(dtok.at[1 - y, c], x2, xs.at[2], xs.at[3], y_peer)

    def input_part():
        def one(s, carry):
            t = dg(dk[s], wp[1], 1, 1) + dg(dv[s], wp[2], 1, 1)
            for e in range(4):
                dtok[e // 2, e % 2, s] = t[e * quarter:(e + 1) * quarter].astype(BF)
            return carry

        lax.fori_loop(0, seqs, one, 0)
        cx1.start()
        dsum[...] += dg(dq[...].reshape(rows, d), wp[0], 1, 1)

    def small(i, slot, dev):
        return copy_to(sbuf.at[i], srecv.at[slot], ss.at[slot], sq.at[slot], dev)

    def sums0():
        sbuf[0, 0:1] = jnp.sum(fold(dq[...].reshape(rows, d).astype(F32)), axis=0, keepdims=True)

        def add(s, acc):
            return acc + fold(dv[s].astype(F32))

        acc = lax.fori_loop(0, seqs, add, jnp.zeros((8, d), F32))
        sbuf[0, 1:2] = jnp.sum(acc, axis=0, keepdims=True)
        for i in range(3):
            sbuf[0, 2 + i:3 + i] = total(part[i])
        for i in range(nu):
            sbuf[0, 5 + i:6 + i] = total(part_up[:, i * d:(i + 1) * d])
        for i in range(3):
            sbuf[0, 5 + nu + i:6 + nu + i] = total(part2[i])
        small(0, 0, core_peer).start()

    def sums1():
        small(0, 0, core_peer).wait_recv()
        sbuf[1] = sbuf[0] + srecv[0]
        small(1, 1, y_peer).start()

    def sums2():
        small(1, 1, y_peer).wait_recv()
        sbuf[2] = sbuf[1] + srecv[1]
        small(2, 2, x_peer).start()

    def sums3():
        small(2, 2, x_peer).wait_recv()
        sbuf[3] = sbuf[2] + srecv[2]
        for e in range(3):
            small(3, 3 + e, z_peers[e]).start()

    so_store = pltpu.make_async_copy(so_v, so_hbm, xs.at[6])

    def sums4():
        for e in range(3):
            small(3, 3 + e, z_peers[e]).wait_recv()
        so_v[...] = sbuf[3] + srecv[3] + srecv[4] + srecv[5]
        so_store.start()

    def add_x1():
        cx1.wait_recv()

        def add(i, carry):
            a, b = i // seqs, i % seqs
            dtok[a, c, b] = (dtok[a, c, b].astype(F32) + x1[a, b].astype(F32)).astype(BF)
            return carry

        lax.fori_loop(0, 2 * seqs, add, 0)

    din_out = pltpu.make_async_copy(x1.at[0], din_hbm, xs.at[4])

    def input_out():
        cx2.wait_recv()

        def out_x(i, carry):
            r = pl.ds(pl.multiple_of(i * quarter, quarter), quarter)
            x1[0, i] = (dsum[r] + dtok[y, c, i].astype(F32) + x2[i].astype(F32)).astype(BF)
            return carry

        lax.fori_loop(0, seqs, out_x, 0)
        din_out.start()

    units = seqs * pairs
    slots_of_units = -(-units // UNITS)
    extra = {3: [rows_back], 9: [lambda: qkv_piece(0)], 10: [lambda: qkv_piece(1), lambda: qkv_piece(2), sums0],
             11: [input_part, sums1], 12: [add_x1, sums2], 13: [cx2.start, sums3], 16: [sums4], 21: [input_out]}

    def drain(p):
        c1(p).wait_send()
        c2(p).wait_send()
        c3(p).wait_send()
        c6(p, near).wait_send()
        for e in range(3):
            c4(p, e).wait_send()
            c5(p, e, z).wait_send()

    def slot(t, carry):
        for i in ORDER:
            p = t - LAGS[i]

            @pl.when(jnp.logical_and(p >= 0, p < pieces))
            def run():
                stages[i](p)

        @pl.when(jnp.logical_and(t > 3, t <= 3 + slots_of_units))
        def attention():
            lo = (t - 4) * UNITS
            lax.fori_loop(lo, jnp.minimum(lo + UNITS, units), unit, 0)

        for at, todo in extra.items():
            @pl.when(t == at)
            def more():
                for f in todo:
                    f()

        old = t - LAGS[5] - 3

        @pl.when(jnp.logical_and(old >= 0, old < pieces))
        def finished():
            drain(old)
        return carry

    lax.fori_loop(3, pieces + LAGS[6], slot, 0)
    small(0, 0, core_peer).wait_send()
    small(1, 1, y_peer).wait_send()
    small(2, 2, x_peer).wait_send()
    for e in range(3):
        small(3, 3 + e, z_peers[e]).wait_send()
    cx1.wait_send()
    cx2.wait_send()

    def stored(p, carry):
        store(p, oo_hbm).wait()
        return carry

    lax.fori_loop(0, pieces, stored, 0)
    for s in range(seqs):
        send_y(s).wait_send()
        send_core(s).wait_send()
        forward_y(s).wait_send()
    din_out.wait()
    so_store.wait()


def layer_part(tokens, lengths, w, qvb, wo, bo, g1, s1, wu, bu, wd, bd, g2, s2, cot):
    seqs, quarter, d = tokens.shape
    rows, keys, pairs, ff = seqs * quarter, 4 * quarter, d // PAIR, wu.shape[1]
    R = d // 4
    nd = nu = ff // d
    n = nd + nu + 4
    h = R // 2
    all_rows = (8 + nu, d)
    vm, hbm = pl.BlockSpec(memory_space=V), pl.BlockSpec(memory_space=ANY)
    S = jax.ShapeDtypeStruct
    own, every, flat = (seqs, quarter, d), (seqs, 4, quarter, d), (rows, d)
    row = V((d,), F32)
    return pl.pallas_call(
        layer_kernel,
        out_shape=(S(flat, BF), S((nd * R, d), BF), S((R, nu * d), BF), S((R, d), BF), S((R, 3 * d), BF), S(own, BF),
                   S(all_rows, F32)),
        in_specs=[pl.BlockSpec(memory_space=pltpu.SMEM)] + [hbm] * 14,
        out_specs=[hbm] * 7,
        scratch_shapes=[V((seqs * keys, d), BF), V((seqs * keys, d), BF), V((2, 2) + own, BF), V(every, BF), V(every, BF),
                        V(every, BF), V(own, BF), V((seqs, pairs, keys, 2 * quarter), BF), V((3, d, d), BF),
                        V(flat, BF), V(flat, BF), V(flat, BF), V(flat, BF), V(own, BF), V(wo.shape, BF),
                        V(flat, F32), V(flat, F32), V(flat, F32), V((rows, 128), F32), V((3, 8, d), F32),
                        V((3, 8, d), F32), V((8, ff), F32), V((2, d), F32), row, row, row, V((ff,), F32), row, row, row,
                        V((n, 2, 2, R, d), BF), V((n, 2, R, d), BF), V((n, R, d), BF), V((n, h, d), BF),
                        V((n, 3, h // 2, d // 2), BF), V((4,) + all_rows, F32), V((6,) + all_rows, F32),
                        V(all_rows, F32), V((2,) + own, BF), V(own, BF), DMA((14 + nd + nu,))]
        + [DMA((seqs,))] * 6 + [DMA((n,))] * 6 + [DMA((n, 3))] * 4 + [DMA((n,))] * 3
        + [DMA((6,))] * 2 + [DMA((7,))],
        name="layer_part",
        compiler_params=pltpu.CompilerParams(collective_id=1, has_side_effects=True, vmem_limit_bytes=63 << 20),
    )(lengths, tokens, cot, w, wo, wu, wd, qvb, bo, g1, s1, bu, bd, g2, s2)


def finish_kernel(d_h, u_h, o_h, q_h, out_h, din_h, sums_h, fd, fu, fo, fq, fout, fdin,
                  qvb_h, outb_h, n1g_h, n1s_h, upb_h, downb_h, n2g_h, n2s_h,
                  low, full, rows, sums_ref, qvb, outb, n1g, n1s, upb, downb, n2g, n2s, ls, os_, ms):
    R, C = low.shape[1:]
    nd, nu = d_h.shape[0] // R, u_h.shape[1] // C
    cut = lambda ref, i: ref.at[:, pl.ds(i * C, C)]
    ends = ([(d_h.at[pl.ds(i * R, R)], fd.at[pl.ds(i * R, R)]) for i in range(nd)]
            + [(cut(u_h, i), cut(fu, i)) for i in range(nu)] + [(o_h, fo)]
            + [(cut(q_h, i), cut(fq, i)) for i in range(3)])
    loads = [pltpu.make_async_copy(s, low.at[i], ls.at[i]) for i, (s, _) in enumerate(ends)]
    stores = [pltpu.make_async_copy(full.at[i], t, os_.at[i]) for i, (_, t) in enumerate(ends)]
    pieces = len(ends)
    loads += [pltpu.make_async_copy(s, rows.at[i], ls.at[pieces + i]) for i, s in enumerate((out_h, din_h))]
    stores += [pltpu.make_async_copy(rows.at[i], t, os_.at[pieces + i]) for i, t in enumerate((fout, fdin))]
    sums_load = pltpu.make_async_copy(sums_h, sums_ref, ms.at[8])
    sums_load.start()
    for cp in loads:
        cp.start()
    small = [pltpu.make_async_copy(s, t, ms.at[i]) for i, (s, t) in enumerate(
        ((qvb, qvb_h), (outb, outb_h), (n1g, n1g_h), (n1s, n1s_h), (upb, upb_h), (downb, downb_h), (n2g, n2g_h),
         (n2s, n2s_h)))]
    sums_load.wait()
    n = lax.axis_index("narrow")
    for i in range(4):
        @pl.when(n == i)
        def pick():
            at = slice(i * R, (i + 1) * R)
            qvb[...] = sums_ref[0:2, at]
            for j, ref in ((2, outb), (3, n1g), (4, n1s), (5 + nu, downb), (6 + nu, n2g), (7 + nu, n2s)):
                ref[...] = sums_ref[j, at]
            upb[...] = sums_ref[5 + i]
    for cp in small:
        cp.start()
    for i, (a, b) in enumerate(zip(loads, stores)):
        a.wait()
        if i < pieces:
            full[i] = low[i].astype(F32)
        b.start()
    for cp in stores + small:
        cp.wait()


def finish_part(down, up, out, qkv, output, input_grad, sums):
    R, d = out.shape
    n = down.shape[0] // R + up.shape[1] // d + 4
    vm, hbm = pl.BlockSpec(memory_space=V), pl.BlockSpec(memory_space=ANY)
    S = jax.ShapeDtypeStruct
    shapes = [S(a.shape, F32) for a in (down, up, out, qkv)] + [S(output.shape, BF)] * 2 + [S((2, R), F32)] + [S((R,), F32)] * 3
    shapes += [S((d,), F32)] + [S((R,), F32)] * 3
    return pl.pallas_call(
        finish_kernel,
        out_shape=shapes,
        in_specs=[hbm] * 7,
        out_specs=[hbm] * 14,
        scratch_shapes=[V((n, R, d), BF), V((n, R, d), F32), V((2,) + output.shape, BF), V(sums.shape, F32)]
        + [V(a.shape, F32) for a in shapes[6:]] + [DMA((n + 2,)), DMA((n + 2,)), DMA((9,))],
        name="finish_part",
        compiler_params=pltpu.CompilerParams(vmem_limit_bytes=60 << 20),
    )(down, up, out, qkv, output, input_grad, sums)


def local(tokens, lengths, qkv_weight, qv_bias, out_weight, out_bias, norm1_gain, norm1_shift, up_weight, up_bias,
          down_weight, down_bias, norm2_gain, norm2_shift, cotangent):
    own = tokens.shape
    output, down, up, out, qkv, input_grad, sums = layer_part(
        tokens, lengths, qkv_weight, qv_bias, out_weight, out_bias, norm1_gain, norm1_shift, up_weight, up_bias,
        down_weight, down_bias, norm2_gain, norm2_shift, cotangent)
    wide = lax.axis_size("wide")
    if wide > 8:
        groups = [[j * 8 + i for j in range(wide // 8)] for i in range(8)]
        down, up, out, qkv = (
            lax.psum(a.astype(F32), "wide", axis_index_groups=groups).astype(BF) for a in (down, up, out, qkv))
        sums = lax.psum(sums, "wide", axis_index_groups=groups)
    down, up, out, qkv, output, input_grad, qvb, outb, n1g, n1s, upb, downb, n2g, n2s = finish_part(
        down, up, out, qkv, output, input_grad.reshape(output.shape), sums)
    return (output.reshape(own), input_grad.reshape(own), qkv, qvb, out, outb, n1g, n1s, up, upb, down, downb, n2g, n2s)


def solution(mesh):
    return jax.shard_map(
        local,
        mesh=mesh,
        in_specs=(
            P("wide", "narrow", None),
            P("wide"),
            P(),
            P(),
            P(),
            P(),
            P(),
            P(),
            P(),
            P(),
            P(),
            P(),
            P(),
            P(),
            P("wide", "narrow", None),
        ),
        out_specs=(
            P("wide", "narrow", None),
            P("wide", "narrow", None),
            P("narrow", None),
            P(None, "narrow"),
            P("narrow", None),
            P("narrow"),
            P("narrow"),
            P("narrow"),
            P("narrow", None),
            P("narrow"),
            P("narrow", None),
            P("narrow"),
            P("narrow"),
            P("narrow"),
        ),
        check_vma=False,
    )
```

```python
import functools

import jax
import jax.numpy as jnp
from jax import lax
from jax.experimental import pallas as pl
from jax.experimental.pallas import tpu as pltpu
from jax.sharding import PartitionSpec as P

H = 12
HD = 64
PAIR = 2 * HD
epsilon = 1e-12
root_half = 0.7071067811865476
inv_root_two_pi = 0.3989422804014327
MESH = pl.DeviceIdType.MESH
F32 = jnp.float32
BF = jnp.bfloat16
V = pltpu.VMEM
DMA = pltpu.SemaphoreType.DMA
ANY = pl.ANY
UNROLL_ATT = 3
UNROLL_UP = 6


def dg(a, b, ca, cb):
    return lax.dot_general(a, b, (((ca,), (cb,)), ((), ())), preferred_element_type=F32)


def copy_to(src, dst, ss, rs, dev):
    return pltpu.make_async_remote_copy(
        src_ref=src, dst_ref=dst, send_sem=ss, recv_sem=rs, device_id=dev, device_id_type=MESH)


def left_lanes(rows):
    return lax.broadcasted_iota(jnp.int32, (rows, PAIR), 1) < HD


def stack_heads(x):
    left = left_lanes(x.shape[0])
    zero = jnp.zeros_like(x)
    return jnp.concatenate([jnp.where(left, x, zero), jnp.where(left, zero, x)], axis=0)


def unstack_heads(x_t):
    q = x_t.shape[1] // 2
    top = lax.broadcasted_iota(jnp.int32, (PAIR, q), 0) < HD
    return jnp.where(top, x_t[:, :q], x_t[:, q:]).T


def fold(x):
    return jnp.sum(x.reshape(x.shape[0] // 8, 8, x.shape[1]), axis=0)


def total(x):
    return jnp.sum(x, axis=0, keepdims=True)


def center_scale(v):
    center = v - jnp.mean(v, axis=-1, keepdims=True)
    scale = lax.rsqrt(jnp.mean(center * center, axis=-1, keepdims=True) + epsilon)
    return center * scale, scale


def norm_grad(g, normed):
    return g - jnp.mean(g, axis=-1, keepdims=True) - normed * jnp.mean(g * normed, axis=-1, keepdims=True)


LAGS = (0, 1, 3, 4, 5, 7, 11)
UNITS = 4
ORDER = (3, 2, 5, 4, 6, 1)
UNROLL_BACK = 3


def layer_kernel(len_ref, tok_h, cot_h, w_h, wo_h, wu_h, wd_h, qvb_h, bo_h, g1_h, s1_h, bu_h, bd_h, g2_h, s2_h,
                 out_h, od_hbm, ou_hbm, oo_hbm, oq_hbm, din_hbm, so_hbm,
                 a_buf, b_buf, dtok, toks, k, v, q, pr, wp, ctx, low1, dffn, datt, dq, wo, dsum, first, normed1,
                 scale1, part, part2, part_up, qvb_ref, bo_v, g1_v, s1_v, bu_v, bd_v, g2_v, s2_v,
                 g, r1, r2, r3, r4, sbuf, srecv, so_v, x1, x2,
                 ls, cs, cr, ys, yr, fs, fr,
                 s1, q1, s2, q2, s3, q3, s4, q4, s5, q5, s6, q6, os_, ss, sq, xs):
    pieces, _, _, R, C = g.shape
    seqs, quarter, d = q.shape
    rows, keys, pairs = seqs * quarter, 4 * quarter, d // PAIR
    ff = wu_h.shape[1]
    nd = nu = ff // d
    h = R // 2
    hr, hc = h // 2, C // 2
    w, n = lax.axis_index("wide"), lax.axis_index("narrow")
    c, y, x, z = n % 2, n // 2, w % 2, (w // 2) % 4
    core_n, y_n = n + 1 - 2 * c, n + 2 - 4 * y
    far_n = core_n + 2 - 4 * y
    core_peer, y_peer, x_peer = (w, core_n), (w, y_n), (w + 1 - 2 * x, n)
    zs = [z + 1 - 2 * (z % 2), z + 2 - 4 * (z // 2), 3 - z]
    z_peers = [(w + 2 * (j - z), n) for j in zs]
    gp = g.reshape(pieces, d, d)
    a_view, b_view = a_buf.reshape(nd, rows, d), b_buf.reshape(nu, rows, d)
    dk, dv = a_buf.reshape(seqs, keys, d), b_buf.reshape(seqs, keys, d)
    slope = dtok.reshape(nd, rows, d)
    tok = datt.reshape(seqs, quarter, d)
    dctx = low1.reshape(seqs, quarter, d)
    out = dq.reshape(rows, d)
    cot = dffn.reshape(seqs, quarter, d)
    toks3, k3, v3 = (r.reshape(seqs, keys, d) for r in (toks, k, v))
    blocks = lambda ref, i: ref.at[:, i * d:(i + 1) * d]
    moves = [(tok_h, tok)] + [(blocks(w_h, i), gp.at[i]) for i in range(3)] + [
        (qvb_h, qvb_ref), (bo_h, bo_v), (g1_h, g1_v), (s1_h, s1_v), (bu_h, bu_v), (bd_h, bd_v), (g2_h, g2_v),
        (s2_h, s2_v), (wo_h, wo)] + [(blocks(wu_h, i), gp.at[nd + i]) for i in range(nu)] + [(cot_h, cot)] + [
        (wd_h.at[pl.ds(i * d, d)], gp.at[nd + nu + i]) for i in range(nd)]
    loads = [pltpu.make_async_copy(s, t, ls.at[i]) for i, (s, t) in enumerate(moves)]
    for cp in loads[:4]:
        cp.start()
    bar = pltpu.get_barrier_semaphore()
    for dev in [core_peer, y_peer, x_peer] + z_peers:
        pl.semaphore_signal(bar, inc=1, device_id=dev, device_id_type=MESH)
    pl.semaphore_wait(bar, 6)

    def send_y(s):
        return copy_to(tok_h.at[s], toks.at[s, n], ys.at[s], yr.at[s], y_peer)

    def send_core(s):
        return copy_to(tok_h.at[s], toks.at[s, n], cs.at[s], cr.at[s], core_peer)

    def forward_y(s):
        return copy_to(toks.at[s, y_n], toks.at[s, y_n], fs.at[s], fr.at[s], core_peer)

    for s in range(seqs):
        send_y(s).start()
        send_core(s).start()
    for cp in loads[4:]:
        cp.start()
    loads[0].wait()
    for s in range(seqs):
        toks[s, n] = tok[s]
    for cp in loads[1:4]:
        cp.wait()
    left = left_lanes(d)
    for p in range(pairs):
        t0, t1, t2 = (gp[p // 2, :, pl.ds((p % 2 * 3 + i) * PAIR, PAIR)].astype(F32) for i in range(3))
        cols = pl.ds(p * PAIR, PAIR)
        wp[0, :, cols] = jnp.where(left, t0, t1).astype(BF)
        wp[1, :, cols] = pltpu.roll(jnp.where(left, t2, t0), HD, 1).astype(BF)
        wp[2, :, cols] = jnp.where(left, t1, t2).astype(BF)
    for cp in loads[4:12]:
        cp.wait()
    bo_ref, g1_ref, s1_ref, bd_ref, g2_ref, s2_ref = (
        r[...].reshape(1, d) for r in (bo_v, g1_v, s1_v, bd_v, g2_v, s2_v))
    own = tok[...].reshape(rows, d)
    q[...] = ((dg(own, wp[0], 1, 0) + qvb_ref[0:1, :]).astype(BF) * 0.125).reshape(seqs, quarter, d)

    def project(s, half):
        blocks = pl.ds(2 * half, 2)
        x = toks[s, blocks].reshape(2 * quarter, d)
        k[s, blocks] = dg(x, wp[1], 1, 0).astype(BF).reshape(2, quarter, d)
        v[s, blocks] = (dg(x, wp[2], 1, 0) + qvb_ref[1:2, :]).astype(BF).reshape(2, quarter, d)

    for s in range(seqs):
        send_core(s).wait_recv()
    for s in range(seqs):
        project(s, y)

    def fetch_far(s):
        copy_to(toks.at[s, y_n], toks.at[s, y_n], ys.at[s], yr.at[s], y_peer).wait_recv()
        forward_y(s).start()

    fetch_far(0)
    for s in range(seqs):
        copy_to(toks.at[s, far_n], toks.at[s, far_n], fs.at[s], fr.at[s], core_peer).wait_recv()
        project(s, 1 - y)
        live = lax.broadcasted_iota(jnp.int32, (keys, 2 * quarter), 0) < len_ref[s]

        def unit(p, carry):
            cols = pl.ds(pl.multiple_of(p * PAIR, PAIR), PAIR)
            qs = stack_heads(q[s, :, cols])
            kp = k[s, :, :, cols].reshape(keys, PAIR)
            vp = v[s, :, :, cols].reshape(keys, PAIR)
            scores = jnp.where(live, dg(kp, qs, 1, 1), -1000000000.0)
            e = jnp.exp(scores - jnp.max(scores, axis=0, keepdims=True))
            probs = (e * (1.0 / jnp.sum(e, axis=0, keepdims=True))).astype(BF)
            pr[s, p] = probs
            ctx[s * quarter:(s + 1) * quarter, cols] = unstack_heads(dg(vp, probs, 0, 0)).astype(BF)
            return carry

        lax.fori_loop(0, pairs // 2, unit, 0, unroll=UNROLL_ATT)
        if s + 1 < seqs:
            fetch_far(s + 1)
        lax.fori_loop(pairs // 2, pairs, unit, 0, unroll=UNROLL_ATT)

    part2[...] = jnp.zeros_like(part2)
    chunk = 64
    chunks = rows // chunk
    loads[12].wait()
    for b in range(d // 256):
        cols = pl.ds(b * 256, 256)
        dsum[:, cols] = (dg(ctx[...], wo[:, cols], 1, 0) + bo_ref[:, b * 256:(b + 1) * 256]
                        + tok[:, :, cols].reshape(rows, 256).astype(F32))

    def norm1(i, carry):
        r = pl.ds(pl.multiple_of(i * chunk, chunk), chunk)
        normed, scale = center_scale(dsum[r])
        x = normed * g1_ref + s1_ref
        normed1[r] = normed
        scale1[r] = jnp.broadcast_to(scale, (chunk, 128))
        first[r] = x
        low1[r] = x.astype(BF)
        return carry

    lax.fori_loop(0, chunks, norm1, 0)
    for cp in loads[13:13 + nu]:
        cp.wait()

    def up(j, carry):
        cols = pl.ds(pl.multiple_of(j * 256, 256), 256)
        at = (j // 3, slice(None), pl.ds(pl.multiple_of(j % 3 * 256, 256), 256))
        pre = dg(low1[...], gp[(nd + at[0],) + at[1:]], 1, 0) + bu_v[cols].reshape(1, 256)
        half = 0.5 + 0.5 * lax.erf(pre * root_half)
        a_view[at] = (pre * half).astype(BF)
        slope[at] = (half + pre * (jnp.exp(-0.5 * pre * pre) * inv_root_two_pi)).astype(BF)
        return carry

    lax.fori_loop(0, ff // 256, up, 0, unroll=UNROLL_UP)
    for cp in loads[13 + nu:]:
        cp.wait()
    for b in range(d // 256):
        cols = pl.ds(b * 256, 256)
        dsum[:, cols] = bd_ref[:, b * 256:(b + 1) * 256] + first[:, cols] + sum(
            dg(a_view[i], gp[nd + nu + i, :, cols], 1, 0) for i in range(ff // d))

    def norm2(i, carry):
        r = pl.ds(pl.multiple_of(i * chunk, chunk), chunk)
        normed, scale = center_scale(dsum[r])
        out[r] = (normed * g2_ref + s2_ref).astype(BF)
        s = i * chunk // quarter
        off = pl.multiple_of(i * chunk - s * quarter, chunk)
        pos = n * quarter + off + lax.broadcasted_iota(jnp.int32, (chunk, d), 0)
        d_out = jnp.where(pos < len_ref[s], cot[s, pl.ds(off, chunk)].astype(F32), 0.0)
        part2[1] += fold(d_out * normed)
        part2[2] += fold(d_out)
        d_second = scale * norm_grad(d_out * g2_ref, normed)
        dsum[r] = d_second
        low = d_second.astype(BF)
        dffn[r] = low
        part2[0] += fold(low.astype(F32))
        return carry

    lax.fori_loop(0, chunks, norm2, 0)
    out_store = pltpu.make_async_copy(out, out_h, xs.at[5])
    out_store.start()

    def cut(j):
        return (pl.ds(pl.multiple_of(x * h + (j // 2) * hr, 16), hr), pl.ds(pl.multiple_of((j % 2) * hc, 128), hc))

    near = pl.ds(pl.multiple_of(x * h, 16), h)
    away = pl.ds(pl.multiple_of((1 - x) * h, 16), h)

    def c1(p):
        return copy_to(g.at[p, 1 - c], r1.at[p], s1.at[p], q1.at[p], core_peer)

    def c2(p):
        return copy_to(g.at[p, c, 1 - y], r2.at[p], s2.at[p], q2.at[p], y_peer)

    def c3(p):
        return copy_to(g.at[p, c, y, away], r3.at[p], s3.at[p], q3.at[p], x_peer)

    def c4(p, e):
        rr, cc = cut(zs[e])
        return copy_to(g.at[p, c, y, rr, cc], r4.at[p, e], s4.at[p, e], q4.at[p, e], z_peers[e])

    def c5(p, e, j):
        rr, cc = cut(j)
        return copy_to(r1.at[p, 0, rr, cc], r1.at[p, 0, rr, cc], s5.at[p, e], q5.at[p, e], z_peers[e])

    def c6(p, rr):
        return copy_to(r1.at[p, 0, rr], r1.at[p, 0, rr], s6.at[p], q6.at[p], x_peer)

    def store(p, dst):
        return pltpu.make_async_copy(r1.at[p, 0], dst, os_.at[p])

    def st1(p):
        c1(p).wait_recv()
        g[p, c] = (g[p, c].astype(F32) + r1[p].astype(F32)).astype(BF)
        c2(p).start()

    def st2(p):
        c2(p).wait_recv()
        g[p, c, y] = (g[p, c, y].astype(F32) + r2[p].astype(F32)).astype(BF)
        c3(p).start()

    def st3(p):
        c3(p).wait_recv()
        g[p, c, y, near] = (g[p, c, y, near].astype(F32) + r3[p].astype(F32)).astype(BF)
        for e in (1, 2, 0):
            c4(p, e).start()

    def st4(p):
        for e in range(3):
            c4(p, e).wait_recv()
        rr, cc = cut(z)
        t = g[p, c, y, rr, cc].astype(F32) + r4[p, 0].astype(F32) + r4[p, 1].astype(F32) + r4[p, 2].astype(F32)
        r1[p, 0, rr, cc] = t.astype(BF)
        for e in (1, 2, 0):
            c5(p, e, z).start()

    def st5(p):
        for e in range(3):
            c5(p, e, zs[e]).wait_recv()
        c6(p, near).start()

    def st6(p):
        c6(p, away).wait_recv()

        @pl.when(p < nd)
        def down():
            store(p, od_hbm.at[pl.ds(p * R, R)]).start()

        @pl.when(jnp.logical_and(p >= nd, p < nd + nu))
        def up():
            store(p, ou_hbm.at[:, pl.ds(pl.multiple_of((p - nd) * C, C), C)]).start()

        @pl.when(p == nd + nu)
        def out():
            store(p, oo_hbm).start()

        @pl.when(p > nd + nu)
        def qkv():
            store(p, oq_hbm.at[:, pl.ds(pl.multiple_of((p - nd - nu - 1) * C, C), C)]).start()

    stages = [None, st1, st2, st3, st4, st5, st6]

    block = 256
    for a in range(d // block):
        def down_block(i, carry):
            t = dg(a_view[i, :, a * block:(a + 1) * block], dffn[...], 0, 0).astype(BF)
            for j in range(nd):
                lo, hi = max(j * R, a * block), min((j + 1) * R, (a + 1) * block)
                if lo < hi:
                    g[j, i % 2, i // 2, lo - j * R:hi - j * R] = t[lo - a * block:hi - a * block]
            return carry

        lax.fori_loop(0, nd, down_block, 0)
        for p in range(a * block // R, nd if a == d // block - 1 else (a + 1) * block // R):
            c1(p).start()
        if a == 1:
            st1(0)
    st1(1)

    def up_back(j, carry):
        at = (j // 3, slice(None), pl.ds(pl.multiple_of(j % 3 * 256, 256), 256))
        low = (dg(dffn[...], gp[nd + nu + j // 3, pl.ds(pl.multiple_of(j % 3 * 256, 256), 256)], 1, 1) * slope[at].astype(F32)).astype(BF)
        b_view[at] = low
        part_up[:, pl.ds(pl.multiple_of(j * 256, 256), 256)] = fold(low.astype(F32))
        return carry

    lax.fori_loop(0, ff // 256, up_back, 0, unroll=UNROLL_BACK)
    for b in range(d // 256):
        cols = pl.ds(b * 256, 256)
        dsum[:, cols] += sum(dg(b_view[i], gp[nd + i, cols, :], 1, 1) for i in range(nu))

    def row_block(p, t):
        for j in range(4):
            g[p, j % 2, j // 2] = t[j * R:(j + 1) * R].astype(BF)

    def up_block(i, carry):
        row_block(nd + i, dg(low1[...], b_view[i], 0, 0))
        c1(nd + i).start()
        return carry

    lax.fori_loop(0, nu, up_block, 0)

    def rows_back():
        part[...] = jnp.zeros_like(part)
        chunk = 64
        gain = g1_v[...].reshape(1, d)

        def norm1_back(i, carry):
            r = pl.ds(pl.multiple_of(i * chunk, chunk), chunk)
            d_first, normed = dsum[r], normed1[r]
            part[1] += fold(d_first * normed)
            part[2] += fold(d_first)
            d_sum = scale1[r, :1] * norm_grad(d_first * gain, normed)
            dsum[r] = d_sum
            low = d_sum.astype(BF)
            datt[r] = low
            part[0] += fold(low.astype(F32))
            return carry

        lax.fori_loop(0, rows // chunk, norm1_back, 0)
        row_block(nd + nu, dg(ctx[...], datt[...], 0, 0))
        c1(nd + nu).start()
        dctx[...] = dg(datt[...], wo[...], 1, 1).astype(BF).reshape(seqs, quarter, d)
        out_store.wait()

    def unit(u, carry):
        s, p = u // pairs, u % pairs
        cols = pl.ds(pl.multiple_of(p * PAIR, PAIR), PAIR)
        qs = stack_heads(q[s, :, cols])
        ds = stack_heads(dctx[s, :, cols])
        low = pr[s, p]
        probs = low.astype(F32)
        t = probs * dg(v3[s, :, cols], ds, 1, 1)
        d_raw = (t - probs * jnp.sum(t, axis=0, keepdims=True)).astype(BF)
        dv[s, :, cols] = dg(low, ds, 1, 0).astype(BF)
        dk[s, :, cols] = dg(d_raw, qs, 1, 0).astype(BF)
        dq[s, :, cols] = (unstack_heads(dg(k3[s, :, cols], d_raw, 0, 0)) * 0.125).astype(BF)
        return carry

    def qkv_piece(i):
        cols = pl.ds(i * 2 * PAIR, 2 * PAIR)
        allt = toks3[...].reshape(seqs * keys, d)
        ga = dg(toks3[:, pl.ds(pl.multiple_of(n * quarter, quarter), quarter)].reshape(rows, d), dq[:, :, cols].reshape(rows, 2 * PAIR), 0, 0)
        gb = dg(allt, a_buf[:, cols], 0, 0)
        gc = dg(allt, b_buf[:, cols], 0, 0)
        left = left_lanes(R)
        p = nd + nu + 1 + i
        for e in range(4):
            rr = slice(e * R, (e + 1) * R)
            for j in range(2):
                sl = slice(j * PAIR, (j + 1) * PAIR)
                aj, bj, cj = ga[rr, sl], pltpu.roll(gb[rr, sl], HD, 1), gc[rr, sl]
                for t, val in enumerate((jnp.where(left, aj, bj), jnp.where(left, cj, aj), jnp.where(left, bj, cj))):
                    g[p, e % 2, e // 2, :, pl.ds((3 * j + t) * PAIR, PAIR)] = val.astype(BF)
        c1(p).start()

    cx1 = copy_to(dtok.at[:, 1 - c], x1, xs.at[0], xs.at[1], core_peer)
    cx2 = copy_to(dtok.at[1 - y, c], x2, xs.at[2], xs.at[3], y_peer)

    def input_part():
        def one(s, carry):
            t = dg(dk[s], wp[1], 1, 1) + dg(dv[s], wp[2], 1, 1)
            for e in range(4):
                dtok[e // 2, e % 2, s] = t[e * quarter:(e + 1) * quarter].astype(BF)
            return carry

        lax.fori_loop(0, seqs, one, 0)
        cx1.start()
        dsum[...] += dg(dq[...].reshape(rows, d), wp[0], 1, 1)

    def small(i, slot, dev):
        return copy_to(sbuf.at[i], srecv.at[slot], ss.at[slot], sq.at[slot], dev)

    def sums0():
        sbuf[0, 0:1] = jnp.sum(fold(dq[...].reshape(rows, d).astype(F32)), axis=0, keepdims=True)

        def add(s, acc):
            return acc + fold(dv[s].astype(F32))

        acc = lax.fori_loop(0, seqs, add, jnp.zeros((8, d), F32))
        sbuf[0, 1:2] = jnp.sum(acc, axis=0, keepdims=True)
        for i in range(3):
            sbuf[0, 2 + i:3 + i] = total(part[i])
        for i in range(nu):
            sbuf[0, 5 + i:6 + i] = total(part_up[:, i * d:(i + 1) * d])
        for i in range(3):
            sbuf[0, 5 + nu + i:6 + nu + i] = total(part2[i])
        small(0, 0, core_peer).start()

    def sums1():
        small(0, 0, core_peer).wait_recv()
        sbuf[1] = sbuf[0] + srecv[0]
        small(1, 1, y_peer).start()

    def sums2():
        small(1, 1, y_peer).wait_recv()
        sbuf[2] = sbuf[1] + srecv[1]
        small(2, 2, x_peer).start()

    def sums3():
        small(2, 2, x_peer).wait_recv()
        sbuf[3] = sbuf[2] + srecv[2]
        for e in range(3):
            small(3, 3 + e, z_peers[e]).start()

    so_store = pltpu.make_async_copy(so_v, so_hbm, xs.at[6])

    def sums4():
        for e in range(3):
            small(3, 3 + e, z_peers[e]).wait_recv()
        so_v[...] = sbuf[3] + srecv[3] + srecv[4] + srecv[5]
        so_store.start()

    def add_x1():
        cx1.wait_recv()

        def add(i, carry):
            a, b = i // seqs, i % seqs
            dtok[a, c, b] = (dtok[a, c, b].astype(F32) + x1[a, b].astype(F32)).astype(BF)
            return carry

        lax.fori_loop(0, 2 * seqs, add, 0)

    din_out = pltpu.make_async_copy(x1.at[0], din_hbm, xs.at[4])

    def input_out():
        cx2.wait_recv()

        def out_x(i, carry):
            r = pl.ds(pl.multiple_of(i * quarter, quarter), quarter)
            x1[0, i] = (dsum[r] + dtok[y, c, i].astype(F32) + x2[i].astype(F32)).astype(BF)
            return carry

        lax.fori_loop(0, seqs, out_x, 0)
        din_out.start()

    units = seqs * pairs
    slots_of_units = -(-units // UNITS)
    extra = {3: [rows_back], 9: [lambda: qkv_piece(0)], 10: [lambda: qkv_piece(1), lambda: qkv_piece(2), sums0],
             11: [input_part, sums1], 12: [add_x1, sums2], 13: [cx2.start, sums3], 16: [sums4], 21: [input_out]}

    def drain(p):
        c1(p).wait_send()
        c2(p).wait_send()
        c3(p).wait_send()
        c6(p, near).wait_send()
        for e in range(3):
            c4(p, e).wait_send()
            c5(p, e, z).wait_send()

    def slot(t, carry):
        for i in ORDER:
            p = t - LAGS[i]

            @pl.when(jnp.logical_and(p >= 0, p < pieces))
            def run():
                stages[i](p)

        @pl.when(jnp.logical_and(t > 3, t <= 3 + slots_of_units))
        def attention():
            lo = (t - 4) * UNITS
            lax.fori_loop(lo, jnp.minimum(lo + UNITS, units), unit, 0)

        for at, todo in extra.items():
            @pl.when(t == at)
            def more():
                for f in todo:
                    f()

        old = t - LAGS[5] - 3

        @pl.when(jnp.logical_and(old >= 0, old < pieces))
        def finished():
            drain(old)
        return carry

    lax.fori_loop(3, pieces + LAGS[6], slot, 0)
    small(0, 0, core_peer).wait_send()
    small(1, 1, y_peer).wait_send()
    small(2, 2, x_peer).wait_send()
    for e in range(3):
        small(3, 3 + e, z_peers[e]).wait_send()
    cx1.wait_send()
    cx2.wait_send()

    def stored(p, carry):
        store(p, oo_hbm).wait()
        return carry

    lax.fori_loop(0, pieces, stored, 0)
    for s in range(seqs):
        send_y(s).wait_send()
        send_core(s).wait_send()
        forward_y(s).wait_send()
    din_out.wait()
    so_store.wait()


def layer_part(tokens, lengths, w, qvb, wo, bo, g1, s1, wu, bu, wd, bd, g2, s2, cot):
    seqs, quarter, d = tokens.shape
    rows, keys, pairs, ff = seqs * quarter, 4 * quarter, d // PAIR, wu.shape[1]
    R = d // 4
    nd = nu = ff // d
    n = nd + nu + 4
    h = R // 2
    all_rows = (8 + nu, d)
    vm, hbm = pl.BlockSpec(memory_space=V), pl.BlockSpec(memory_space=ANY)
    S = jax.ShapeDtypeStruct
    own, every, flat = (seqs, quarter, d), (seqs, 4, quarter, d), (rows, d)
    row = V((d,), F32)
    return pl.pallas_call(
        layer_kernel,
        out_shape=(S(flat, BF), S((nd * R, d), BF), S((R, nu * d), BF), S((R, d), BF), S((R, 3 * d), BF), S(own, BF),
                   S(all_rows, F32)),
        in_specs=[pl.BlockSpec(memory_space=pltpu.SMEM)] + [hbm] * 14,
        out_specs=[hbm] * 7,
        scratch_shapes=[V((seqs * keys, d), BF), V((seqs * keys, d), BF), V((2, 2) + own, BF), V(every, BF), V(every, BF),
                        V(every, BF), V(own, BF), V((seqs, pairs, keys, 2 * quarter), BF), V((3, d, d), BF),
                        V(flat, BF), V(flat, BF), V(flat, BF), V(flat, BF), V(own, BF), V(wo.shape, BF),
                        V(flat, F32), V(flat, F32), V(flat, F32), V((rows, 128), F32), V((3, 8, d), F32),
                        V((3, 8, d), F32), V((8, ff), F32), V((2, d), F32), row, row, row, V((ff,), F32), row, row, row,
                        V((n, 2, 2, R, d), BF), V((n, 2, R, d), BF), V((n, R, d), BF), V((n, h, d), BF),
                        V((n, 3, h // 2, d // 2), BF), V((4,) + all_rows, F32), V((6,) + all_rows, F32),
                        V(all_rows, F32), V((2,) + own, BF), V(own, BF), DMA((14 + nd + nu,))]
        + [DMA((seqs,))] * 6 + [DMA((n,))] * 6 + [DMA((n, 3))] * 4 + [DMA((n,))] * 3
        + [DMA((6,))] * 2 + [DMA((7,))],
        name="layer_part",
        compiler_params=pltpu.CompilerParams(collective_id=1, has_side_effects=True, vmem_limit_bytes=63 << 20),
    )(lengths, tokens, cot, w, wo, wu, wd, qvb, bo, g1, s1, bu, bd, g2, s2)


def finish_kernel(d_h, u_h, o_h, q_h, out_h, din_h, sums_h, fd, fu, fo, fq, fout, fdin,
                  qvb_h, outb_h, n1g_h, n1s_h, upb_h, downb_h, n2g_h, n2s_h,
                  low, full, rows, sums_ref, qvb, outb, n1g, n1s, upb, downb, n2g, n2s, ls, os_, ms):
    R, C = low.shape[1:]
    nd, nu = d_h.shape[0] // R, u_h.shape[1] // C
    cut = lambda ref, i: ref.at[:, pl.ds(i * C, C)]
    ends = ([(d_h.at[pl.ds(i * R, R)], fd.at[pl.ds(i * R, R)]) for i in range(nd)]
            + [(cut(u_h, i), cut(fu, i)) for i in range(nu)] + [(o_h, fo)]
            + [(cut(q_h, i), cut(fq, i)) for i in range(3)])
    loads = [pltpu.make_async_copy(s, low.at[i], ls.at[i]) for i, (s, _) in enumerate(ends)]
    stores = [pltpu.make_async_copy(full.at[i], t, os_.at[i]) for i, (_, t) in enumerate(ends)]
    pieces = len(ends)
    loads += [pltpu.make_async_copy(s, rows.at[i], ls.at[pieces + i]) for i, s in enumerate((out_h, din_h))]
    stores += [pltpu.make_async_copy(rows.at[i], t, os_.at[pieces + i]) for i, t in enumerate((fout, fdin))]
    sums_load = pltpu.make_async_copy(sums_h, sums_ref, ms.at[8])
    sums_load.start()
    for cp in loads:
        cp.start()
    small = [pltpu.make_async_copy(s, t, ms.at[i]) for i, (s, t) in enumerate(
        ((qvb, qvb_h), (outb, outb_h), (n1g, n1g_h), (n1s, n1s_h), (upb, upb_h), (downb, downb_h), (n2g, n2g_h),
         (n2s, n2s_h)))]
    sums_load.wait()
    n = lax.axis_index("narrow")
    for i in range(4):
        @pl.when(n == i)
        def pick():
            at = slice(i * R, (i + 1) * R)
            qvb[...] = sums_ref[0:2, at]
            for j, ref in ((2, outb), (3, n1g), (4, n1s), (5 + nu, downb), (6 + nu, n2g), (7 + nu, n2s)):
                ref[...] = sums_ref[j, at]
            upb[...] = sums_ref[5 + i]
    for cp in small:
        cp.start()
    for i, (a, b) in enumerate(zip(loads, stores)):
        a.wait()
        if i < pieces:
            full[i] = low[i].astype(F32)
        b.start()
    for cp in stores + small:
        cp.wait()


def finish_part(down, up, out, qkv, output, input_grad, sums):
    R, d = out.shape
    n = down.shape[0] // R + up.shape[1] // d + 4
    vm, hbm = pl.BlockSpec(memory_space=V), pl.BlockSpec(memory_space=ANY)
    S = jax.ShapeDtypeStruct
    shapes = [S(a.shape, F32) for a in (down, up, out, qkv)] + [S(output.shape, BF)] * 2 + [S((2, R), F32)] + [S((R,), F32)] * 3
    shapes += [S((d,), F32)] + [S((R,), F32)] * 3
    return pl.pallas_call(
        finish_kernel,
        out_shape=shapes,
        in_specs=[hbm] * 7,
        out_specs=[hbm] * 14,
        scratch_shapes=[V((n, R, d), BF), V((n, R, d), F32), V((2,) + output.shape, BF), V(sums.shape, F32)]
        + [V(a.shape, F32) for a in shapes[6:]] + [DMA((n + 2,)), DMA((n + 2,)), DMA((9,))],
        name="finish_part",
        compiler_params=pltpu.CompilerParams(vmem_limit_bytes=60 << 20),
    )(down, up, out, qkv, output, input_grad, sums)


def local(tokens, lengths, qkv_weight, qv_bias, out_weight, out_bias, norm1_gain, norm1_shift, up_weight, up_bias,
          down_weight, down_bias, norm2_gain, norm2_shift, cotangent):
    own = tokens.shape
    output, down, up, out, qkv, input_grad, sums = layer_part(
        tokens, lengths, qkv_weight, qv_bias, out_weight, out_bias, norm1_gain, norm1_shift, up_weight, up_bias,
        down_weight, down_bias, norm2_gain, norm2_shift, cotangent)
    wide = lax.axis_size("wide")
    if wide > 8:
        groups = [[j * 8 + i for j in range(wide // 8)] for i in range(8)]
        down, up, out, qkv = (
            lax.psum(a.astype(F32), "wide", axis_index_groups=groups).astype(BF) for a in (down, up, out, qkv))
        sums = lax.psum(sums, "wide", axis_index_groups=groups)
    down, up, out, qkv, output, input_grad, qvb, outb, n1g, n1s, upb, downb, n2g, n2s = finish_part(
        down, up, out, qkv, output, input_grad.reshape(output.shape), sums)
    return (output.reshape(own), input_grad.reshape(own), qkv, qvb, out, outb, n1g, n1s, up, upb, down, downb, n2g, n2s)


def solution(mesh):
    return jax.shard_map(
        local,
        mesh=mesh,
        in_specs=(
            P("wide", "narrow", None),
            P("wide"),
            P(),
            P(),
            P(),
            P(),
            P(),
            P(),
            P(),
            P(),
            P(),
            P(),
            P(),
            P(),
            P("wide", "narrow", None),
        ),
        out_specs=(
            P("wide", "narrow", None),
            P("wide", "narrow", None),
            P("narrow", None),
            P(None, "narrow"),
            P("narrow", None),
            P("narrow"),
            P("narrow"),
            P("narrow"),
            P("narrow", None),
            P("narrow"),
            P("narrow", None),
            P("narrow"),
            P("narrow"),
            P("narrow"),
        ),
        check_vma=False,
    )
```
